512 devices in a mesh: dp: 32 (over x_hi, z), spatial: 16 (over x_lo, y, core).
Axes of the slice: x: 4 (x_hi: 2, x_lo: 2; x = x_hi * 2 + x_lo), y: 4, z: 16, core: 2. Of those that a mesh axis runs over, the one named last changes fastest.
Arguments:
- latents: bfloat16 [64, 32, 32, 640], P('dp', 'spatial'), may hold values from -16 to 16
- plan: bfloat16 [64, 256, 640], P('dp', 'spatial'), may hold values from -45 to 45
- conv_weight: bfloat16 [9, 640, 640], P(None, 'dp'), may hold values from -0.078125 to 0.078125
- gn_gain: float32 [640], replicated, may hold values from 0.5 to 2
- attn_weights: bfloat16 [4, 640, 640], P(None, 'dp'), may hold values from -0.25 to 0.25
- cotangent: bfloat16 [64, 32, 32, 640], P('dp', 'spatial'), may hold values from -6 to 6
Outputs:
- block_out: bfloat16 [64, 32, 32, 640], P('dp', 'spatial')
- weight_grads: float32 [640, 2, 640], P('dp')
The draws below stay inside these ranges and needn't reach their ends.
All inputs are finite; a program needn't handle non-finite values.
Results may differ from the reference program's by a relative error of at most 0.03.
The reference program's roundings to bfloat16 on the way (of `hidden`, `mixed`, `probs_b`, `attended`, `grad_att`, `dscore` and `dquery`) count: a program that leaves them out, or rounds other values in their place, can miss the bound.
Values may be sent and summed in bfloat16 or wider, within the bound.
A program may use at most 64 MiB of HBM per device.

```python
import math
import jax
import jax.numpy as jnp
from jax import lax

D = 640
GROUPS = 32
HEAD = 64
LAT = 32
IMAGES = 64
PLAN = 256
TOKENS = 65536


def draw_latents(key, part):
    key_base, key_chan = jax.random.split(key, 2)
    base = jnp.clip(jax.random.normal(key_base, (IMAGES, LAT, LAT, D), jnp.float32), -4.0, 4.0)
    level = jnp.arange(LAT, dtype=jnp.float32) / (LAT - 1)
    channel_scale = jax.random.uniform(key_chan, (D,), jnp.float32, 0.5, 1.5)
    row_scale = 0.5 + level
    values = base * row_scale[None, :, None, None] * channel_scale
    return jnp.clip(values, -16.0, 16.0).astype(jnp.bfloat16)


def draw_plan(key, part):
    key_base = jax.random.fold_in(key, 0)
    base = jnp.clip(jax.random.normal(key_base, (IMAGES, PLAN, D), jnp.float32), -6.0, 6.0)
    return jnp.clip(base, -45.0, 45.0).astype(jnp.bfloat16)


def block_scale(stream_key, dims, cuts, smallest, largest):
    factor_of, own = 1.0, jax.random.fold_in(stream_key, 6)
    for axis_at, parts in cuts:
        steps = jnp.exp(jax.random.uniform(jax.random.fold_in(own, axis_at), (parts,), jnp.float32, smallest / len(cuts), largest / len(cuts)))
        factor_of = factor_of * jnp.repeat(steps, dims[axis_at] // parts).reshape([-1 if axis == axis_at else 1 for axis in range(len(dims))])
    return factor_of


def centred(stream_key, dims, deviation, reach, cuts=(), held_as=jnp.bfloat16):
    loudness = block_scale(stream_key, dims, cuts, -0.22, 0.18) if cuts else 1.0
    entries = jax.random.normal(stream_key, dims, jnp.float32) * deviation * loudness
    return jnp.minimum(jnp.maximum(entries, -reach), reach).astype(held_as)


def setup_inputs(seed: int = 0) -> dict:
    splits = jax.random.split(jax.random.key(seed), 7)
    latents = draw_latents(jax.random.fold_in(splits[6], 71), 0)
    plan = draw_plan(jax.random.fold_in(splits[6], 71), 0)
    conv_weight = centred(splits[2], (9, D, D), (9 * D) ** -0.5, 0.078125, ((1, 32),))
    gn_gain = jnp.clip(jnp.exp(jax.random.uniform(splits[3], (D,), jnp.float32, math.log(0.5), math.log(2.0))), 0.5, 2.0)
    attn_weights = centred(splits[4], (4, D, D), D ** -0.5, 0.25, ((1, 32),))
    cotangent = centred(splits[5], (IMAGES, LAT, LAT, D), 1.0, 6.0, ((0, 32), (1, 16)))
    return dict(latents=latents, plan=plan, conv_weight=conv_weight, gn_gain=gn_gain, attn_weights=attn_weights, cotangent=cotangent)


def reference(latents, plan, conv_weight, gn_gain, attn_weights, cotangent):
    heads = D // HEAD
    per_group = D // GROUPS
    scale = 1.0 / math.sqrt(HEAD)
    weight_q = attn_weights[0]
    weight_k = attn_weights[1]
    weight_v = attn_weights[2]
    weight_o = attn_weights[3]

    def one_image(carry, inputs):
        image, plan_image, cot_image = inputs
        flat = image.astype(jnp.float32).reshape(LAT * LAT, GROUPS, per_group)
        counted = float(LAT * LAT * per_group)
        means = lax.optimization_barrier(jnp.sum(flat, axis=(0, 2))) / counted
        variance = lax.optimization_barrier(jnp.sum(flat * flat, axis=(0, 2))) / counted - means * means
        normed = (flat - means[None, :, None]) * lax.rsqrt(variance + 1e-05)[None, :, None]
        normed = normed.reshape(LAT, LAT, D) * gn_gain
        hidden = jax.nn.silu(normed).astype(jnp.bfloat16)
        padded = jnp.pad(hidden, ((1, 1), (1, 1), (0, 0)))
        conv_sum = jnp.zeros((LAT * LAT, D), jnp.float32)
        for offset_y in range(3):
            for offset_x in range(3):
                window = padded[offset_y:offset_y + LAT, offset_x:offset_x + LAT].reshape(LAT * LAT, D)
                conv_sum = conv_sum + jnp.dot(window, conv_weight[3 * offset_y + offset_x], preferred_element_type=jnp.float32)
        mixed = (image.reshape(LAT * LAT, D).astype(jnp.float32) + conv_sum).astype(jnp.bfloat16)
        queries = jnp.dot(mixed, weight_q, preferred_element_type=jnp.float32).astype(jnp.bfloat16)
        keys = jnp.dot(plan_image, weight_k, preferred_element_type=jnp.float32).astype(jnp.bfloat16)
        values = jnp.dot(plan_image, weight_v, preferred_element_type=jnp.float32).astype(jnp.bfloat16)
        query_heads = queries.astype(jnp.float32).reshape(LAT * LAT, heads, HEAD)
        key_heads = keys.astype(jnp.float32).reshape(PLAN, heads, HEAD)
        value_heads = values.astype(jnp.float32).reshape(PLAN, heads, HEAD)
        scores = jnp.einsum('nhe,mhe->hnm', query_heads, key_heads) * scale
        maxima = lax.optimization_barrier(jnp.max(scores, axis=-1, keepdims=True))
        expo = jnp.exp(scores - maxima)
        probs = expo / lax.optimization_barrier(jnp.sum(expo, axis=-1, keepdims=True))
        probs_b = probs.astype(jnp.bfloat16)
        attended = jnp.einsum('hnm,mhe->nhe', probs_b.astype(jnp.float32), value_heads)
        attended = attended.reshape(LAT * LAT, D).astype(jnp.bfloat16)
        output = (mixed.astype(jnp.float32) + jnp.dot(attended, weight_o, preferred_element_type=jnp.float32)).astype(jnp.bfloat16)
        grad_in = cot_image.reshape(LAT * LAT, D)
        grad_att = jnp.dot(grad_in, weight_o.T, preferred_element_type=jnp.float32).astype(jnp.bfloat16)
        grad_heads = grad_att.astype(jnp.float32).reshape(LAT * LAT, heads, HEAD)
        dprob = jnp.einsum('nhe,mhe->hnm', grad_heads, value_heads)
        dscore = (probs * (dprob - lax.optimization_barrier(jnp.sum(probs * dprob, axis=-1, keepdims=True))) * scale).astype(jnp.bfloat16)
        dquery = jnp.einsum('hnm,mhe->nhe', dscore.astype(jnp.float32), key_heads)
        dquery = dquery.reshape(LAT * LAT, D).astype(jnp.bfloat16)
        grad_q = carry[0] + jnp.dot(mixed.T, dquery, preferred_element_type=jnp.float32)
        grad_o = carry[1] + jnp.dot(attended.T, grad_in, preferred_element_type=jnp.float32)
        return ((grad_q, grad_o), output.reshape(LAT, LAT, D))
    start = (jnp.zeros((D, D), jnp.float32), jnp.zeros((D, D), jnp.float32))
    totals, block_out = lax.scan(one_image, start, (latents, plan, cotangent))
    factor = 1.0 / math.sqrt(TOKENS)
    weight_grads = jnp.stack([totals[0], totals[1]], axis=1) * factor
    return (block_out, weight_grads)
```

```python
import math

import jax
import jax.numpy as jnp
from jax import lax
from jax.experimental import pallas as pl
from jax.experimental.pallas import tpu as pltpu
from jax.sharding import PartitionSpec as P

GROUPS = 32
HEAD = 64
NX = 4
NY = 4
QUAD = 4
MESH = pl.DeviceIdType.MESH
VMEM_LIMIT = 62 * 1024 * 1024

eps_norm = 1e-05


def wrap(value, n):
    return lax.rem(value + n, n)


class Spot:
    def __init__(self):
        self.nz = lax.axis_size("dp") // 2
        dp = lax.axis_index("dp")
        self.s = lax.axis_index("spatial")
        self.xh = lax.div(dp, self.nz)
        self.z = lax.rem(dp, self.nz)
        self.xl = lax.div(self.s, 2 * NY)
        self.y = lax.rem(lax.div(self.s, 2), NY)
        self.c = lax.rem(self.s, 2)
        self.x = 2 * self.xh + self.xl
        self.dp = dp

    def at(self, x=None, y=None, z=None, c=None):
        x = self.x if x is None else wrap(x, NX)
        y = self.y if y is None else wrap(y, NY)
        z = self.z if z is None else wrap(z, self.nz)
        c = self.c if c is None else c
        return (lax.div(x, 2) * self.nz + z, (lax.rem(x, 2) * NY + y) * 2 + c)

    def band(self, s):
        return (self.dp, s)


def send(src, dst, send_sem, recv_sem, device):
    pltpu.make_async_remote_copy(
        src_ref=src,
        dst_ref=dst,
        send_sem=send_sem,
        recv_sem=recv_sem,
        device_id=device,
        device_id_type=MESH,
    ).start()


def await_bytes(ref, sem):
    pltpu.make_async_copy(ref, ref, sem).wait()


def greet(spot, devices):
    barrier = pltpu.get_barrier_semaphore()
    for device in devices:
        pl.semaphore_signal(barrier, inc=1, device_id=device, device_id_type=MESH)
    pl.semaphore_wait(barrier, len(devices))


def gather_kernel(
    wslice, lat, plan, sums, cot, gain,
    block_out, ops,
    wmain, wext, zbuf, tmpf, stage, planb, halo, sbuf, taps, keys, vals, gatt,
    z_send, zr_recv, zl_recv, a_send, b_send, c_send, d_send, e_send, f_send,
    a_recv, b_recv, c_recv, d_recv, e_recv, f_recv,
    misc_send, misc_recv,
):
    me = Spot()
    nz, x, y, z, c, s = me.nz, me.x, me.y, me.z, me.c, me.s
    spatial = 4 * NY
    per_core = 2 * NY
    nq = nz // QUAD
    shard = 20
    unit = QUAD * shard
    half = nz * shard
    side = jnp.where(me.xl == 0, -1, 1)
    other_x = me.at(x=x + side)
    twin = me.at(c=1 - c)

    def sid(xx, yy):
        return c * per_core + lax.rem(wrap(xx, NX), 2) * NY + wrap(yy, NY)

    mates = [me.band(wrap(s + k, spatial)) for k in range(1, spatial)]
    greet(me, mates + [me.at(z=z + 1), me.at(z=z - 1), other_x])

    for k, mate in enumerate(mates):
        send(sums, sbuf.at[s], misc_send.at[0], misc_recv.at[0], mate)
    send(lat.at[:, 0], halo.at[1], misc_send.at[1], misc_recv.at[1], me.band(wrap(s - 1, spatial)))
    send(lat.at[:, 1], halo.at[0], misc_send.at[2], misc_recv.at[2], me.band(wrap(s + 1, spatial)))
    send(wslice, zbuf.at[z], z_send.at[0], zr_recv.at[0], me.at(z=z + 1))
    send(wslice, zbuf.at[z], z_send.at[1], zl_recv.at[0], me.at(z=z - 1))
    zbuf[z] = wslice[...]
    my_sid = sid(x, y)
    for dx in range(2):
        for dy in range(NY):
            if dx or dy:
                target = ((me.dp), (lax.rem(me.xl + dx, 2) * NY + wrap(y + dy, NY)) * 2 + c)
                send(plan, planb.at[:, my_sid], misc_send.at[3], misc_recv.at[3], target)
    planb[:, my_sid] = plan[...]
    sbuf[s] = sums[...]

    def z_step(k):
        await_bytes(zbuf.at[0], zr_recv.at[k - 1])
        if k < nz // 2:
            slot = wrap(z - k, nz)
            send(zbuf.at[slot], zbuf.at[slot], z_send.at[0], zr_recv.at[k], me.at(z=z + 1))
        if k < nz // 2:
            await_bytes(zbuf.at[0], zl_recv.at[k - 1])
            if k < nz // 2 - 1:
                slot = wrap(z + k, nz)
                send(zbuf.at[slot], zbuf.at[slot], z_send.at[1], zl_recv.at[k], me.at(z=z - 1))

    def block(xx, yy, q, colours=slice(None), dirs=slice(None)):
        row = pl.multiple_of(lax.div(wrap(xx, NX), 2) * half + q * unit, 16)
        return wmain.at[sid(xx, yy), colours, dirs, pl.ds(row, unit), :]

    def move(r, q, xx, yy, colours, dirs, send_sem, recv_sem, device):
        ref = block(xx, yy, q, colours, dirs)
        send(ref, ref, send_sem, recv_sem.at[r], device)

    every = slice(None)
    north, south = me.at(y=y + 1), me.at(y=y - 1)
    east, west = me.at(x=x + 1), me.at(x=x - 1)

    def part_a(r, q):
        for i in range(QUAD):
            tmpf[...] = zbuf[q * QUAD + i].astype(jnp.float32)
            for j in range(5):
                stage[j, i * shard:(i + 1) * shard, :] = tmpf[j * shard:(j + 1) * shard, :]
        row = pl.multiple_of(me.xh * half + q * unit, 16)
        for j in range(4):
            wmain[my_sid, j // 2, j % 2, pl.ds(row, unit), :] = stage[j].astype(jnp.bfloat16)
        wext[pl.ds(row, unit), :] = stage[4].astype(jnp.bfloat16)
        for device in (east, west, north, south):
            move(r, q, x, y, every, every, a_send, a_recv, device)
        send(wext.at[pl.ds(row, unit), :], wext.at[pl.ds(row, unit), :], e_send, e_recv, other_x)
        move(0, q, x, y, every, every, f_send, f_recv, twin)

    def part_b(r, q):
        await_bytes(wmain.at[pl.ds(0, 4), :, :, pl.ds(0, unit), :], a_recv.at[r])
        move(r, q, x - 1, y, every, pl.ds(0, 1), b_send, b_recv, east)
        move(r, q, x + 1, y, every, pl.ds(1, 1), b_send, b_recv, west)
        move(r, q, x, y - 1, every, pl.ds(0, 1), b_send, b_recv, north)
        move(r, q, x, y + 1, every, pl.ds(1, 1), b_send, b_recv, south)
        for k in (1, -1):
            for device in (north, south):
                move(r, q, x + k, y, pl.ds(0, 1), every, c_send, c_recv, device)
            for device in (east, west):
                move(r, q, x, y + k, pl.ds(1, 1), every, c_send, c_recv, device)
        for k in (1, -1):
            move(0, q, x + k, y, every, every, f_send, f_recv, twin)
            move(0, q, x, y + k, every, every, f_send, f_recv, twin)

    def part_c(r, q):
        await_bytes(wmain.at[pl.ds(0, 2), :, :, pl.ds(0, unit), :], b_recv.at[r])
        for device in (north, south):
            move(r, q, x + 2, y, pl.ds(0, 1), every, c_send, c_recv, device)
        for device in (east, west):
            move(r, q, x, y + 2, pl.ds(1, 1), every, c_send, c_recv, device)
        move(0, q, x + 2, y, every, every, f_send, f_recv, twin)
        move(0, q, x, y + 2, every, every, f_send, f_recv, twin)

    def part_d(r, q):
        await_bytes(wmain.at[pl.ds(0, 6), :, :, pl.ds(0, unit), :], c_recv.at[r])
        for k in (1, -1, 2):
            move(r, q, x + k, y - 1, pl.ds(0, 1), pl.ds(0, 1), d_send, d_recv, north)
            move(r, q, x + k, y + 1, pl.ds(0, 1), pl.ds(1, 1), d_send, d_recv, south)
            move(r, q, x - 1, y + k, pl.ds(1, 1), pl.ds(0, 1), d_send, d_recv, east)
            move(r, q, x + 1, y + k, pl.ds(1, 1), pl.ds(1, 1), d_send, d_recv, west)
        for i in (1, -1):
            for j in (1, -1):
                move(0, q, x + i, y + j, every, every, f_send, f_recv, twin)

    def part_e(r, q):
        await_bytes(wmain.at[pl.ds(0, 3), :, :, pl.ds(0, unit), :], d_recv.at[r])
        for i, j in ((1, 2), (-1, 2), (2, 1), (2, -1), (2, 2)):
            move(0, q, x + i, y + j, every, every, f_send, f_recv, twin)

    quad, inner = lax.div(z, QUAD), lax.rem(z, QUAD)
    near = jnp.where(inner < QUAD // 2, -1, 1)
    if nq == 4:
        rounds = [quad, wrap(quad + near, nq), wrap(quad - near, nq), wrap(quad + 2, nq)]
        steps = [3, 2, 2, 1]
    else:
        rounds, steps = [quad], [nz // 2]
    done = 0

    def steps_for(r):
        nonlocal done
        for _ in range(steps[r]):
            done += 1
            z_step(done)

    steps_for(0)
    part_a(0, rounds[0])
    await_bytes(planb.at[:, pl.ds(0, per_core - 1)], misc_recv.at[3])
    mine = planb.at[:, pl.ds(c * per_core, per_core)]
    send(mine, mine, misc_send.at[4], misc_recv.at[4], twin)
    await_bytes(sbuf.at[pl.ds(0, spatial - 1)], misc_recv.at[0])
    await_bytes(halo.at[0], misc_recv.at[1])
    await_bytes(halo.at[0], misc_recv.at[2])
    norm_taps(me, lat, gain, halo, sbuf, taps)
    for r in range(nq):
        if r + 1 < nq:
            steps_for(r + 1)
        part_b(r, rounds[r])
        part_c(r, rounds[r])
        if r + 1 < nq:
            part_a(r + 1, rounds[r + 1])
        if r:
            part_d(r - 1, rounds[r - 1])
        if r > 1:
            part_e(r - 2, rounds[r - 2])
    part_d(nq - 1, rounds[nq - 1])
    if nq > 1:
        part_e(nq - 2, rounds[nq - 2])
    part_e(nq - 1, rounds[nq - 1])

    await_bytes(planb.at[:, pl.ds(0, per_core)], misc_recv.at[4])
    await_bytes(wext.at[pl.ds(0, half)], e_recv)
    await_bytes(wmain.at[pl.ds(0, per_core)], f_recv.at[0])

    await_bytes(sbuf.at[pl.ds(0, spatial - 1)], misc_send.at[0])
    await_bytes(halo.at[0], misc_send.at[1])
    await_bytes(halo.at[0], misc_send.at[2])
    await_bytes(planb.at[:, pl.ds(0, per_core - 1)], misc_send.at[3])
    await_bytes(planb.at[:, pl.ds(0, per_core)], misc_send.at[4])
    await_bytes(zbuf.at[pl.ds(0, nz // 2)], z_send.at[0])
    await_bytes(zbuf.at[pl.ds(0, nz // 2 - 1)], z_send.at[1])
    await_bytes(wmain.at[pl.ds(0, 2)], a_send)
    await_bytes(wmain.at[pl.ds(0, 1)], b_send)
    await_bytes(wmain.at[pl.ds(0, 3)], c_send)
    await_bytes(wmain.at[pl.ds(0, 3), pl.ds(0, 1)], d_send)
    await_bytes(wext.at[pl.ds(0, half)], e_send)
    await_bytes(wmain.at[pl.ds(0, per_core)], f_send)

    plan_side(cot, planb, wmain, wext, keys, vals, gatt)
    convolve(lat, wmain, wext, taps, ops.at[0, 0])
    attend(
        ops.at[0, 0], wmain, wext, keys, vals, gatt, ops.at[1, 0], ops.at[0, 1], block_out
    )
    ops[1, 1] = cot[...].reshape(ops.shape[2:])


def gather_all(wslice, latents, plan, sums, cotangent, gain):
    nz = lax.axis_size("dp") // 2
    spatial = 4 * NY
    nq = nz // QUAD
    rows = 2 * nz * 20
    images, band_rows, columns, channels = latents.shape
    tokens = images * band_rows * columns
    plan_tokens = spatial * plan.shape[1]
    bf16, f32 = jnp.bfloat16, jnp.float32
    dma = pltpu.SemaphoreType.DMA
    return pl.pallas_call(
        gather_kernel,
        out_shape=[
            jax.ShapeDtypeStruct(latents.shape, bf16),
            jax.ShapeDtypeStruct((2, 2, tokens, channels), bf16),
        ],
        in_specs=[pl.BlockSpec(memory_space=pltpu.VMEM)] * 6,
        out_specs=[pl.BlockSpec(memory_space=pltpu.VMEM)] * 2,
        scratch_shapes=[
            pltpu.VMEM((spatial, 2, 2, rows, 128), bf16),
            pltpu.VMEM((rows, 128), bf16),
            pltpu.VMEM((nz, 112, 128), bf16),
            pltpu.VMEM((112, 128), f32),
            pltpu.VMEM((5, QUAD * 20, 128), f32),
            pltpu.VMEM((images, spatial) + plan.shape[1:], bf16),
            pltpu.VMEM((2, images, columns, channels), bf16),
            pltpu.VMEM((spatial, 8, channels), f32),
            pltpu.VMEM((3, images, band_rows + 2, columns, channels), bf16),
            pltpu.VMEM((images, plan_tokens, channels), bf16),
            pltpu.VMEM((images, plan_tokens, channels), bf16),
            pltpu.VMEM((tokens, channels), bf16),
            dma((2,)), dma((nz // 2,)), dma((nz // 2,)),
            dma, dma, dma, dma, dma, dma,
            dma((nq,)), dma((nq,)), dma((nq,)), dma((nq,)), dma, dma((1,)),
            dma((5,)), dma((5,)),
        ],
        compiler_params=pltpu.CompilerParams(
            collective_id=0, has_side_effects=True, vmem_limit_bytes=VMEM_LIMIT
        ),
        name="gather_all",
    )(wslice, latents, plan, sums, cotangent, gain)


def column_block(wmain, wext, index):
    if index < 64:
        return wmain[index // 4, index % 4 // 2, index % 2]
    return wext[...]


def columns_of(wmain, wext, matrix, start, stop):
    parts = [column_block(wmain, wext, 5 * matrix + n) for n in range(start, stop)]
    return parts[0] if len(parts) == 1 else jnp.concatenate(parts, axis=1)


SPANS = ((0, 2), (2, 4), (4, 5))


def norm_taps(me, lat, gain, halo, sbuf, taps):
    images, band_rows, columns, channels = lat.shape
    spatial = 4 * NY
    f32 = jnp.float32
    tot = sbuf[0]
    for i in range(1, spatial):
        tot = tot + sbuf[i]
    wide = channels // GROUPS
    one = lax.broadcasted_iota(jnp.int32, (channels, channels), 0).astype(f32)
    two = lax.broadcasted_iota(jnp.int32, (channels, channels), 1).astype(f32)
    same = jnp.floor((one + 0.5) * (1.0 / wide)) == jnp.floor((two + 0.5) * (1.0 / wide))
    grouped = jnp.dot(
        tot, same.astype(f32), preferred_element_type=f32, precision=lax.Precision.HIGHEST
    )
    counted = float(band_rows * spatial * columns * wide)
    row_at = lax.broadcasted_iota(jnp.int32, (columns, channels), 0)
    for i in range(images):
        mean = grouped[i:i + 1] / counted
        variance = grouped[images + i:images + i + 1] / counted - mean * mean
        inverse = lax.rsqrt(variance + eps_norm)
        for r in range(band_rows + 2):
            if r == 0:
                cells = halo[0, i]
            elif r == band_rows + 1:
                cells = halo[1, i]
            else:
                cells = lat[i, r - 1]
            normed = (cells.astype(f32) - mean) * inverse * gain[...]
            hidden = (normed / (1.0 + jnp.exp(-normed))).astype(jnp.bfloat16).astype(f32)
            if r == 0:
                hidden = jnp.where(me.s == 0, 0.0, hidden)
            if r == band_rows + 1:
                hidden = jnp.where(me.s == spatial - 1, 0.0, hidden)
            before = jnp.where(row_at == 0, 0.0, pltpu.roll(hidden, 1, 0))
            after = jnp.where(row_at == columns - 1, 0.0, pltpu.roll(hidden, columns - 1, 0))
            taps[0, i, r] = before.astype(jnp.bfloat16)
            taps[1, i, r] = hidden.astype(jnp.bfloat16)
            taps[2, i, r] = after.astype(jnp.bfloat16)


def plan_side(cot, planb, wmain, wext, keys, vals, gatt):
    images, spatial, plan_rows, channels = planb.shape
    f32, bf16 = jnp.float32, jnp.bfloat16
    for start, stop in SPANS:
        lanes = slice(128 * start, 128 * stop)
        weight_k = columns_of(wmain, wext, 10, start, stop)
        weight_v = columns_of(wmain, wext, 11, start, stop)
        for i in range(images):
            rows = planb[i].reshape(spatial * plan_rows, channels)
            keys[i, :, lanes] = jnp.dot(rows, weight_k, preferred_element_type=f32).astype(bf16)
            vals[i, :, lanes] = jnp.dot(rows, weight_v, preferred_element_type=f32).astype(bf16)
    total = None
    flat = cot[...].reshape(-1, channels)
    for start, stop in SPANS:
        weight_o = columns_of(wmain, wext, 12, start, stop)
        part = lax.dot_general(
            flat[:, 128 * start:128 * stop], weight_o, (((1,), (1,)), ((), ())),
            preferred_element_type=f32,
        )
        total = part if total is None else total + part
    gatt[...] = total.astype(bf16)


def convolve(lat, wmain, wext, taps, mixed):
    images, band_rows, columns, channels = lat.shape
    tokens = images * band_rows * columns
    flat = lat[...].reshape(tokens, channels)
    for start, stop in SPANS:
        lanes = slice(128 * start, 128 * stop)
        total = None
        for t in range(9):
            window = taps[t % 3, :, t // 3:t // 3 + band_rows].reshape(tokens, channels)
            part = jnp.dot(
                window, columns_of(wmain, wext, t, start, stop), preferred_element_type=jnp.float32
            )
            total = part if total is None else total + part
        mixed[:, lanes] = (flat[:, lanes].astype(jnp.float32) + total).astype(jnp.bfloat16)


def attend(mixed, wmain, wext, keys, vals, gatt, attended, dquery, block_out):
    images, band_rows, columns, channels = block_out.shape
    f32, bf16 = jnp.float32, jnp.bfloat16
    scale = 1.0 / math.sqrt(HEAD)
    cells = band_rows * columns
    tokens = images * cells
    nt = (((1,), (1,)), ((), ()))
    left = lax.broadcasted_iota(jnp.int32, (cells, 128), 1) < HEAD
    zero = jnp.zeros((cells, 128), bf16)

    def two_heads(value):
        return jnp.concatenate([jnp.where(left, value, zero), jnp.where(left, zero, value)], 0)

    def one_row(value):
        return jnp.where(left, value[:cells], value[cells:]).astype(bf16)

    flat = mixed[...]
    for start, stop in SPANS:
        queries = jnp.dot(
            flat, columns_of(wmain, wext, 9, start, stop), preferred_element_type=f32
        ).astype(bf16)
        for n in range(start, stop):
            lanes = slice(128 * n, 128 * n + 128)
            here = slice(128 * (n - start), 128 * (n - start) + 128)
            for i in range(images):
                rows = slice(cells * i, cells * i + cells)
                key, val = keys[i, :, lanes], vals[i, :, lanes]
                query = two_heads(queries[rows, here])
                grad = two_heads(gatt[rows, lanes])
                scores = lax.dot_general(query, key, nt, preferred_element_type=f32) * scale
                expo = jnp.exp(scores - jnp.max(scores, axis=-1, keepdims=True))
                probs = expo / jnp.sum(expo, axis=-1, keepdims=True)
                dprob = lax.dot_general(grad, val, nt, preferred_element_type=f32)
                inner = jnp.sum(probs * dprob, axis=-1, keepdims=True)
                dscore = (probs * (dprob - inner) * scale).astype(bf16)
                attended[rows, lanes] = one_row(
                    jnp.dot(probs.astype(bf16), val, preferred_element_type=f32)
                )
                dquery[rows, lanes] = one_row(jnp.dot(dscore, key, preferred_element_type=f32))
    for start, stop in SPANS:
        lanes = slice(128 * start, 128 * stop)
        result = flat[:, lanes].astype(f32) + jnp.dot(
            attended[...], columns_of(wmain, wext, 12, start, stop), preferred_element_type=f32
        )
        block_out[:, :, :, lanes] = result.astype(bf16).reshape(
            images, band_rows, columns, 128 * (stop - start)
        )


def reduce_kernel(
    factor,
    ops, perm,
    out,
    rcv, gf, gb, r1, h, r2, total, zs, zr, fin,
    op_sems, s1_send, s1_recv, s2_send, s2_recv, z_sems, o_sems,
):
    me = Spot()
    nz, x, y, z, c, s = me.nz, me.x, me.y, me.z, me.c, me.s
    spatial = 4 * NY
    zh = nz // 2
    small = zh * 5
    big = 4 * small
    twin = me.at(c=1 - c)
    mates = [me.band(wrap(s + k, spatial)) for k in range(1, spatial)]
    away = jnp.where(me.xl == 0, -1, 1)
    greet(
        me,
        mates + [me.at(z=z + k) for k in range(1, nz)] + [me.at(x=x + away), me.at(x=x + 2)],
    )
    send(ops.at[1 - c], rcv, op_sems.at[0], op_sems.at[1], twin)
    own = ops[c]
    await_bytes(rcv, op_sems.at[1])
    lhs = jnp.concatenate([own[0], rcv[0]], axis=0)
    rhs = jnp.concatenate([own[1], rcv[1]], axis=0)
    lhs = jnp.dot(lhs, perm[...], preferred_element_type=jnp.float32).astype(jnp.bfloat16)
    grads = lax.dot_general(
        lhs, rhs, (((0,), (0,)), ((), ())), preferred_element_type=jnp.float32
    ) * factor
    gf[...] = grads
    gb[...] = grads.astype(jnp.bfloat16)
    first = c == 0
    a1 = jnp.where(first, y, x)
    a2 = jnp.where(first, x, y)
    for k in (2, 1, 3):
        to = wrap(a1 + k, 4)
        device = me.at(x=jnp.where(first, x, to), y=jnp.where(first, to, y))
        send(
            gb.at[pl.ds(pl.multiple_of(to * big, 32), big)],
            r1.at[k - 1], s1_send.at[k - 1], s1_recv.at[k - 1], device,
        )
    acc = gf[pl.ds(pl.multiple_of(a1 * big, 32), big)]
    for k in (1, 3, 2):
        await_bytes(r1.at[k - 1], s1_recv.at[k - 1])
        acc = acc + r1[k - 1].astype(jnp.float32)
    h[...] = acc
    for k in (2, 1, 3):
        to = wrap(a2 + k, 4)
        device = me.at(x=jnp.where(first, to, x), y=jnp.where(first, y, to))
        send(
            h.at[pl.ds(pl.multiple_of(to * small, 8), small)],
            r2.at[k - 1], s2_send.at[k - 1], s2_recv.at[k - 1], device,
        )
    acc = h[pl.ds(pl.multiple_of(a2 * small, 8), small)]
    for k in (1, 3, 2):
        await_bytes(r2.at[k - 1], s2_recv.at[k - 1])
        acc = acc + r2[k - 1]
    total[...] = acc
    zs[...] = jnp.zeros_like(zs)
    for i in range(zh):
        zs[i, 0:5, :] = total[5 * i:5 * i + 5, :]
    for i in range(zh):
        to = me.xl * zh + i

        @pl.when(to != z)
        def _():
            send(zs.at[i], zr.at[z], z_sems.at[0], z_sems.at[1], me.at(z=to))

    active = lax.div(z, zh) == me.xl

    @pl.when(active)
    def _():
        zr[z] = zs[z - me.xl * zh]
        await_bytes(zr.at[pl.ds(0, nz - 1)], z_sems.at[1])
        piece = zr[0]
        for i in range(1, nz):
            piece = piece + zr[i]
        fin[...] = piece
        for mate in mates:
            send(fin, out.at[c * NY + y], o_sems.at[0], o_sems.at[1], mate)
        out[c * NY + y] = piece
        await_bytes(out.at[pl.ds(0, 2 * NY - 1)], o_sems.at[1])
        await_bytes(zr.at[pl.ds(0, spatial - 1)], o_sems.at[0])
        await_bytes(zs.at[pl.ds(0, zh - 1)], z_sems.at[0])

    @pl.when(jnp.logical_not(active))
    def _():
        await_bytes(out, o_sems.at[1])
        await_bytes(zs, z_sems.at[0])

    await_bytes(rcv, op_sems.at[0])
    for k in range(3):
        await_bytes(r1.at[k], s1_send.at[k])
        await_bytes(r2.at[k], s2_send.at[k])


def reduce_all(ops, factor):
    nz = lax.axis_size("dp") // 2
    me = Spot()
    spatial = 4 * NY
    zh = nz // 2
    small, big = 5 * zh, 20 * zh
    rows, columns = ops.shape[-1], ops.shape[-1]
    used = 8 * big // 2
    natural = jnp.arange(rows)
    xx = natural // (20 * zh)
    yy = natural % 20 // 5
    place = jnp.where(me.c == 0, yy * 4 + xx, xx * 4 + yy) * small
    place = place + natural // 20 % zh * 5 + natural % 5
    perm = (place[:, None] == jnp.arange(used)[None, :]).astype(jnp.bfloat16)
    bf16, f32 = jnp.bfloat16, jnp.float32
    dma = pltpu.SemaphoreType.DMA
    import functools

    pieces = pl.pallas_call(
        functools.partial(reduce_kernel, factor),
        out_shape=jax.ShapeDtypeStruct((2 * NY, 8, columns), f32),
        in_specs=[pl.BlockSpec(memory_space=pltpu.VMEM)] * 2,
        out_specs=pl.BlockSpec(memory_space=pltpu.VMEM),
        scratch_shapes=[
            pltpu.VMEM(ops.shape[1:], bf16),
            pltpu.VMEM((used, columns), f32),
            pltpu.VMEM((used, columns), bf16),
            pltpu.VMEM((3, big, columns), bf16),
            pltpu.VMEM((big, columns), f32),
            pltpu.VMEM((3, small, columns), f32),
            pltpu.VMEM((small, columns), f32),
            pltpu.VMEM((zh, 8, columns), f32),
            pltpu.VMEM((max(nz, spatial), 8, columns), f32),
            pltpu.VMEM((8, columns), f32),
            dma((2,)), dma((3,)), dma((3,)), dma((3,)), dma((3,)), dma((2,)), dma((2,)),
        ],
        compiler_params=pltpu.CompilerParams(
            collective_id=1, has_side_effects=True, vmem_limit_bytes=VMEM_LIMIT
        ),
        name="reduce_all",
    )(ops, perm)
    pieces = pieces.reshape(2, NY, 8, columns)[:, :, :5]
    return pieces.transpose(1, 2, 0, 3).reshape(20, 2, columns)


def weight_slice(conv_weight, attn_weights):
    me = Spot()
    taps = conv_weight.shape[0] + attn_weights.shape[0]
    rows, channels = conv_weight.shape[1:]
    shard = jnp.concatenate([conv_weight, attn_weights], 0)
    shard = shard.reshape(taps, rows, channels // 128, 128).transpose(0, 2, 1, 3)
    shard = shard.reshape(-1, rows, 128)
    first = 4 * (me.c * 2 * NY + me.xl * NY + me.y)
    own = lax.dynamic_slice_in_dim(shard, first, 4, 0)
    own = jnp.concatenate([own, shard[-1:]], 0).reshape(-1, 128)
    return jnp.pad(own, ((0, 12), (0, 0)))


def body(latents, plan, conv_weight, gn_gain, attn_weights, cotangent):
    images, band_rows, columns, channels = latents.shape
    flat = latents.astype(jnp.float32).reshape(images, band_rows * columns, channels)
    sums = jnp.concatenate(
        [jnp.sum(flat, 1), jnp.sum(flat * flat, 1), jnp.zeros((8 - 2 * images, channels))], 0
    )
    block_out, ops = gather_all(
        weight_slice(conv_weight, attn_weights), latents, plan, sums, cotangent, gn_gain[None]
    )
    cells = images * band_rows * columns
    factor = 1.0 / math.sqrt(cells * lax.axis_size("dp") * lax.axis_size("spatial"))
    return (block_out, reduce_all(ops, factor))


def solution(mesh):
    return jax.shard_map(
        body,
        mesh=mesh,
        in_specs=(
            P("dp", "spatial", None, None),
            P("dp", "spatial", None),
            P(None, "dp", None),
            P(),
            P(None, "dp", None),
            P("dp", "spatial", None, None),
        ),
        out_specs=(P("dp", "spatial", None, None), P("dp", None, None)),
        check_vma=False,
    )
```

```python
import functools
import math

import jax
import jax.numpy as jnp
from jax import lax
from jax.experimental import pallas as pl
from jax.experimental.pallas import tpu as pltpu
from jax.sharding import PartitionSpec as P

GROUPS = 32
HEAD = 64
NX = 4
NY = 4
BANDS = 16
CORE = 2 * NY
SHARD = 20
UNIT = 4 * SHARD
MESH = pl.DeviceIdType.MESH
VMEM_LIMIT = 62 * 1024 * 1024
SPANS = ((0, 2), (2, 4), (4, 5))
BF16 = jnp.bfloat16
F32 = jnp.float32
NT = (((1,), (1,)), ((), ()))

eps_norm = 1e-05


def wrap(value, n):
    return lax.rem(value + n, n)


class Spot:
    def __init__(self, nz):
        self.nz = nz
        self.dp = lax.axis_index("dp")
        self.s = lax.axis_index("spatial")
        self.xh = lax.div(self.dp, nz)
        self.z = lax.rem(self.dp, nz)
        self.xl = lax.div(self.s, CORE)
        self.y = lax.rem(lax.div(self.s, 2), NY)
        self.c = lax.rem(self.s, 2)
        self.x = 2 * self.xh + self.xl

    def at(self, x=None, y=None, z=None, c=None):
        x = self.x if x is None else wrap(x, NX)
        y = self.y if y is None else wrap(y, NY)
        z = self.z if z is None else wrap(z, self.nz)
        c = self.c if c is None else c
        return (lax.div(x, 2) * self.nz + z, (lax.rem(x, 2) * NY + y) * 2 + c)

    def sid(self, x, y):
        return self.c * CORE + lax.rem(wrap(x, NX), 2) * NY + wrap(y, NY)


def send(src, dst, send_sem, recv_sem, device):
    pltpu.make_async_remote_copy(
        src_ref=src,
        dst_ref=dst,
        send_sem=send_sem,
        recv_sem=recv_sem,
        device_id=device,
        device_id_type=MESH,
    ).start()


def await_bytes(ref, sem):
    pltpu.make_async_copy(ref, ref, sem).wait()


def reach(nz):
    steps = [0]
    for k in range(1, nz // 2):
        steps += [k, -k]
    return steps + [nz // 2]


def ints(shape, axis):
    return lax.broadcasted_iota(jnp.int32, shape, axis)


def floor_of(values, width):
    return jnp.floor((values + 0.5) * (1.0 / width))


def one_hot(names, rows):
    at = ints((rows, names.shape[1]), 0).astype(F32)
    return jnp.where(at == names, 1.0, 0.0).astype(BF16)


def arrival_order(me, channels):
    nz = me.nz
    bits = nz.bit_length() - 1
    place = ints((1, channels), 1)
    head = 2 * nz * 16
    late = place - head
    main = place < head
    slot = jnp.where(main, place >> 4, late >> 2)
    row = jnp.where(main, place & 15, 16 + (late & 3))
    half, slot = slot >> bits, slot & (nz - 1)
    step = jnp.where((slot & 1) == 1, (slot + 1) >> 1, -(slot >> 1))
    names = (half * nz + ((me.z + step + nz) & (nz - 1))) * SHARD + row
    return one_hot(names.astype(F32), channels)


def scatter_order(me, channels):
    zh = me.nz // 2
    small = 5 * zh
    place = ints((1, channels), 1).astype(F32)
    outer = floor_of(place, 4 * small)
    place = place - outer * (4 * small)
    inner = floor_of(place, small)
    place = place - inner * small
    zi = floor_of(place, 5)
    i = place - 5 * zi
    first = me.c == 0
    xx = jnp.where(first, inner, outer)
    yy = jnp.where(first, outer, inner)
    names = (xx * zh + zi) * SHARD + yy * 5 + i
    return one_hot(names, channels)


def group_table(channels):
    rows = ints((channels, 128), 0).astype(F32)
    lanes = ints((channels, 128), 1).astype(F32)
    return jnp.where(floor_of(rows, channels // GROUPS) == lanes, 1.0, 0.0)


def own_slice(me, conv, attn, wslice, extra, spare):
    taps, _, channels = conv.shape
    per = channels // 128
    first = 4 * me.sid(me.x, me.y)
    for j in range(4):
        block = first + j
        matrix = lax.div(block, per)
        lanes = pl.ds(pl.multiple_of(lax.rem(block, per) * 128, 128), 128)
        one = conv[jnp.minimum(matrix, taps - 1), :, lanes].astype(F32)
        two = attn[jnp.maximum(matrix - taps, 0), :, lanes].astype(F32)
        rows = jnp.where(matrix < taps, one, two)
        wslice[16 * j:16 * j + 16, :] = rows[0:16].astype(BF16)
        spare[4 * j:4 * j + 4, :] = rows[16:20]
    wslice[64:80, :] = spare[...].astype(BF16)
    extra[0:20, :] = attn[attn.shape[0] - 1, :, channels - 128:channels]
    extra[20:32, :] = jnp.zeros((12, 128), BF16)


def band_sums(lat, table, sums):
    images, band_rows, columns, channels = lat.shape
    rows = []
    for power in (1, 2):
        for i in range(images):
            cells = lat[i].reshape(band_rows * columns, channels).astype(F32)
            rows.append(jnp.sum(cells * cells if power == 2 else cells, axis=0, keepdims=True))
    rows.append(jnp.zeros((8 - 2 * images, channels), F32))
    sums[...] = jnp.dot(
        jnp.concatenate(rows, axis=0), table,
        preferred_element_type=F32, precision=lax.Precision.HIGHEST,
    )


def norm_taps(me, lat, gain, halo, sbuf, order, taps):
    images, band_rows, columns, channels = lat.shape
    tot = sbuf[0]
    for i in range(1, BANDS):
        tot = tot + sbuf[i]
    grouped = lax.dot_general(
        tot, group_table(channels), NT, preferred_element_type=F32, precision=lax.Precision.HIGHEST
    )
    counted = float(band_rows * BANDS * columns * (channels // GROUPS))
    row_at = ints((columns, channels), 0)
    for i in range(images):
        mean = grouped[i:i + 1] / counted
        variance = grouped[images + i:images + i + 1] / counted - mean * mean
        inverse = lax.rsqrt(variance + eps_norm)
        for r in range(band_rows + 2):
            if r == 0:
                cells = halo[0, i]
            elif r == band_rows + 1:
                cells = halo[1, i]
            else:
                cells = lat[i, r - 1]
            normed = (cells.astype(F32) - mean) * inverse * gain[...]
            hidden = (normed / (1.0 + jnp.exp(-normed))).astype(BF16)
            hidden = jnp.dot(hidden, order[...], preferred_element_type=F32)
            if r == 0:
                hidden = jnp.where(me.s == 0, 0.0, hidden)
            if r == band_rows + 1:
                hidden = jnp.where(me.s == BANDS - 1, 0.0, hidden)
            before = jnp.where(row_at == 0, 0.0, pltpu.roll(hidden, 1, 0))
            after = jnp.where(row_at == columns - 1, 0.0, pltpu.roll(hidden, columns - 1, 0))
            taps[0, i, r] = before.astype(BF16)
            taps[1, i, r] = hidden.astype(BF16)
            taps[2, i, r] = after.astype(BF16)


class Weights:
    def __init__(self, wmain, wext, wleft):
        self.wmain, self.wext, self.wleft = wmain, wext, wleft

    def gather_left(self):
        wmain, wext, wleft = self.wmain, self.wext, self.wleft
        count = wmain.shape[1] * wmain.shape[2] * 4
        low = ints((count // 2, 8, 128), 1) < 4

        def paired(tile):
            tile = tile.reshape(count // 2, 2, 8, 128)
            even, odd = tile[:, 0], tile[:, 1]
            first = jnp.where(low, even, pltpu.roll(odd, 4, 1))
            second = jnp.where(low, pltpu.roll(even, 4, 1), odd)
            return [v.reshape(count * 4, 128).astype(BF16) for v in (first, second)]

        def step(sid, carry):
            tile = wmain[sid, :, :, :, :, 64:80, :].reshape(count, 16, 128).astype(F32)
            for part in range(2):
                first, second = paired(tile[:, 8 * part:8 * part + 8])
                wleft[4 * sid + 2 * part] = first
                wleft[4 * sid + 2 * part + 1] = second
            return carry

        lax.fori_loop(0, wmain.shape[0], step, 0)
        tile = wext[:, :, 16:32, :].reshape(count, 16, 128).astype(F32)
        wleft[4 * wmain.shape[0]] = paired(tile[:, 0:8])[0]

    def block(self, index):
        wmain, wext = self.wmain, self.wext
        if index < 4 * wmain.shape[0]:
            j = index % 4
            head = wmain[index // 4, :, :, :, :, 16 * j:16 * j + 16, :]
        else:
            head = wext[:, :, 0:16, :]
        return jnp.concatenate([head.reshape(-1, 128), self.wleft[index]], axis=0)

    def columns(self, matrix, start, stop):
        parts = [self.block(5 * matrix + n) for n in range(start, stop)]
        return parts[0] if len(parts) == 1 else jnp.concatenate(parts, axis=1)


def order_plan(planb, order):
    images, bands, plan_rows, channels = planb.shape
    for i in range(images):
        rows = planb[i].reshape(bands * plan_rows, channels)
        rows = jnp.dot(rows, order[...], preferred_element_type=F32).astype(BF16)
        planb[i] = rows.reshape(bands, plan_rows, channels)


def plan_side(cot, planb, weights, order, keys, vals, gatt):
    images, bands, plan_rows, channels = planb.shape
    for start, stop in SPANS:
        lanes = slice(128 * start, 128 * stop)
        weight_k = weights.columns(10, start, stop)
        weight_v = weights.columns(11, start, stop)
        for i in range(images):
            rows = planb[i].reshape(bands * plan_rows, channels)
            keys[i, :, lanes] = jnp.dot(rows, weight_k, preferred_element_type=F32).astype(BF16)
            vals[i, :, lanes] = jnp.dot(rows, weight_v, preferred_element_type=F32).astype(BF16)
    total = None
    flat = cot[...].reshape(-1, channels)
    for start, stop in SPANS:
        part = lax.dot_general(
            flat[:, 128 * start:128 * stop], weights.columns(12, start, stop), NT,
            preferred_element_type=F32,
        )
        total = part if total is None else total + part
    total = lax.dot_general(total.astype(BF16), order[...], NT, preferred_element_type=F32)
    gatt[...] = total.astype(BF16)


def convolve(lat, weights, taps, mixed):
    images, band_rows, columns, channels = lat.shape
    tokens = images * band_rows * columns
    flat = lat[...].reshape(tokens, channels)
    for start, stop in SPANS:
        lanes = slice(128 * start, 128 * stop)
        total = None
        for t in range(9):
            window = taps[t % 3, :, t // 3:t // 3 + band_rows].reshape(tokens, channels)
            part = jnp.dot(window, weights.columns(t, start, stop), preferred_element_type=F32)
            total = part if total is None else total + part
        mixed[:, lanes] = (flat[:, lanes].astype(F32) + total).astype(BF16)


def attend(mixed, weights, order, keys, vals, gatt, attended, dquery, block_out):
    images, band_rows, columns, channels = block_out.shape
    scale = 1.0 / math.sqrt(HEAD)
    cells = band_rows * columns
    left = ints((cells, 128), 1) < HEAD
    zero = jnp.zeros((cells, 128), BF16)

    def two_heads(value):
        return jnp.concatenate([jnp.where(left, value, zero), jnp.where(left, zero, value)], 0)

    def one_row(value):
        return jnp.where(left, value[:cells], value[cells:]).astype(BF16)

    flat = mixed[...]
    ordered = jnp.dot(flat, order[...], preferred_element_type=F32).astype(BF16)
    for start, stop in SPANS:
        queries = jnp.dot(
            ordered, weights.columns(9, start, stop), preferred_element_type=F32
        ).astype(BF16)
        for n in range(start, stop):
            lanes = slice(128 * n, 128 * n + 128)
            here = slice(128 * (n - start), 128 * (n - start) + 128)
            for i in range(images):
                rows = slice(cells * i, cells * i + cells)
                key, val = keys[i, :, lanes], vals[i, :, lanes]
                query = two_heads(queries[rows, here])
                grad = two_heads(gatt[rows, lanes])
                scores = lax.dot_general(query, key, NT, preferred_element_type=F32) * scale
                expo = jnp.exp(scores - jnp.max(scores, axis=-1, keepdims=True))
                probs = expo / jnp.sum(expo, axis=-1, keepdims=True)
                dprob = lax.dot_general(grad, val, NT, preferred_element_type=F32)
                inner = jnp.sum(probs * dprob, axis=-1, keepdims=True)
                dscore = (probs * (dprob - inner) * scale).astype(BF16)
                attended[rows, lanes] = one_row(
                    jnp.dot(probs.astype(BF16), val, preferred_element_type=F32)
                )
                dquery[rows, lanes] = one_row(jnp.dot(dscore, key, preferred_element_type=F32))
    ordered = jnp.dot(attended[...], order[...], preferred_element_type=F32).astype(BF16)
    for start, stop in SPANS:
        lanes = slice(128 * start, 128 * stop)
        result = flat[:, lanes].astype(F32) + jnp.dot(
            ordered, weights.columns(12, start, stop), preferred_element_type=F32
        )
        block_out[:, :, :, lanes] = result.astype(BF16).reshape(
            images, band_rows, columns, 128 * (stop - start)
        )


def reduce_gradient(
    me, factor, ops, perm, out,
    rcv, gf, gb, r1, h, r2, total, zs, zr, fin,
    op_sems, s1_send, s1_recv, s2_send, s2_recv, z_send, z_recv, o_send, o_recv,
):
    nz, x, y, z, c = me.nz, me.x, me.y, me.z, me.c
    zh = nz // 2
    small = zh * 5
    big = 4 * small
    twin = me.at(c=1 - c)
    mates = [(me.dp, wrap(me.s + k, BANDS)) for k in range(1, BANDS)]
    spans = [pl.ds(128 * a, 128 * (b - a)) for a, b in SPANS]
    send(ops.at[1 - c], rcv, op_sems.at[0], op_sems.at[1], twin)
    own = ops[c]
    lhs_own = jnp.dot(own[0], perm[...], preferred_element_type=F32).astype(BF16)
    await_bytes(rcv, op_sems.at[1])
    lhs_far = jnp.dot(rcv[0], perm[...], preferred_element_type=F32).astype(BF16)
    lhs = jnp.concatenate([lhs_own, lhs_far], axis=0)
    first = c == 0
    a1 = jnp.where(first, y, x)
    a2 = jnp.where(first, x, y)
    active = lax.div(z, zh) == me.xl
    for p, (start, stop) in enumerate(SPANS):
        lanes = slice(128 * start, 128 * stop)
        rhs = jnp.concatenate([own[1][:, lanes], rcv[1, :, lanes]], axis=0)
        grads = lax.dot_general(
            lhs, rhs, (((0,), (0,)), ((), ())), preferred_element_type=F32
        ) * factor
        gf[:, lanes] = grads
        gb[:, lanes] = grads.astype(BF16)
        for k in (2, 1, 3):
            to = wrap(a1 + k, 4)
            device = me.at(x=jnp.where(first, x, to), y=jnp.where(first, to, y))
            send(
                gb.at[pl.ds(pl.multiple_of(to * big, 32), big), spans[p]],
                r1.at[k - 1, :, spans[p]], s1_send.at[p], s1_recv.at[p], device,
            )

    def part_two(p):
        span = spans[p]
        await_bytes(r1.at[:, :, span], s1_recv.at[p])
        acc = gf[pl.ds(pl.multiple_of(a1 * big, 32), big), span]
        for k in range(3):
            acc = acc + r1[k, :, span].astype(F32)
        h[:, span] = acc
        for k in (2, 1, 3):
            to = wrap(a2 + k, 4)
            device = me.at(x=jnp.where(first, to, x), y=jnp.where(first, y, to))
            send(
                h.at[pl.ds(pl.multiple_of(to * small, 8), small), span],
                r2.at[k - 1, :, span], s2_send.at[p], s2_recv.at[p], device,
            )

    def part_three(p):
        span = spans[p]
        await_bytes(r2.at[:, :, span], s2_recv.at[p])
        acc = h[pl.ds(pl.multiple_of(a2 * small, 8), small), span]
        for k in range(3):
            acc = acc + r2[k, :, span]
        total[:, span] = acc
        for i in range(zh):
            zs[i, 0:5, span] = total[5 * i:5 * i + 5, span]
        for i in range(zh):
            to = me.xl * zh + i

            @pl.when(to != z)
            def _():
                send(
                    zs.at[i, :, span], zr.at[z, :, span],
                    z_send.at[p], z_recv.at[p], me.at(z=to),
                )

    zs[...] = jnp.zeros_like(zs)
    part_two(0)
    part_two(1)
    part_three(0)
    part_two(2)
    part_three(1)
    part_three(2)

    @pl.when(active)
    def _():
        for p, span in enumerate(spans):
            zr[z, :, span] = zs[z - me.xl * zh, :, span]
            await_bytes(zr.at[pl.ds(0, nz - 1), :, span], z_recv.at[p])
            piece = zr[0, :, span]
            for i in range(1, nz):
                piece = piece + zr[i, :, span]
            fin[:, span] = piece
            for mate in mates:
                send(
                    fin.at[:, span], out.at[c * NY + y, :, span], o_send.at[p], o_recv.at[p], mate
                )
            out[c * NY + y, :, span] = piece
        for p, span in enumerate(spans):
            await_bytes(out.at[pl.ds(0, CORE - 1), :, span], o_recv.at[p])
            await_bytes(zr.at[pl.ds(0, BANDS - 1), :, span], o_send.at[p])
            await_bytes(zs.at[pl.ds(0, zh - 1), :, span], z_send.at[p])

    @pl.when(jnp.logical_not(active))
    def _():
        for p, span in enumerate(spans):
            await_bytes(out.at[:, :, span], o_recv.at[p])
            await_bytes(zs.at[:, :, span], z_send.at[p])

    await_bytes(rcv, op_sems.at[0])
    for p, span in enumerate(spans):
        await_bytes(r1.at[:, :, span], s1_send.at[p])
        await_bytes(r2.at[:, :, span], s2_send.at[p])


def block_kernel(
    nz, factor,
    lat, plan, conv, attn, gain, cot,
    block_out, grad_out,
    wmain, wext, wleft, wslice, extra, spare, sums, planb, halo, sbuf, order, perm,
    taps, keys, vals, gatt, ops,
    rcv, gf, gb, r1, h, r2, total, zs, zr, fin,
    z_send, z_recv, x_sems, a_send, b_send, c_send, d_send, f_send,
    a_recv, b_recv, c_recv, d_recv, f_recv, misc_send, misc_recv,
    op_sems, s1_send, s1_recv, s2_send, s2_recv, g_send, g_recv, o_send, o_recv,
):
    me = Spot(nz)
    x, y, z, c, s = me.x, me.y, me.z, me.c, me.s
    channels = lat.shape[-1]
    rounds = nz // 4
    twin = me.at(c=1 - c)
    north, south = me.at(y=y + 1), me.at(y=y - 1)
    east, west = me.at(x=x + 1), me.at(x=x - 1)
    side = jnp.where(me.xl == 0, -1, 1)
    other_x = me.at(x=x + side)
    mates = [(me.dp, wrap(s + k, BANDS)) for k in range(1, BANDS)]
    greeted = mates + [me.at(z=z + k) for k in range(1, nz)] + [other_x, me.at(x=x + 2)]
    barrier = pltpu.get_barrier_semaphore()
    for device in greeted:
        pl.semaphore_signal(barrier, inc=1, device_id=device, device_id_type=MESH)
    my_sid = me.sid(x, y)
    own_slice(me, conv, attn, wslice, extra, spare)
    band_sums(lat, group_table(channels), sums)
    pl.semaphore_wait(barrier, len(greeted))

    steps = reach(nz)
    for slot, step in enumerate(steps):
        if slot:
            back = steps.index(-step) if -step in steps else slot
            send(
                wslice, wmain.at[my_sid, me.xh, back // 4, back % 4 // 2, back % 2],
                z_send, z_recv.at[back // 4], me.at(z=z + step),
            )
    for mate in mates:
        send(sums, sbuf.at[s], misc_send.at[0], misc_recv.at[0], mate)
    send(lat.at[:, 0], halo.at[1], misc_send.at[1], misc_recv.at[1], (me.dp, wrap(s - 1, BANDS)))
    send(lat.at[:, 1], halo.at[0], misc_send.at[2], misc_recv.at[2], (me.dp, wrap(s + 1, BANDS)))

    @pl.when(c == 0)
    def _():
        for slot, step in enumerate(steps):
            if slot:
                back = steps.index(-step) if -step in steps else slot
                send(extra, wext.at[me.xh, back], x_sems.at[0], x_sems.at[1], me.at(z=z + step))

    pair = (me.dp, ((1 - me.xl) * NY + y) * 2 + c)
    send(plan, planb.at[:, my_sid], misc_send.at[3], misc_recv.at[3], pair)
    for k in (1, 3, 2):
        send(plan, planb.at[:, my_sid], misc_send.at[4], misc_recv.at[4], me.at(y=y + k))

    wmain[my_sid, me.xh, 0, 0, 0] = wslice[...]
    wext[me.xh, 0] = extra[...]
    planb[:, my_sid] = plan[...]
    sbuf[s] = sums[...]
    order[...] = arrival_order(me, channels)
    every = slice(None)

    def block(r, xx, yy, colours, dirs):
        return wmain.at[me.sid(xx, yy), lax.div(wrap(xx, NX), 2), r, colours, dirs]

    def move(r, xx, yy, colours, dirs, send_sem, recv_sem, device):
        ref = block(r, xx, yy, colours, dirs)
        send(ref, ref, send_sem, recv_sem, device)

    def hand_over(r, cells):
        for i, j in cells:
            move(r, x + i, y + j, every, every, f_send, f_recv, twin)

    def units(n):
        return wmain.at[pl.ds(0, n), 0, 0]

    def part_a(r):
        await_bytes(zwait(r), z_recv.at[r])
        for device in (east, west, north, south):
            move(r, x, y, every, every, a_send, a_recv.at[r], device)
        hand_over(r, [(0, 0)])

    def zwait(r):
        return wmain.at[pl.ds(0, 3), 0, 0, 0, 0] if r == 0 else wmain.at[pl.ds(0, 4), 0, 0, 0, 0]

    def part_b(r):
        await_bytes(units(4), a_recv.at[r])
        low, high = pl.ds(0, 1), pl.ds(1, 1)
        move(r, x - 1, y, every, low, b_send, b_recv.at[r], east)
        move(r, x + 1, y, every, high, b_send, b_recv.at[r], west)
        move(r, x, y - 1, every, low, b_send, b_recv.at[r], north)
        move(r, x, y + 1, every, high, b_send, b_recv.at[r], south)
        for k in (1, -1):
            for device in (north, south):
                move(r, x + k, y, low, every, c_send, c_recv.at[r], device)
            for device in (east, west):
                move(r, x, y + k, high, every, c_send, c_recv.at[r], device)
        hand_over(r, [(1, 0), (-1, 0), (0, 1), (0, -1)])

    def part_c(r):
        await_bytes(units(2), b_recv.at[r])
        low, high = pl.ds(0, 1), pl.ds(1, 1)
        for device in (north, south):
            move(r, x + 2, y, low, every, c_send, c_recv.at[r], device)
        for device in (east, west):
            move(r, x, y + 2, high, every, c_send, c_recv.at[r], device)
        hand_over(r, [(2, 0), (0, 2)])

    def part_d(r):
        await_bytes(units(6), c_recv.at[r])
        low, high = pl.ds(0, 1), pl.ds(1, 1)
        for k in (1, -1, 2):
            move(r, x + k, y - 1, low, low, d_send, d_recv.at[r], north)
            move(r, x + k, y + 1, low, high, d_send, d_recv.at[r], south)
            move(r, x - 1, y + k, high, low, d_send, d_recv.at[r], east)
            move(r, x + 1, y + k, high, high, d_send, d_recv.at[r], west)
        hand_over(r, [(1, 1), (1, -1), (-1, 1), (-1, -1)])

    def part_e(r):
        await_bytes(units(3), d_recv.at[r])
        hand_over(r, [(1, 2), (-1, 2), (2, 1), (2, -1), (2, 2)])

    def normalise():
        await_bytes(sbuf.at[pl.ds(0, BANDS - 1)], misc_recv.at[0])
        await_bytes(halo.at[0], misc_recv.at[1])
        await_bytes(halo.at[0], misc_recv.at[2])
        norm_taps(me, lat, gain, halo, sbuf, order, taps)

    def plan_two():
        await_bytes(planb.at[:, 0], misc_recv.at[3])
        theirs = planb.at[:, c * CORE + (1 - me.xl) * NY + y]
        for k in (1, 3, 2):
            send(theirs, theirs, misc_send.at[5], misc_recv.at[5], me.at(y=y + k))

    def plan_three():
        await_bytes(planb.at[:, pl.ds(0, 3)], misc_recv.at[4])
        await_bytes(planb.at[:, pl.ds(0, 3)], misc_recv.at[5])
        mine = planb.at[:, pl.ds(c * CORE, CORE)]
        send(mine, mine, misc_send.at[6], misc_recv.at[6], twin)

    def plan_four():
        await_bytes(planb.at[:, pl.ds(0, CORE)], misc_recv.at[6])
        await_bytes(planb.at[:, pl.ds(0, CORE)], misc_send.at[6])
        await_bytes(planb.at[:, 0], misc_send.at[3])
        await_bytes(planb.at[:, pl.ds(0, 3)], misc_send.at[4])
        await_bytes(planb.at[:, pl.ds(0, 3)], misc_send.at[5])
        order_plan(planb, order)
        perm[...] = scatter_order(me, channels)

    part_a(0)
    plan_two()
    normalise()
    part_b(0)
    for r in range(1, rounds):
        part_a(r)
        part_c(r - 1)
        if r == 1:
            plan_three()
        if r > 1:
            part_e(r - 2)
        part_b(r)
        part_d(r - 1)
        if r == 2:
            plan_four()
    if rounds < 3:
        if rounds < 2:
            plan_three()
        plan_four()
    if rounds > 1:
        part_c(rounds - 1)
        part_e(rounds - 2)
    else:
        part_c(0)

    @pl.when(c == 0)
    def _():
        await_bytes(wext.at[0, pl.ds(0, nz - 1)], x_sems.at[1])
        half = wext.at[me.xh]
        send(half, half, x_sems.at[2], x_sems.at[3], other_x)

    part_d(rounds - 1)
    part_e(rounds - 1)

    @pl.when(c == 0)
    def _():
        await_bytes(wext.at[0], x_sems.at[3])
        send(wext, wext, x_sems.at[4], x_sems.at[5], twin)

    await_bytes(wmain.at[pl.ds(0, CORE)], f_recv)

    @pl.when(c == 0)
    def _():
        await_bytes(wext.at[0, pl.ds(0, nz - 1)], x_sems.at[0])
        await_bytes(wext.at[0], x_sems.at[2])
        await_bytes(wext, x_sems.at[4])

    @pl.when(c != 0)
    def _():
        await_bytes(wext, x_sems.at[5])

    weights = Weights(wmain, wext, wleft)
    weights.gather_left()
    plan_side(cot, planb, weights, order, keys, vals, gatt)
    convolve(lat, weights, taps, ops.at[0, 0])
    attend(
        ops.at[0, 0], weights, order, keys, vals, gatt, ops.at[1, 0], ops.at[0, 1], block_out
    )
    ops[1, 1] = cot[...].reshape(ops.shape[2:])
    reduce_gradient(
        me, factor, ops, perm, grad_out,
        rcv, gf, gb, r1, h, r2, total, zs, zr, fin,
        op_sems, s1_send, s1_recv, s2_send, s2_recv, g_send, g_recv, o_send, o_recv,
    )

    await_bytes(sbuf.at[pl.ds(0, BANDS - 1)], misc_send.at[0])
    await_bytes(halo.at[0], misc_send.at[1])
    await_bytes(halo.at[0], misc_send.at[2])
    await_bytes(wmain.at[pl.ds(0, nz - 1), 0, 0, 0, 0], z_send)
    await_bytes(wmain.at[pl.ds(0, 4), 0], a_send)
    await_bytes(wmain.at[pl.ds(0, 2), 0], b_send)
    await_bytes(wmain.at[pl.ds(0, 6), 0], c_send)
    await_bytes(wmain.at[pl.ds(0, 3), 0], d_send)
    await_bytes(wmain.at[pl.ds(0, CORE)], f_send)


def body(latents, plan, conv_weight, gn_gain, attn_weights, cotangent):
    images, band_rows, columns, channels = latents.shape
    nz = lax.axis_size("dp") // 2
    tokens = images * band_rows * columns
    plan_tokens = BANDS * plan.shape[1]
    factor = 1.0 / math.sqrt(tokens * 2 * nz * BANDS)
    zh = nz // 2
    small, big = 5 * zh, 20 * zh
    rounds = nz // 4
    dma = pltpu.SemaphoreType.DMA
    vmem = pltpu.VMEM
    block_out, pieces = pl.pallas_call(
        functools.partial(block_kernel, nz, factor),
        out_shape=[
            jax.ShapeDtypeStruct(latents.shape, BF16),
            jax.ShapeDtypeStruct((CORE, 8, channels), F32),
        ],
        in_specs=[pl.BlockSpec(memory_space=vmem)] * 6,
        out_specs=[pl.BlockSpec(memory_space=vmem)] * 2,
        scratch_shapes=[
            vmem((BANDS, 2, rounds, 2, 2, UNIT, 128), BF16),
            vmem((2, nz, 32, 128), BF16),
            vmem((65, 2 * nz * 4, 128), BF16),
            vmem((UNIT, 128), BF16),
            vmem((32, 128), BF16),
            vmem((16, 128), F32),
            vmem((8, 128), F32),
            vmem((images, BANDS) + plan.shape[1:], BF16),
            vmem((2, images, columns, channels), BF16),
            vmem((BANDS, 8, 128), F32),
            vmem((channels, channels), BF16),
            vmem((channels, channels), BF16),
            vmem((3, images, band_rows + 2, columns, channels), BF16),
            vmem((images, plan_tokens, channels), BF16),
            vmem((images, plan_tokens, channels), BF16),
            vmem((tokens, channels), BF16),
            vmem((2, 2, tokens, channels), BF16),
            vmem((2, tokens, channels), BF16),
            vmem((4 * big, channels), F32),
            vmem((4 * big, channels), BF16),
            vmem((3, big, channels), BF16),
            vmem((big, channels), F32),
            vmem((3, small, channels), F32),
            vmem((small, channels), F32),
            vmem((zh, 8, channels), F32),
            vmem((max(nz, BANDS), 8, channels), F32),
            vmem((8, channels), F32),
            dma, dma((rounds,)), dma((6,)), dma, dma, dma, dma, dma,
            dma((rounds,)), dma((rounds,)), dma((rounds,)), dma((rounds,)), dma, dma((7,)), dma((7,)),
            dma((2,)), dma((3,)), dma((3,)), dma((3,)), dma((3,)), dma((3,)), dma((3,)),
            dma((3,)), dma((3,)),
        ],
        compiler_params=pltpu.CompilerParams(
            collective_id=0, has_side_effects=True, vmem_limit_bytes=VMEM_LIMIT
        ),
        name="block",
    )(latents, plan, conv_weight, attn_weights, gn_gain[None], cotangent)
    pieces = pieces.reshape(2, NY, 8, channels)[:, :, :5]
    return (block_out, pieces.transpose(1, 2, 0, 3).reshape(20, 2, channels))


def solution(mesh):
    return jax.shard_map(
        body,
        mesh=mesh,
        in_specs=(
            P("dp", "spatial", None, None),
            P("dp", "spatial", None),
            P(None, "dp", None),
            P(),
            P(None, "dp", None),
            P("dp", "spatial", None, None),
        ),
        out_specs=(P("dp", "spatial", None, None), P("dp", None, None)),
        check_vma=False,
    )
```

```python
import functools
import math

import jax
import jax.numpy as jnp
from jax import lax
from jax.experimental import pallas as pl
from jax.experimental.pallas import tpu as pltpu
from jax.sharding import PartitionSpec as P

GROUPS = 32
HEAD = 64
NX = 4
NY = 4
BANDS = 16
CORE = 2 * NY
SHARD = 20
UNIT = 4 * SHARD
MESH = pl.DeviceIdType.MESH
VMEM_LIMIT = 62 * 1024 * 1024
SPANS = ((0, 2), (2, 4), (4, 5))
BF16 = jnp.bfloat16
F32 = jnp.float32
NT = (((1,), (1,)), ((), ()))

eps_norm = 1e-05


def wrap(value, n):
    return lax.rem(value + n, n)


class Spot:
    def __init__(self, nz):
        self.nz = nz
        self.dp = lax.axis_index("dp")
        self.s = lax.axis_index("spatial")
        self.xh = lax.div(self.dp, nz)
        self.z = lax.rem(self.dp, nz)
        self.xl = lax.div(self.s, CORE)
        self.y = lax.rem(lax.div(self.s, 2), NY)
        self.c = lax.rem(self.s, 2)
        self.x = 2 * self.xh + self.xl

    def at(self, x=None, y=None, z=None, c=None):
        x = self.x if x is None else wrap(x, NX)
        y = self.y if y is None else wrap(y, NY)
        z = self.z if z is None else wrap(z, self.nz)
        c = self.c if c is None else c
        return (lax.div(x, 2) * self.nz + z, (lax.rem(x, 2) * NY + y) * 2 + c)

    def sid(self, x, y):
        return self.c * CORE + lax.rem(wrap(x, NX), 2) * NY + wrap(y, NY)


def send(src, dst, send_sem, recv_sem, device):
    pltpu.make_async_remote_copy(
        src_ref=src,
        dst_ref=dst,
        send_sem=send_sem,
        recv_sem=recv_sem,
        device_id=device,
        device_id_type=MESH,
    ).start()


def await_bytes(ref, sem):
    pltpu.make_async_copy(ref, ref, sem).wait()


def reach(nz):
    steps = [0]
    for k in range(1, nz // 2):
        steps += [k, -k]
    return steps + [nz // 2]


def ints(shape, axis):
    return lax.broadcasted_iota(jnp.int32, shape, axis)


def floor_of(values, width):
    return jnp.floor((values + 0.5) * (1.0 / width))


def one_hot(names, rows):
    at = ints((rows, names.shape[1]), 0).astype(F32)
    return jnp.where(at == names, 1.0, 0.0).astype(BF16)


def arrival_order(me, channels):
    nz = me.nz
    bits = nz.bit_length() - 1
    place = ints((1, channels), 1)
    head = 2 * nz * 16
    late = place - head
    main = place < head
    slot = jnp.where(main, place >> 4, late >> 2)
    row = jnp.where(main, place & 15, 16 + (late & 3))
    half, slot = slot >> bits, slot & (nz - 1)
    step = jnp.where((slot & 1) == 1, (slot + 1) >> 1, -(slot >> 1))
    names = (half * nz + ((me.z + step + nz) & (nz - 1))) * SHARD + row
    return one_hot(names.astype(F32), channels)


def scatter_order(me, channels):
    zh = me.nz // 2
    small = 5 * zh
    place = ints((1, channels), 1).astype(F32)
    outer = floor_of(place, 4 * small)
    place = place - outer * (4 * small)
    inner = floor_of(place, small)
    place = place - inner * small
    zi = floor_of(place, 5)
    i = place - 5 * zi
    first = me.c == 0
    xx = jnp.where(first, inner, outer)
    yy = jnp.where(first, outer, inner)
    half = floor_of(xx, 2)
    names = (half * me.nz + 2 * zi + xx - 2 * half) * SHARD + yy * 5 + i
    return one_hot(names, channels)


def group_table(channels):
    rows = ints((channels, 128), 0).astype(F32)
    lanes = ints((channels, 128), 1).astype(F32)
    return jnp.where(floor_of(rows, channels // GROUPS) == lanes, 1.0, 0.0)


def own_slice(me, conv, attn, wslice, extra, spare):
    taps, _, channels = conv.shape
    per = channels // 128
    first = 4 * me.sid(me.x, me.y)
    for j in range(4):
        block = first + j
        matrix = lax.div(block, per)
        lanes = pl.ds(pl.multiple_of(lax.rem(block, per) * 128, 128), 128)
        one = conv[jnp.minimum(matrix, taps - 1), :, lanes].astype(F32)
        two = attn[jnp.maximum(matrix - taps, 0), :, lanes].astype(F32)
        rows = jnp.where(matrix < taps, one, two)
        wslice[16 * j:16 * j + 16, :] = rows[0:16].astype(BF16)
        spare[4 * j:4 * j + 4, :] = rows[16:20]
    wslice[64:80, :] = spare[...].astype(BF16)
    extra[0:20, :] = attn[attn.shape[0] - 1, :, channels - 128:channels]
    extra[20:32, :] = jnp.zeros((12, 128), BF16)


def band_sums(lat, table, sums):
    images, band_rows, columns, channels = lat.shape
    rows = []
    for power in (1, 2):
        for i in range(images):
            cells = lat[i].reshape(band_rows * columns, channels).astype(F32)
            rows.append(jnp.sum(cells * cells if power == 2 else cells, axis=0, keepdims=True))
    rows.append(jnp.zeros((8 - 2 * images, channels), F32))
    sums[...] = jnp.dot(
        jnp.concatenate(rows, axis=0), table,
        preferred_element_type=F32, precision=lax.Precision.HIGHEST,
    )


def norm_taps(me, lat, gain, halo, sbuf, order, taps):
    images, band_rows, columns, channels = lat.shape
    tot = sbuf[0]
    for i in range(1, BANDS):
        tot = tot + sbuf[i]
    grouped = lax.dot_general(
        tot, group_table(channels), NT, preferred_element_type=F32, precision=lax.Precision.HIGHEST
    )
    counted = float(band_rows * BANDS * columns * (channels // GROUPS))
    row_at = ints((columns, channels), 0)
    for i in range(images):
        mean = grouped[i:i + 1] / counted
        variance = grouped[images + i:images + i + 1] / counted - mean * mean
        inverse = lax.rsqrt(variance + eps_norm)
        for r in range(band_rows + 2):
            if r == 0:
                cells = halo[0, i]
            elif r == band_rows + 1:
                cells = halo[1, i]
            else:
                cells = lat[i, r - 1]
            normed = (cells.astype(F32) - mean) * inverse * gain[...]
            hidden = (normed / (1.0 + jnp.exp(-normed))).astype(BF16)
            hidden = jnp.dot(hidden, order[...], preferred_element_type=F32)
            if r == 0:
                hidden = jnp.where(me.s == 0, 0.0, hidden)
            if r == band_rows + 1:
                hidden = jnp.where(me.s == BANDS - 1, 0.0, hidden)
            before = jnp.where(row_at == 0, 0.0, pltpu.roll(hidden, 1, 0))
            after = jnp.where(row_at == columns - 1, 0.0, pltpu.roll(hidden, columns - 1, 0))
            taps[0, i, r] = before.astype(BF16)
            taps[1, i, r] = hidden.astype(BF16)
            taps[2, i, r] = after.astype(BF16)


class Weights:
    def __init__(self, wmain, wext, wleft):
        self.wmain, self.wext, self.wleft = wmain, wext, wleft

    def gather_left(self):
        wmain, wext, wleft = self.wmain, self.wext, self.wleft
        count = wmain.shape[1] * wmain.shape[2] * 4
        low = ints((count // 2, 8, 128), 1) < 4

        def paired(tile):
            tile = tile.reshape(count // 2, 2, 8, 128)
            even, odd = tile[:, 0], tile[:, 1]
            first = jnp.where(low, even, pltpu.roll(odd, 4, 1))
            second = jnp.where(low, pltpu.roll(even, 4, 1), odd)
            return [v.reshape(count * 4, 128).astype(BF16) for v in (first, second)]

        def step(sid, carry):
            tile = wmain[sid, :, :, :, :, 64:80, :].reshape(count, 16, 128).astype(F32)
            for part in range(2):
                first, second = paired(tile[:, 8 * part:8 * part + 8])
                wleft[4 * sid + 2 * part] = first
                wleft[4 * sid + 2 * part + 1] = second
            return carry

        lax.fori_loop(0, wmain.shape[0], step, 0)
        tile = wext[:, :, 16:32, :].reshape(count, 16, 128).astype(F32)
        wleft[4 * wmain.shape[0]] = paired(tile[:, 0:8])[0]

    def block(self, index):
        wmain, wext = self.wmain, self.wext
        if index < 4 * wmain.shape[0]:
            j = index % 4
            head = wmain[index // 4, :, :, :, :, 16 * j:16 * j + 16, :]
        else:
            head = wext[:, :, 0:16, :]
        return jnp.concatenate([head.reshape(-1, 128), self.wleft[index]], axis=0)

    def columns(self, matrix, start, stop):
        parts = [self.block(5 * matrix + n) for n in range(start, stop)]
        return parts[0] if len(parts) == 1 else jnp.concatenate(parts, axis=1)


def order_plan(planb, order):
    images, bands, plan_rows, channels = planb.shape
    for i in range(images):
        rows = planb[i].reshape(bands * plan_rows, channels)
        rows = jnp.dot(rows, order[...], preferred_element_type=F32).astype(BF16)
        planb[i] = rows.reshape(bands, plan_rows, channels)


def plan_side(cot, planb, weights, order, keys, vals, gatt):
    images, bands, plan_rows, channels = planb.shape
    for start, stop in SPANS:
        lanes = slice(128 * start, 128 * stop)
        weight_k = weights.columns(10, start, stop)
        weight_v = weights.columns(11, start, stop)
        for i in range(images):
            rows = planb[i].reshape(bands * plan_rows, channels)
            keys[i, :, lanes] = jnp.dot(rows, weight_k, preferred_element_type=F32).astype(BF16)
            vals[i, :, lanes] = jnp.dot(rows, weight_v, preferred_element_type=F32).astype(BF16)
    total = None
    flat = cot[...].reshape(-1, channels)
    for start, stop in SPANS:
        part = lax.dot_general(
            flat[:, 128 * start:128 * stop], weights.columns(12, start, stop), NT,
            preferred_element_type=F32,
        )
        total = part if total is None else total + part
    total = lax.dot_general(total.astype(BF16), order[...], NT, preferred_element_type=F32)
    gatt[...] = total.astype(BF16)


def convolve(lat, weights, taps, mixed):
    images, band_rows, columns, channels = lat.shape
    tokens = images * band_rows * columns
    flat = lat[...].reshape(tokens, channels)
    for start, stop in SPANS:
        lanes = slice(128 * start, 128 * stop)
        total = None
        for t in range(9):
            window = taps[t % 3, :, t // 3:t // 3 + band_rows].reshape(tokens, channels)
            part = jnp.dot(window, weights.columns(t, start, stop), preferred_element_type=F32)
            total = part if total is None else total + part
        mixed[:, lanes] = (flat[:, lanes].astype(F32) + total).astype(BF16)


def attend(mixed, weights, order, keys, vals, gatt, attended, dquery, block_out):
    images, band_rows, columns, channels = block_out.shape
    scale = 1.0 / math.sqrt(HEAD)
    cells = band_rows * columns
    left = ints((cells, 128), 1) < HEAD
    zero = jnp.zeros((cells, 128), BF16)

    def two_heads(value):
        return jnp.concatenate([jnp.where(left, value, zero), jnp.where(left, zero, value)], 0)

    def one_row(value):
        return jnp.where(left, value[:cells], value[cells:]).astype(BF16)

    flat = mixed[...]
    ordered = jnp.dot(flat, order[...], preferred_element_type=F32).astype(BF16)
    for start, stop in SPANS:
        queries = jnp.dot(
            ordered, weights.columns(9, start, stop), preferred_element_type=F32
        ).astype(BF16)
        for n in range(start, stop):
            lanes = slice(128 * n, 128 * n + 128)
            here = slice(128 * (n - start), 128 * (n - start) + 128)
            for i in range(images):
                rows = slice(cells * i, cells * i + cells)
                key, val = keys[i, :, lanes], vals[i, :, lanes]
                query = two_heads(queries[rows, here])
                grad = two_heads(gatt[rows, lanes])
                scores = lax.dot_general(query, key, NT, preferred_element_type=F32) * scale
                expo = jnp.exp(scores - jnp.max(scores, axis=-1, keepdims=True))
                probs = expo / jnp.sum(expo, axis=-1, keepdims=True)
                dprob = lax.dot_general(grad, val, NT, preferred_element_type=F32)
                inner = jnp.sum(probs * dprob, axis=-1, keepdims=True)
                dscore = (probs * (dprob - inner) * scale).astype(BF16)
                attended[rows, lanes] = one_row(
                    jnp.dot(probs.astype(BF16), val, preferred_element_type=F32)
                )
                dquery[rows, lanes] = one_row(jnp.dot(dscore, key, preferred_element_type=F32))
    ordered = jnp.dot(attended[...], order[...], preferred_element_type=F32).astype(BF16)
    for start, stop in SPANS:
        lanes = slice(128 * start, 128 * stop)
        result = flat[:, lanes].astype(F32) + jnp.dot(
            ordered, weights.columns(12, start, stop), preferred_element_type=F32
        )
        block_out[:, :, :, lanes] = result.astype(BF16).reshape(
            images, band_rows, columns, 128 * (stop - start)
        )


def reduce_gradient(
    me, factor, ops, perm, out,
    rcv, gf, gb, r1, h, r2, total, zs, zr, fin,
    op_sems, s1_send, s1_recv, s2_send, s2_recv, z_send, z_recv, o_send, o_recv,
):
    nz, x, y, z, c = me.nz, me.x, me.y, me.z, me.c
    zh = nz // 2
    small = zh * 5
    big = 4 * small
    twin = me.at(c=1 - c)
    mates = [(me.dp, wrap(me.s + k, BANDS)) for k in range(1, BANDS)]
    spans = [pl.ds(128 * a, 128 * (b - a)) for a, b in SPANS]
    send(ops.at[1 - c, c], rcv.at[c], op_sems.at[2], op_sems.at[3], twin)
    own = ops[c]
    lhs_own = jnp.dot(own[0], perm[...], preferred_element_type=F32).astype(BF16)
    await_bytes(rcv.at[0], op_sems.at[1])
    await_bytes(rcv.at[0], op_sems.at[3])
    lhs_far = jnp.dot(rcv[0], perm[...], preferred_element_type=F32).astype(BF16)
    lhs = jnp.concatenate([lhs_own, lhs_far], axis=0)
    first = c == 0
    a1 = jnp.where(first, y, x)
    a2 = jnp.where(first, x, y)
    active = lax.rem(z, 2) == me.xl
    for p, (start, stop) in enumerate(SPANS):
        lanes = slice(128 * start, 128 * stop)
        rhs = jnp.concatenate([own[1][:, lanes], rcv[1, :, lanes]], axis=0)
        grads = lax.dot_general(
            lhs, rhs, (((0,), (0,)), ((), ())), preferred_element_type=F32
        ) * factor
        gf[:, lanes] = grads
        gb[:, lanes] = grads.astype(BF16)
        for k in (2, 1, 3):
            to = wrap(a1 + k, 4)
            device = me.at(x=jnp.where(first, x, to), y=jnp.where(first, to, y))
            send(
                gb.at[pl.ds(pl.multiple_of(to * big, 32), big), spans[p]],
                r1.at[k - 1, :, spans[p]], s1_send.at[p], s1_recv.at[p], device,
            )

    def part_two(p):
        span = spans[p]
        await_bytes(r1.at[:, :, span], s1_recv.at[p])
        acc = gf[pl.ds(pl.multiple_of(a1 * big, 32), big), span]
        for k in range(3):
            acc = acc + r1[k, :, span].astype(F32)
        h[:, span] = acc
        for k in (2, 1, 3):
            to = wrap(a2 + k, 4)
            device = me.at(x=jnp.where(first, to, x), y=jnp.where(first, y, to))
            send(
                h.at[pl.ds(pl.multiple_of(to * small, 8), small), span],
                r2.at[k - 1, :, span], s2_send.at[p], s2_recv.at[p], device,
            )

    def part_three(p):
        span = spans[p]
        await_bytes(r2.at[:, :, span], s2_recv.at[p])
        acc = h[pl.ds(pl.multiple_of(a2 * small, 8), small), span]
        for k in range(3):
            acc = acc + r2[k, :, span]
        total[:, span] = acc
        for i in range(zh):
            zs[i, 0:5, span] = total[5 * i:5 * i + 5, span]
        for i in range(zh):
            to = 2 * i + me.xl

            @pl.when(to != z)
            def _():
                send(
                    zs.at[i, :, span], zr.at[z, :, span],
                    z_send.at[p], z_recv.at[p], me.at(z=to),
                )

    zs[...] = jnp.zeros_like(zs)
    part_two(0)
    part_two(1)
    part_three(0)
    part_two(2)
    part_three(1)
    part_three(2)

    @pl.when(active)
    def _():
        for p, span in enumerate(spans):
            zr[z, :, span] = zs[lax.div(z, 2), :, span]
            await_bytes(zr.at[pl.ds(0, nz - 1), :, span], z_recv.at[p])
            piece = zr[0, :, span]
            for i in range(1, nz):
                piece = piece + zr[i, :, span]
            fin[:, span] = piece
            for mate in mates:
                send(
                    fin.at[:, span], out.at[c * NY + y, :, span], o_send.at[p], o_recv.at[p], mate
                )
            out[c * NY + y, :, span] = piece
        for p, span in enumerate(spans):
            await_bytes(out.at[pl.ds(0, CORE - 1), :, span], o_recv.at[p])
            await_bytes(zr.at[pl.ds(0, BANDS - 1), :, span], o_send.at[p])
            await_bytes(zs.at[pl.ds(0, zh - 1), :, span], z_send.at[p])

    @pl.when(jnp.logical_not(active))
    def _():
        for p, span in enumerate(spans):
            await_bytes(out.at[:, :, span], o_recv.at[p])
            await_bytes(zs.at[:, :, span], z_send.at[p])

    await_bytes(rcv.at[0], op_sems.at[0])
    await_bytes(rcv.at[0], op_sems.at[2])
    for p, span in enumerate(spans):
        await_bytes(r1.at[:, :, span], s1_send.at[p])
        await_bytes(r2.at[:, :, span], s2_send.at[p])


def block_kernel(
    nz, factor,
    lat, plan, conv, attn, gain, cot,
    block_out, grad_out,
    wmain, wext, wleft, wslice, extra, spare, sums, planb, halo, sbuf, order, perm,
    taps, keys, vals, gatt, ops,
    rcv, gf, gb, r1, h, r2, total, zs, zr, fin, pieces,
    z_send, z_recv, x_sems, a_send, b_send, c_send, d_send, f_send,
    a_recv, b_recv, c_recv, d_recv, f_recv, misc_send, misc_recv,
    op_sems, s1_send, s1_recv, s2_send, s2_recv, g_send, g_recv, o_send, o_recv, near,
):
    me = Spot(nz)
    x, y, z, c, s = me.x, me.y, me.z, me.c, me.s
    channels = lat.shape[-1]
    rounds = nz // 4
    twin = me.at(c=1 - c)
    north, south = me.at(y=y + 1), me.at(y=y - 1)
    east, west = me.at(x=x + 1), me.at(x=x - 1)
    side = jnp.where(me.xl == 0, -1, 1)
    other_x = me.at(x=x + side)
    mates = [(me.dp, wrap(s + k, BANDS)) for k in range(1, BANDS)]
    greeted = mates + [me.at(z=z + k) for k in (1, -1, 2, -2)] + [other_x, me.at(x=x + 2)]
    barrier = pltpu.get_barrier_semaphore()
    for device in greeted:
        pl.semaphore_signal(barrier, inc=1, device_id=device, device_id_type=MESH)
    my_sid = me.sid(x, y)
    own_slice(me, conv, attn, wslice, extra, spare)
    band_sums(lat, group_table(channels), sums)
    pl.semaphore_wait(barrier, len(greeted))

    steps = reach(nz)

    def spread(low, high):
        for slot, step in enumerate(steps):
            if low < abs(step) <= high:
                back = steps.index(-step) if -step in steps else slot
                send(
                    wslice, wmain.at[my_sid, me.xh, back // 4, back % 4 // 2, back % 2],
                    z_send, z_recv.at[back // 4], me.at(z=z + step),
                )

    def widen(k):
        for step in (k, -k):
            pl.semaphore_signal(
                near.at[k // 4], inc=1, device_id=me.at(z=z + step), device_id_type=MESH
            )

    spread(0, 2)
    widen(2)
    for mate in mates:
        send(sums, sbuf.at[s], misc_send.at[0], misc_recv.at[0], mate)
    send(lat.at[:, 0], halo.at[1], misc_send.at[1], misc_recv.at[1], (me.dp, wrap(s - 1, BANDS)))
    send(lat.at[:, 1], halo.at[0], misc_send.at[2], misc_recv.at[2], (me.dp, wrap(s + 1, BANDS)))
    pair = (me.dp, ((1 - me.xl) * NY + y) * 2 + c)
    send(plan, planb.at[:, my_sid], misc_send.at[3], misc_recv.at[3], pair)
    for k in (1, 3, 2):
        send(plan, planb.at[:, my_sid], misc_send.at[4], misc_recv.at[4], me.at(y=y + k))
    pl.semaphore_wait(near.at[0], 2)
    spread(2, 4)
    widen(4)
    order[...] = arrival_order(me, channels)
    pl.semaphore_wait(near.at[1], 2)
    spread(4, nz)

    @pl.when(c == 0)
    def _():
        for slot, step in enumerate(steps):
            if slot:
                back = steps.index(-step) if -step in steps else slot
                send(extra, wext.at[me.xh, back], x_sems.at[0], x_sems.at[1], me.at(z=z + step))

    wmain[my_sid, me.xh, 0, 0, 0] = wslice[...]
    wext[me.xh, 0] = extra[...]
    planb[:, my_sid] = plan[...]
    sbuf[s] = sums[...]
    ops[1, 1] = cot[...].reshape(ops.shape[2:])
    every = slice(None)

    def block(r, xx, yy, colours, dirs):
        return wmain.at[me.sid(xx, yy), lax.div(wrap(xx, NX), 2), r, colours, dirs]

    def move(r, xx, yy, colours, dirs, send_sem, recv_sem, device):
        ref = block(r, xx, yy, colours, dirs)
        send(ref, ref, send_sem, recv_sem, device)

    def hand_over(r, cells):
        for i, j in cells:
            move(r, x + i, y + j, every, every, f_send, f_recv, twin)

    def units(n):
        return wmain.at[pl.ds(0, n), 0, 0]

    def part_a(r):
        await_bytes(zwait(r), z_recv.at[r])
        for device in (east, west, north, south):
            move(r, x, y, every, every, a_send, a_recv.at[r], device)
        hand_over(r, [(0, 0)])

    def zwait(r):
        return wmain.at[pl.ds(0, 3), 0, 0, 0, 0] if r == 0 else wmain.at[pl.ds(0, 4), 0, 0, 0, 0]

    def part_b(r):
        await_bytes(units(4), a_recv.at[r])
        low, high = pl.ds(0, 1), pl.ds(1, 1)
        move(r, x - 1, y, every, low, b_send, b_recv.at[r], east)
        move(r, x + 1, y, every, high, b_send, b_recv.at[r], west)
        move(r, x, y - 1, every, low, b_send, b_recv.at[r], north)
        move(r, x, y + 1, every, high, b_send, b_recv.at[r], south)
        for k in (1, -1):
            for device in (north, south):
                move(r, x + k, y, low, every, c_send, c_recv.at[r], device)
            for device in (east, west):
                move(r, x, y + k, high, every, c_send, c_recv.at[r], device)
        hand_over(r, [(1, 0), (-1, 0), (0, 1), (0, -1)])

    def part_c(r):
        await_bytes(units(2), b_recv.at[r])
        low, high = pl.ds(0, 1), pl.ds(1, 1)
        for device in (north, south):
            move(r, x + 2, y, low, every, c_send, c_recv.at[r], device)
        for device in (east, west):
            move(r, x, y + 2, high, every, c_send, c_recv.at[r], device)
        hand_over(r, [(2, 0), (0, 2)])

    def part_d(r):
        await_bytes(units(6), c_recv.at[r])
        low, high = pl.ds(0, 1), pl.ds(1, 1)
        for k in (1, -1, 2):
            move(r, x + k, y - 1, low, low, d_send, d_recv.at[r], north)
            move(r, x + k, y + 1, low, high, d_send, d_recv.at[r], south)
            move(r, x - 1, y + k, high, low, d_send, d_recv.at[r], east)
            move(r, x + 1, y + k, high, high, d_send, d_recv.at[r], west)
        hand_over(r, [(1, 1), (1, -1), (-1, 1), (-1, -1)])

    def part_e(r):
        await_bytes(units(3), d_recv.at[r])
        hand_over(r, [(1, 2), (-1, 2), (2, 1), (2, -1), (2, 2)])

    def normalise():
        await_bytes(sbuf.at[pl.ds(0, BANDS - 1)], misc_recv.at[0])
        await_bytes(halo.at[0], misc_recv.at[1])
        await_bytes(halo.at[0], misc_recv.at[2])
        norm_taps(me, lat, gain, halo, sbuf, order, taps)

    def plan_two():
        await_bytes(planb.at[:, 0], misc_recv.at[3])
        theirs = planb.at[:, c * CORE + (1 - me.xl) * NY + y]
        for k in (1, 3, 2):
            send(theirs, theirs, misc_send.at[5], misc_recv.at[5], me.at(y=y + k))

    def plan_three():
        await_bytes(planb.at[:, pl.ds(0, 3)], misc_recv.at[4])
        await_bytes(planb.at[:, pl.ds(0, 3)], misc_recv.at[5])
        mine = planb.at[:, pl.ds(c * CORE, CORE)]
        send(mine, mine, misc_send.at[6], misc_recv.at[6], twin)

    def plan_four():
        await_bytes(planb.at[:, pl.ds(0, CORE)], misc_recv.at[6])
        await_bytes(planb.at[:, pl.ds(0, CORE)], misc_send.at[6])
        await_bytes(planb.at[:, 0], misc_send.at[3])
        await_bytes(planb.at[:, pl.ds(0, 3)], misc_send.at[4])
        await_bytes(planb.at[:, pl.ds(0, 3)], misc_send.at[5])
        order_plan(planb, order)
        perm[...] = scatter_order(me, channels)

    part_a(0)
    part_b(0)
    plan_two()
    part_a(1)
    normalise()
    part_c(0)
    part_b(1)
    part_d(0)
    part_a(2)
    part_c(1)
    part_a(3)
    plan_three()
    part_e(0)
    part_b(2)
    part_d(1)
    part_b(3)
    part_c(2)
    part_e(1)
    plan_four()
    part_c(3)
    part_d(2)

    @pl.when(c == 0)
    def _():
        await_bytes(wext.at[0, pl.ds(0, nz - 1)], x_sems.at[1])
        half = wext.at[me.xh]
        send(half, half, x_sems.at[2], x_sems.at[3], other_x)

    part_d(3)
    part_e(2)
    part_e(3)

    @pl.when(c == 0)
    def _():
        await_bytes(wext.at[0], x_sems.at[3])
        send(wext, wext, x_sems.at[4], x_sems.at[5], twin)

    await_bytes(wmain.at[pl.ds(0, CORE)], f_recv)

    @pl.when(c == 0)
    def _():
        await_bytes(wext.at[0, pl.ds(0, nz - 1)], x_sems.at[0])
        await_bytes(wext.at[0], x_sems.at[2])
        await_bytes(wext, x_sems.at[4])

    @pl.when(c != 0)
    def _():
        await_bytes(wext, x_sems.at[5])

    weights = Weights(wmain, wext, wleft)
    weights.gather_left()
    plan_side(cot, planb, weights, order, keys, vals, gatt)
    convolve(lat, weights, taps, ops.at[0, 0])
    send(ops.at[1 - c, 1 - c], rcv.at[1 - c], op_sems.at[0], op_sems.at[1], twin)
    attend(
        ops.at[0, 0], weights, order, keys, vals, gatt, ops.at[1, 0], ops.at[0, 1], block_out
    )
    reduce_gradient(
        me, factor, ops, perm, pieces,
        rcv, gf, gb, r1, h, r2, total, zs, zr, fin,
        op_sems, s1_send, s1_recv, s2_send, s2_recv, g_send, g_recv, o_send, o_recv,
    )

    for g in range(2):
        for k in range(NY):
            grad_out[5 * k:5 * k + 5, g, :] = pieces[g * NY + k, 0:5, :]

    await_bytes(sbuf.at[pl.ds(0, BANDS - 1)], misc_send.at[0])
    await_bytes(halo.at[0], misc_send.at[1])
    await_bytes(halo.at[0], misc_send.at[2])
    await_bytes(wmain.at[pl.ds(0, nz - 1), 0, 0, 0, 0], z_send)
    await_bytes(wmain.at[pl.ds(0, 4), 0], a_send)
    await_bytes(wmain.at[pl.ds(0, 2), 0], b_send)
    await_bytes(wmain.at[pl.ds(0, 6), 0], c_send)
    await_bytes(wmain.at[pl.ds(0, 3), 0], d_send)
    await_bytes(wmain.at[pl.ds(0, CORE)], f_send)


def body(latents, plan, conv_weight, gn_gain, attn_weights, cotangent):
    images, band_rows, columns, channels = latents.shape
    nz = lax.axis_size("dp") // 2
    tokens = images * band_rows * columns
    plan_tokens = BANDS * plan.shape[1]
    factor = 1.0 / math.sqrt(tokens * 2 * nz * BANDS)
    zh = nz // 2
    small, big = 5 * zh, 20 * zh
    rounds = nz // 4
    dma = pltpu.SemaphoreType.DMA
    vmem = pltpu.VMEM
    return tuple(pl.pallas_call(
        functools.partial(block_kernel, nz, factor),
        out_shape=[
            jax.ShapeDtypeStruct(latents.shape, BF16),
            jax.ShapeDtypeStruct((SHARD, 2, channels), F32),
        ],
        in_specs=[pl.BlockSpec(memory_space=vmem)] * 6,
        out_specs=[pl.BlockSpec(memory_space=vmem)] * 2,
        scratch_shapes=[
            vmem((BANDS, 2, rounds, 2, 2, UNIT, 128), BF16),
            vmem((2, nz, 32, 128), BF16),
            vmem((65, 2 * nz * 4, 128), BF16),
            vmem((UNIT, 128), BF16),
            vmem((32, 128), BF16),
            vmem((16, 128), F32),
            vmem((8, 128), F32),
            vmem((images, BANDS) + plan.shape[1:], BF16),
            vmem((2, images, columns, channels), BF16),
            vmem((BANDS, 8, 128), F32),
            vmem((channels, channels), BF16),
            vmem((channels, channels), BF16),
            vmem((3, images, band_rows + 2, columns, channels), BF16),
            vmem((images, plan_tokens, channels), BF16),
            vmem((images, plan_tokens, channels), BF16),
            vmem((tokens, channels), BF16),
            vmem((2, 2, tokens, channels), BF16),
            vmem((2, tokens, channels), BF16),
            vmem((4 * big, channels), F32),
            vmem((4 * big, channels), BF16),
            vmem((3, big, channels), BF16),
            vmem((big, channels), F32),
            vmem((3, small, channels), F32),
            vmem((small, channels), F32),
            vmem((zh, 8, channels), F32),
            vmem((max(nz, BANDS), 8, channels), F32),
            vmem((8, channels), F32),
            vmem((CORE, 8, channels), F32),
            dma, dma((rounds,)), dma((6,)), dma, dma, dma, dma, dma,
            dma((rounds,)), dma((rounds,)), dma((rounds,)), dma((rounds,)), dma, dma((7,)), dma((7,)),
            dma((4,)), dma((3,)), dma((3,)), dma((3,)), dma((3,)), dma((3,)), dma((3,)),
            dma((3,)), dma((3,)), pltpu.SemaphoreType.REGULAR((2,)),
        ],
        compiler_params=pltpu.CompilerParams(
            collective_id=0, has_side_effects=True, vmem_limit_bytes=VMEM_LIMIT
        ),
        name="block",
    )(latents, plan, conv_weight, attn_weights, gn_gain, cotangent))


def solution(mesh):
    return jax.shard_map(
        body,
        mesh=mesh,
        in_specs=(
            P("dp", "spatial", None, None),
            P("dp", "spatial", None),
            P(None, "dp", None),
            P(),
            P(None, "dp", None),
            P("dp", "spatial", None, None),
        ),
        out_specs=(P("dp", "spatial", None, None), P("dp", None, None)),
        check_vma=False,
    )
```

```python
import functools
import math

import jax
import jax.numpy as jnp
from jax import lax
from jax.experimental import pallas as pl
from jax.experimental.pallas import tpu as pltpu
from jax.sharding import PartitionSpec as P

GROUPS = 32
HEAD = 64
NX = 4
NY = 4
BANDS = 16
CORE = 2 * NY
SHARD = 20
UNIT = 4 * SHARD
MESH = pl.DeviceIdType.MESH
VMEM_LIMIT = 62 * 1024 * 1024
SPANS = ((0, 2), (2, 4), (4, 5))
GRAD_SPANS = ((0, 3), (3, 5))
ORDER = (
    ("a", 0), ("a", 1), ("b", 0), ("plan", 2), ("norm", 0), ("c", 0), ("b", 1), ("d", 0), ("a", 2),
    ("c", 1), ("a", 3), ("plan", 3), ("e", 0), ("b", 2), ("d", 1), ("b", 3), ("c", 2), ("e", 1),
    ("left", 0), ("plan", 4), ("c", 3), ("d", 2), ("ext", 0), ("left", 1), ("d", 3), ("e", 2), ("e", 3),
)
BF16 = jnp.bfloat16
F32 = jnp.float32
NT = (((1,), (1,)), ((), ()))

eps_norm = 1e-05


def wrap(value, n):
    return lax.rem(value + n, n)


class Spot:
    def __init__(self, nz):
        self.nz = nz
        self.dp = lax.axis_index("dp")
        self.s = lax.axis_index("spatial")
        self.xh = lax.div(self.dp, nz)
        self.z = lax.rem(self.dp, nz)
        self.xl = lax.div(self.s, CORE)
        self.y = lax.rem(lax.div(self.s, 2), NY)
        self.c = lax.rem(self.s, 2)
        self.x = 2 * self.xh + self.xl

    def at(self, x=None, y=None, z=None, c=None):
        x = self.x if x is None else wrap(x, NX)
        y = self.y if y is None else wrap(y, NY)
        z = self.z if z is None else wrap(z, self.nz)
        c = self.c if c is None else c
        return (lax.div(x, 2) * self.nz + z, (lax.rem(x, 2) * NY + y) * 2 + c)

    def place(self, x, y):
        at = lax.rem(wrap(x, NX), 2) * NY + wrap(y, NY)
        return at + jnp.where(at >= 6, 2 * self.c, 0)

    def sid(self, x, y):
        return self.c * CORE + lax.rem(wrap(x, NX), 2) * NY + wrap(y, NY)


def send(src, dst, send_sem, recv_sem, device):
    pltpu.make_async_remote_copy(
        src_ref=src,
        dst_ref=dst,
        send_sem=send_sem,
        recv_sem=recv_sem,
        device_id=device,
        device_id_type=MESH,
    ).start()


def await_bytes(ref, sem):
    pltpu.make_async_copy(ref, ref, sem).wait()


def reach(nz):
    steps = [0]
    for k in range(1, nz // 2):
        steps += [k, -k]
    return steps + [nz // 2]


def ints(shape, axis):
    return lax.broadcasted_iota(jnp.int32, shape, axis)


def floor_of(values, width):
    return jnp.floor((values + 0.5) * (1.0 / width))


def one_hot(names, rows):
    at = ints((rows, names.shape[1]), 0).astype(F32)
    return jnp.where(at == names, 1.0, 0.0).astype(BF16)


def arrival_order(me, channels):
    nz = me.nz
    bits = nz.bit_length() - 1
    place = ints((1, channels), 1)
    head = 2 * nz * 16
    late = place - head
    main = place < head
    slot = jnp.where(main, place >> 4, late >> 2)
    row = jnp.where(main, place & 15, 16 + (late & 3))
    half, slot = slot >> bits, slot & (nz - 1)
    step = jnp.where((slot & 1) == 1, (slot + 1) >> 1, -(slot >> 1))
    names = (half * nz + ((me.z + step + nz) & (nz - 1))) * SHARD + row
    return one_hot(names.astype(F32), channels)


def scatter_order(me, channels):
    zh = me.nz // 2
    small = 5 * zh
    place = ints((1, channels), 1).astype(F32)
    outer = floor_of(place, 4 * small)
    place = place - outer * (4 * small)
    inner = floor_of(place, small)
    place = place - inner * small
    zi = floor_of(place, 5)
    i = place - 5 * zi
    first = me.c == 0
    xx = jnp.where(first, inner, outer)
    yy = jnp.where(first, outer, inner)
    half = floor_of(xx, 2)
    names = (half * me.nz + 2 * zi + xx - 2 * half) * SHARD + yy * 5 + i
    return one_hot(names, channels)


def group_table(channels):
    rows = ints((channels, 128), 0).astype(F32)
    lanes = ints((channels, 128), 1).astype(F32)
    return jnp.where(floor_of(rows, channels // GROUPS) == lanes, 1.0, 0.0)


def own_slice(me, conv, attn, wslice, extra, spare):
    taps, _, channels = conv.shape
    first = 4 * (me.xl * NY + me.y)
    for j in range(4):
        block = first + j
        shared = block - 24 + 8 * me.c
        alone = block < 24
        matrix = jnp.where(alone, lax.div(block, 2), jnp.minimum(shared, 12))
        at = jnp.where(shared < 12, 2, shared - 12)
        at = jnp.where(alone, lax.rem(block, 2) + 3 * me.c, at)
        lanes = pl.ds(pl.multiple_of(at * 128, 128), 128)
        one = conv[jnp.minimum(matrix, taps - 1), :, lanes].astype(F32)
        two = attn[jnp.maximum(matrix - taps, 0), :, lanes].astype(F32)
        rows = jnp.where(matrix < taps, one, two)
        wslice[16 * j:16 * j + 16, :] = rows[0:16].astype(BF16)
        spare[4 * j:4 * j + 4, :] = rows[16:20]
    wslice[64:80, :] = spare[...].astype(BF16)
    extra[0:20, :] = attn[attn.shape[0] - 1, :, channels - 128:channels]
    extra[20:32, :] = jnp.zeros((12, 128), BF16)


def band_sums(lat, table, sums):
    images, band_rows, columns, channels = lat.shape
    rows = []
    for power in (1, 2):
        for i in range(images):
            cells = lat[i].reshape(band_rows * columns, channels).astype(F32)
            rows.append(jnp.sum(cells * cells if power == 2 else cells, axis=0, keepdims=True))
    rows.append(jnp.zeros((8 - 2 * images, channels), F32))
    sums[...] = jnp.dot(
        jnp.concatenate(rows, axis=0), table,
        preferred_element_type=F32, precision=lax.Precision.HIGHEST,
    )


def norm_taps(me, band_rows, latu, gain, halo, sbuf, order, taps):
    images, rows, columns, channels = latu.shape
    tot = sbuf[0]
    for i in range(1, BANDS):
        tot = tot + sbuf[i]
    grouped = lax.dot_general(
        tot, group_table(channels), NT, preferred_element_type=F32, precision=lax.Precision.HIGHEST
    )
    counted = float(band_rows * BANDS * columns * (channels // GROUPS))
    row_at = ints((columns, channels), 0)
    for i in range(images):
        mean = grouped[i:i + 1] / counted
        variance = grouped[images + i:images + i + 1] / counted - mean * mean
        inverse = lax.rsqrt(variance + eps_norm)
        for r in range(rows + 2):
            if r == 0:
                cells = halo[0, i]
            elif r == rows + 1:
                cells = halo[1, i]
            else:
                cells = latu[i, r - 1]
            normed = (cells.astype(F32) - mean) * inverse * gain[...]
            hidden = (normed / (1.0 + jnp.exp(-normed))).astype(BF16)
            hidden = jnp.dot(hidden, order[...], preferred_element_type=F32)
            if r == 0:
                hidden = jnp.where(me.s < 2, 0.0, hidden)
            if r == rows + 1:
                hidden = jnp.where(me.s >= BANDS - 2, 0.0, hidden)
            before = jnp.where(row_at == 0, 0.0, pltpu.roll(hidden, 1, 0))
            after = jnp.where(row_at == columns - 1, 0.0, pltpu.roll(hidden, columns - 1, 0))
            taps[0, i, r] = before.astype(BF16)
            taps[1, i, r] = hidden.astype(BF16)
            taps[2, i, r] = after.astype(BF16)


class Weights:
    def __init__(self, wmain, wext, wleft):
        self.wmain, self.wext, self.wleft = wmain, wext, wleft

    def gather_left(self, r):
        wmain, wleft = self.wmain, self.wleft
        half = wleft.shape[1] // 2

        def step(sid, carry):
            tile = wmain[sid, :, r, :, :, 64:80, :].reshape(8, 16, 128).astype(F32)
            for part in range(2):
                for which, rows in enumerate(self.paired(tile[:, 8 * part:8 * part + 8])):
                    rows = rows.reshape(2, 16, 128)
                    wleft[4 * sid + 2 * part + which, 16 * r:16 * r + 16, :] = rows[0]
                    wleft[4 * sid + 2 * part + which, half + 16 * r:half + 16 * r + 16, :] = rows[1]
            return carry

        lax.fori_loop(0, wmain.shape[0], step, 0)

    def gather_ext(self):
        wext = self.wext
        count = wext.shape[0] * wext.shape[1]
        tile = wext[:, :, 16:32, :].reshape(count, 16, 128).astype(F32)
        self.wleft[self.wleft.shape[0] - 1] = self.paired(tile[:, 0:8])[0]

    def paired(self, tile):
        count = tile.shape[0]
        low = ints((count // 2, 8, 128), 1) < 4
        tile = tile.reshape(count // 2, 2, 8, 128)
        even, odd = tile[:, 0], tile[:, 1]
        first = jnp.where(low, even, pltpu.roll(odd, 4, 1))
        second = jnp.where(low, pltpu.roll(even, 4, 1), odd)
        return [v.reshape(count * 4, 128).astype(BF16) for v in (first, second)]

    def block(self, index):
        wmain, wext = self.wmain, self.wext
        if index < 4 * wmain.shape[0]:
            j = index % 4
            head = wmain[index // 4, :, :, :, :, 16 * j:16 * j + 16, :]
        else:
            head = wext[:, :, 0:16, :]
        return jnp.concatenate([head.reshape(-1, 128), self.wleft[index]], axis=0)

    def alone(self, matrix):
        return jnp.concatenate([self.block(2 * matrix), self.block(2 * matrix + 1)], axis=1)

    def shared(self, start, stop):
        parts = [self.block(24 + n) for n in range(start, stop)]
        return parts[0] if len(parts) == 1 else jnp.concatenate(parts, axis=1)

    def out(self, start, stop):
        return self.shared(12 + start, 12 + stop)


def own_lanes(c):
    return pl.ds(pl.multiple_of(384 * c, 128), 256)


MIDDLE = slice(256, 384)


def order_plan(planb, order):
    images, bands, plan_rows, channels = planb.shape
    for i in range(images):
        rows = planb[i].reshape(bands * plan_rows, channels)
        rows = jnp.dot(rows, order[...], preferred_element_type=F32).astype(BF16)
        planb[i] = rows.reshape(bands, plan_rows, channels)


def plan_side(c, cot, planb, weights, order, keys, vals, gatt):
    images, bands, plan_rows, channels = planb.shape
    for target, matrix in ((keys, 10), (vals, 11)):
        weight = weights.alone(matrix)
        for i in range(images):
            rows = planb[i].reshape(bands * plan_rows, channels)
            part = jnp.dot(rows, weight, preferred_element_type=F32).astype(BF16)
            target[i, :, own_lanes(c)] = part
        rows = planb[c].reshape(bands * plan_rows, channels)
        part = jnp.dot(rows, weights.shared(matrix, matrix + 1), preferred_element_type=F32)
        target[c, :, MIDDLE] = part.astype(BF16)
    total = None
    flat = cot[...]
    for start, stop in SPANS:
        part = lax.dot_general(
            flat[:, 128 * start:128 * stop], weights.out(start, stop), NT,
            preferred_element_type=F32,
        )
        total = part if total is None else total + part
    total = total.astype(BF16)
    for lanes, rows in ((own_lanes(c), own_lanes(c)), (MIDDLE, MIDDLE)):
        part = lax.dot_general(total, order[rows, :], NT, preferred_element_type=F32)
        gatt[:, lanes] = part.astype(BF16)


def convolve(c, band_rows, latu, weights, taps, mixed):
    images, rows, columns, channels = latu.shape
    tokens = images * rows * columns
    total = None
    for t in range(9):
        window = taps[t % 3, :, t // 3:t // 3 + rows].reshape(tokens, channels)
        part = jnp.dot(window, weights.alone(t), preferred_element_type=F32)
        total = part if total is None else total + part
    flat = latu[:, :, :, own_lanes(c)].reshape(tokens, 256)
    mixed[:, own_lanes(c)] = (flat.astype(F32) + total).astype(BF16)
    total = None
    first = band_rows * c
    for t in range(9):
        window = taps[t % 3, :, pl.ds(t // 3 + first, band_rows)]
        window = window.reshape(images * band_rows * columns, channels)
        part = jnp.dot(window, weights.shared(t, t + 1), preferred_element_type=F32)
        total = part if total is None else total + part
    flat = latu[:, pl.ds(first, band_rows), :, MIDDLE].reshape(-1, 128)
    middle = (flat.astype(F32) + total).astype(BF16)
    cells = band_rows * columns
    for i in range(images):
        mixed[own_cells(c, i, cells), MIDDLE] = middle[cells * i:cells * i + cells]


def own_cells(c, i, cells):
    return pl.ds(pl.multiple_of(2 * cells * i + cells * c, 16), cells)


def attend(c, mixed, weights, order, keys, vals, gatt, middle, attended, dquery):
    images = keys.shape[0]
    scale = 1.0 / math.sqrt(HEAD)
    cells = mixed.shape[0] // images
    left = ints((cells, 128), 1) < HEAD
    zero = jnp.zeros((cells, 128), BF16)

    def two_heads(value):
        return jnp.concatenate([jnp.where(left, value, zero), jnp.where(left, zero, value)], 0)

    def one_row(value):
        return jnp.where(left, value[:cells], value[cells:]).astype(BF16)

    def heads(query, i, rows, lanes):
        key, val = keys[i, :, lanes], vals[i, :, lanes]
        query, grad = two_heads(query), two_heads(gatt[rows, lanes])
        scores = lax.dot_general(query, key, NT, preferred_element_type=F32) * scale
        expo = jnp.exp(scores - jnp.max(scores, axis=-1, keepdims=True))
        probs = expo / jnp.sum(expo, axis=-1, keepdims=True)
        dprob = lax.dot_general(grad, val, NT, preferred_element_type=F32)
        inner = jnp.sum(probs * dprob, axis=-1, keepdims=True)
        dscore = (probs * (dprob - inner) * scale).astype(BF16)
        attended[rows, lanes] = one_row(
            jnp.dot(probs.astype(BF16), val, preferred_element_type=F32)
        )
        dquery[rows, lanes] = one_row(jnp.dot(dscore, key, preferred_element_type=F32))

    ordered = jnp.dot(mixed[...], order[...], preferred_element_type=F32).astype(BF16)
    queries = jnp.dot(ordered, weights.alone(9), preferred_element_type=F32).astype(BF16)
    middle[...] = jnp.dot(
        ordered, weights.shared(9, 10), preferred_element_type=F32
    ).astype(BF16)
    for n in range(2):
        lanes = pl.ds(pl.multiple_of(384 * c + 128 * n, 128), 128)
        for i in range(images):
            rows = slice(cells * i, cells * i + cells)
            heads(queries[rows, 128 * n:128 * n + 128], i, rows, lanes)
    rows = pl.ds(pl.multiple_of(cells * c, 128), cells)
    heads(middle[rows, :], c, rows, MIDDLE)


def project(c, mixed, weights, order, attended, block_out):
    images, band_rows, columns, channels = block_out.shape
    cells = band_rows * columns
    own = [attended[own_cells(c, i, cells), :] for i in range(images)]
    flat = [mixed[own_cells(c, i, cells), :] for i in range(images)]
    own, flat = jnp.concatenate(own, axis=0), jnp.concatenate(flat, axis=0)
    own = jnp.dot(own, order[...], preferred_element_type=F32).astype(BF16)
    for start, stop in SPANS:
        lanes = slice(128 * start, 128 * stop)
        result = flat[:, lanes].astype(F32) + jnp.dot(
            own, weights.out(start, stop), preferred_element_type=F32
        )
        block_out[:, :, :, lanes] = result.astype(BF16).reshape(
            images, band_rows, columns, 128 * (stop - start)
        )


def reduce_gradient(
    me, factor, ops, perm, out, meanwhile,
    gf, gb, r1, h, r2, total, zs, zr, fin,
    s1_send, s1_recv, s2_send, s2_recv, z_send, z_recv, o_send, o_recv,
):
    nz, x, y, z, c = me.nz, me.x, me.y, me.z, me.c
    zh = nz // 2
    small = zh * 5
    big = 4 * small
    mates = [(me.dp, wrap(me.s + k, BANDS)) for k in range(1, BANDS)]
    spans = [pl.ds(128 * a, 128 * (b - a)) for a, b in GRAD_SPANS]
    lhs = jnp.dot(ops[c, 0], perm[...], preferred_element_type=F32).astype(BF16)
    first = c == 0
    a1 = jnp.where(first, y, x)
    a2 = jnp.where(first, x, y)
    active = lax.rem(z, 2) == me.xl
    for p, (start, stop) in enumerate(GRAD_SPANS):
        lanes = slice(128 * start, 128 * stop)
        rhs = ops[c, 1, :, lanes]
        grads = lax.dot_general(
            lhs, rhs, (((0,), (0,)), ((), ())), preferred_element_type=F32
        ) * factor
        gf[:, lanes] = grads
        gb[:, lanes] = grads.astype(BF16)
        for k in (2, 1, 3):
            to = wrap(a1 + k, 4)
            device = me.at(x=jnp.where(first, x, to), y=jnp.where(first, to, y))
            send(
                gb.at[pl.ds(pl.multiple_of(to * big, 32), big), spans[p]],
                r1.at[k - 1, :, spans[p]], s1_send.at[p], s1_recv.at[p], device,
            )

    def part_two(p):
        span = spans[p]
        await_bytes(r1.at[:, :, span], s1_recv.at[p])
        acc = gf[pl.ds(pl.multiple_of(a1 * big, 32), big), span]
        for k in range(3):
            acc = acc + r1[k, :, span].astype(F32)
        h[:, span] = acc
        for k in (2, 1, 3):
            to = wrap(a2 + k, 4)
            device = me.at(x=jnp.where(first, to, x), y=jnp.where(first, y, to))
            send(
                h.at[pl.ds(pl.multiple_of(to * small, 8), small), span],
                r2.at[k - 1, :, span], s2_send.at[p], s2_recv.at[p], device,
            )

    def part_three(p):
        span = spans[p]
        await_bytes(r2.at[:, :, span], s2_recv.at[p])
        acc = h[pl.ds(pl.multiple_of(a2 * small, 8), small), span]
        for k in range(3):
            acc = acc + r2[k, :, span]
        total[:, span] = acc
        for i in range(zh):
            zs[i, 0:5, span] = total[5 * i:5 * i + 5, span]
        for i in range(zh):
            to = 2 * i + me.xl

            @pl.when(to != z)
            def _():
                send(
                    zs.at[i, :, span], zr.at[z, :, span],
                    z_send.at[p], z_recv.at[p], me.at(z=to),
                )

    zs[...] = jnp.zeros_like(zs)
    meanwhile()
    part_two(0)
    part_two(1)
    part_three(0)
    part_three(1)

    @pl.when(active)
    def _():
        for p, span in enumerate(spans):
            zr[z, :, span] = zs[lax.div(z, 2), :, span]
            await_bytes(zr.at[pl.ds(0, nz - 1), :, span], z_recv.at[p])
            piece = zr[0, :, span]
            for i in range(1, nz):
                piece = piece + zr[i, :, span]
            fin[:, span] = piece
            for mate in mates:
                send(
                    fin.at[:, span], out.at[c * NY + y, :, span], o_send.at[p], o_recv.at[p], mate
                )
            out[c * NY + y, :, span] = piece
        for p, span in enumerate(spans):
            await_bytes(out.at[pl.ds(0, CORE - 1), :, span], o_recv.at[p])
            await_bytes(zr.at[pl.ds(0, BANDS - 1), :, span], o_send.at[p])
            await_bytes(zs.at[pl.ds(0, zh - 1), :, span], z_send.at[p])

    @pl.when(jnp.logical_not(active))
    def _():
        for p, span in enumerate(spans):
            await_bytes(out.at[:, :, span], o_recv.at[p])
            await_bytes(zs.at[:, :, span], z_send.at[p])

    for p, span in enumerate(spans):
        await_bytes(r1.at[:, :, span], s1_send.at[p])
        await_bytes(r2.at[:, :, span], s2_send.at[p])


def block_kernel(
    nz, factor,
    lat, plan, conv, attn, gain, cot,
    block_out, grad_out,
    wmain, wext, wleft, wslice, extra, spare, sums, planb, halo, sbuf, order, perm,
    taps, keys, vals, gatt, ops, latu, middle,
    gf, gb, r1, h, r2, total, zs, zr, fin, pieces,
    z_send, z_recv, x_sems, a_send, b_send, c_send, d_send, f_send,
    a_recv, b_recv, c_recv, d_recv, f_recv, misc_send, misc_recv,
    op_sems, s1_send, s1_recv, s2_send, s2_recv, g_send, g_recv, o_send, o_recv, near,
):
    me = Spot(nz)
    x, y, z, c, s = me.x, me.y, me.z, me.c, me.s
    channels = lat.shape[-1]
    rounds = nz // 4
    twin = me.at(c=1 - c)
    north, south = me.at(y=y + 1), me.at(y=y - 1)
    east, west = me.at(x=x + 1), me.at(x=x - 1)
    side = jnp.where(me.xl == 0, -1, 1)
    other_x = me.at(x=x + side)
    mates = [(me.dp, wrap(s + k, BANDS)) for k in range(1, BANDS)]
    greeted = mates + [me.at(z=z + k) for k in (1, -1, 2, -2)] + [other_x, me.at(x=x + 2)]
    barrier = pltpu.get_barrier_semaphore()
    for device in greeted:
        pl.semaphore_signal(barrier, inc=1, device_id=device, device_id_type=MESH)
    my_sid, my_place = me.sid(x, y), me.place(x, y)
    images, band_rows, columns, _ = lat.shape
    cells = band_rows * columns
    own_slice(me, conv, attn, wslice, extra, spare)
    for i in range(images):
        ops[1, 1, own_cells(c, i, cells), :] = cot[i].reshape(cells, channels)
    pl.semaphore_wait(barrier, len(greeted))

    steps = reach(nz)

    def spread(low, high):
        for slot, step in enumerate(steps):
            if low < abs(step) <= high:
                back = steps.index(-step) if -step in steps else slot
                send(
                    wslice, wmain.at[my_place, me.xh, back // 4, back % 4 // 2, back % 2],
                    z_send, z_recv.at[back // 4], me.at(z=z + step),
                )

    def widen(k):
        for step in (k, -k):
            pl.semaphore_signal(
                near.at[k // 4], inc=1, device_id=me.at(z=z + step), device_id_type=MESH
            )

    spread(0, 2)
    widen(2)
    chip = wrap(lax.div(s, 2) + 2 * c - 1, BANDS // 2)
    for core in range(2):
        send(
            lat.at[:, c], halo.at[1 - c], misc_send.at[1], misc_recv.at[2 - c],
            (me.dp, 2 * chip + core),
        )
    send(lat, latu.at[:, pl.ds(band_rows * c, band_rows)], misc_send.at[2], misc_recv.at[7], twin)
    for i in range(images):
        ref = ops.at[1, 1, own_cells(c, i, cells)]
        send(ref, ref, op_sems.at[6], op_sems.at[7], twin)
    pair = (me.dp, ((1 - me.xl) * NY + y) * 2 + c)
    send(plan, planb.at[:, my_sid], misc_send.at[3], misc_recv.at[3], pair)
    for k in (1, 3, 2):
        send(plan, planb.at[:, my_sid], misc_send.at[4], misc_recv.at[4], me.at(y=y + k))
    band_sums(lat, group_table(channels), sums)
    pl.semaphore_wait(near.at[0], 2)
    spread(2, 4)
    widen(4)
    for mate in mates:
        send(sums, sbuf.at[s], misc_send.at[0], misc_recv.at[0], mate)
    order[...] = arrival_order(me, channels)
    pl.semaphore_wait(near.at[1], 2)
    spread(4, nz)

    @pl.when(c == 0)
    def _():
        for slot, step in enumerate(steps):
            if slot:
                back = steps.index(-step) if -step in steps else slot
                send(extra, wext.at[me.xh, back], x_sems.at[0], x_sems.at[1], me.at(z=z + step))

    wmain[my_place, me.xh, 0, 0, 0] = wslice[...]
    latu[:, pl.ds(band_rows * c, band_rows)] = lat[...]
    wext[me.xh, 0] = extra[...]
    planb[:, my_sid] = plan[...]
    sbuf[s] = sums[...]
    every = slice(None)

    def block(r, xx, yy, colours, dirs):
        return wmain.at[me.place(xx, yy), lax.div(wrap(xx, NX), 2), r, colours, dirs]

    def move(r, xx, yy, colours, dirs, send_sem, recv_sem, device):
        ref = block(r, xx, yy, colours, dirs)
        send(ref, ref, send_sem, recv_sem, device)

    def units(n):
        return wmain.at[pl.ds(0, n), 0, 0]

    def part_a(r):
        await_bytes(zwait(r), z_recv.at[r])
        for device in (east, west, north, south):
            move(r, x, y, every, every, a_send, a_recv.at[r], device)

    def zwait(r):
        return wmain.at[pl.ds(0, 3), 0, 0, 0, 0] if r == 0 else wmain.at[pl.ds(0, 4), 0, 0, 0, 0]

    def part_b(r):
        await_bytes(units(4), a_recv.at[r])
        low, high = pl.ds(0, 1), pl.ds(1, 1)
        move(r, x - 1, y, every, low, b_send, b_recv.at[r], east)
        move(r, x + 1, y, every, high, b_send, b_recv.at[r], west)
        move(r, x, y - 1, every, low, b_send, b_recv.at[r], north)
        move(r, x, y + 1, every, high, b_send, b_recv.at[r], south)
        for k in (1, -1):
            for device in (north, south):
                move(r, x + k, y, low, every, c_send, c_recv.at[r], device)
            for device in (east, west):
                move(r, x, y + k, high, every, c_send, c_recv.at[r], device)

    def part_c(r):
        await_bytes(units(2), b_recv.at[r])
        low, high = pl.ds(0, 1), pl.ds(1, 1)
        for device in (north, south):
            move(r, x + 2, y, low, every, c_send, c_recv.at[r], device)
        for device in (east, west):
            move(r, x, y + 2, high, every, c_send, c_recv.at[r], device)

    def part_d(r):
        await_bytes(units(6), c_recv.at[r])
        low, high = pl.ds(0, 1), pl.ds(1, 1)
        for k in (1, -1, 2):
            move(r, x + k, y - 1, low, low, d_send, d_recv.at[r], north)
            move(r, x + k, y + 1, low, high, d_send, d_recv.at[r], south)
            move(r, x - 1, y + k, high, low, d_send, d_recv.at[r], east)
            move(r, x + 1, y + k, high, high, d_send, d_recv.at[r], west)

    def part_e(r):
        await_bytes(units(3), d_recv.at[r])
        both = wmain.at[pl.ds(6 + 2 * c, 2), :, r]
        send(both, both, f_send, f_recv.at[r], twin)

    def normalise():
        await_bytes(sbuf.at[pl.ds(0, BANDS - 1)], misc_recv.at[0])
        await_bytes(halo.at[0], misc_recv.at[1])
        await_bytes(halo.at[0], misc_recv.at[2])
        await_bytes(lat, misc_recv.at[7])
        norm_taps(me, band_rows, latu, gain, halo, sbuf, order, taps)

    def plan_two():
        await_bytes(planb.at[:, 0], misc_recv.at[3])
        theirs = planb.at[:, c * CORE + (1 - me.xl) * NY + y]
        for k in (1, 3, 2):
            send(theirs, theirs, misc_send.at[5], misc_recv.at[5], me.at(y=y + k))

    def plan_three():
        await_bytes(planb.at[:, pl.ds(0, 3)], misc_recv.at[4])
        await_bytes(planb.at[:, pl.ds(0, 3)], misc_recv.at[5])
        mine = planb.at[:, pl.ds(c * CORE, CORE)]
        send(mine, mine, misc_send.at[6], misc_recv.at[6], twin)

    def plan_four():
        await_bytes(planb.at[:, pl.ds(0, CORE)], misc_recv.at[6])
        await_bytes(planb.at[:, pl.ds(0, CORE)], misc_send.at[6])
        await_bytes(planb.at[:, 0], misc_send.at[3])
        await_bytes(planb.at[:, pl.ds(0, 3)], misc_send.at[4])
        await_bytes(planb.at[:, pl.ds(0, 3)], misc_send.at[5])
        order_plan(planb, order)
        perm[...] = scatter_order(me, channels)

    weights = Weights(wmain, wext, wleft)

    def left(r):
        await_bytes(wmain.at[pl.ds(0, 2), :, 0], f_recv.at[r])
        weights.gather_left(r)

    def ext(_):
        @pl.when(c == 0)
        def _():
            await_bytes(wext.at[0, pl.ds(0, nz - 1)], x_sems.at[1])
            half = wext.at[me.xh]
            send(half, half, x_sems.at[2], x_sems.at[3], other_x)

    plans = {2: plan_two, 3: plan_three, 4: plan_four}
    acts = dict(
        a=part_a, b=part_b, c=part_c, d=part_d, e=part_e, left=left, ext=ext,
        plan=lambda k: plans[k](), norm=lambda _: normalise(),
    )
    for name, r in ORDER:
        acts[name](r)

    @pl.when(c == 0)
    def _():
        await_bytes(wext.at[0], x_sems.at[3])
        send(wext, wext, x_sems.at[4], x_sems.at[5], twin)

    left(2)
    left(3)

    @pl.when(c == 0)
    def _():
        await_bytes(wext.at[0, pl.ds(0, nz - 1)], x_sems.at[0])
        await_bytes(wext.at[0], x_sems.at[2])
        await_bytes(wext, x_sems.at[4])

    @pl.when(c != 0)
    def _():
        await_bytes(wext, x_sems.at[5])

    weights.gather_ext()
    mixed, attended, dquery = ops.at[0, 0], ops.at[1, 0], ops.at[0, 1]
    part = mixed.at[pl.ds(0, images * cells)]

    def swap_columns(ref, own_rows, sem):
        wide = ref.at[:, own_lanes(c)]
        send(wide, wide, op_sems.at[sem], op_sems.at[sem + 1], twin)
        for rows in own_rows:
            slim = ref.at[rows, MIDDLE]
            send(slim, slim, op_sems.at[sem], op_sems.at[sem + 1], twin)

    convolve(c, band_rows, latu, weights, taps, mixed)
    swap_columns(mixed, [own_cells(c, i, cells) for i in range(images)], 0)
    await_bytes(part, op_sems.at[7])
    plan_side(c, ops.at[1, 1], planb, weights, order, keys, vals, gatt)
    await_bytes(part, op_sems.at[1])
    attend(c, mixed, weights, order, keys, vals, gatt, middle, attended, dquery)
    image = [pl.ds(pl.multiple_of(2 * cells * c, 128), 2 * cells)]
    swap_columns(attended, image, 2)
    swap_columns(dquery, image, 4)
    await_bytes(part, op_sems.at[3])
    await_bytes(part, op_sems.at[5])
    reduce_gradient(
        me, factor, ops, perm, pieces,
        lambda: project(c, mixed, weights, order, attended, block_out),
        gf, gb, r1, h, r2, total, zs, zr, fin,
        s1_send, s1_recv, s2_send, s2_recv, g_send, g_recv, o_send, o_recv,
    )
    for sem in (0, 2, 4, 6):
        await_bytes(part, op_sems.at[sem])

    for g in range(2):
        for k in range(NY):
            grad_out[5 * k:5 * k + 5, g, :] = pieces[g * NY + k, 0:5, :]

    await_bytes(sbuf.at[pl.ds(0, BANDS - 1)], misc_send.at[0])
    await_bytes(halo, misc_send.at[1])
    await_bytes(lat, misc_send.at[2])
    await_bytes(wmain.at[pl.ds(0, 5), 0, pl.ds(0, 3), 0, 0], z_send)
    await_bytes(wmain.at[pl.ds(0, 4), 0], a_send)
    await_bytes(wmain.at[pl.ds(0, 2), 0], b_send)
    await_bytes(wmain.at[pl.ds(0, 6), 0], c_send)
    await_bytes(wmain.at[pl.ds(0, 3), 0], d_send)
    await_bytes(wmain.at[pl.ds(0, 2)], f_send)


def body(latents, plan, conv_weight, gn_gain, attn_weights, cotangent):
    images, band_rows, columns, channels = latents.shape
    nz = lax.axis_size("dp") // 2
    tokens = images * band_rows * columns
    plan_tokens = BANDS * plan.shape[1]
    factor = 1.0 / math.sqrt(tokens * 2 * nz * BANDS)
    zh = nz // 2
    small, big = 5 * zh, 20 * zh
    rounds = nz // 4
    dma = pltpu.SemaphoreType.DMA
    vmem = pltpu.VMEM
    return tuple(pl.pallas_call(
        functools.partial(block_kernel, nz, factor),
        out_shape=[
            jax.ShapeDtypeStruct(latents.shape, BF16),
            jax.ShapeDtypeStruct((SHARD, 2, channels), F32),
        ],
        in_specs=[pl.BlockSpec(memory_space=vmem)] * 6,
        out_specs=[pl.BlockSpec(memory_space=vmem)] * 2,
        scratch_shapes=[
            vmem((10, 2, rounds, 2, 2, UNIT, 128), BF16),
            vmem((2, nz, 32, 128), BF16),
            vmem((41, 2 * nz * 4, 128), BF16),
            vmem((UNIT, 128), BF16),
            vmem((32, 128), BF16),
            vmem((16, 128), F32),
            vmem((8, 128), F32),
            vmem((images, BANDS) + plan.shape[1:], BF16),
            vmem((2, images, columns, channels), BF16),
            vmem((BANDS, 8, 128), F32),
            vmem((channels, channels), BF16),
            vmem((channels, channels), BF16),
            vmem((3, images, 2 * band_rows + 2, columns, channels), BF16),
            vmem((images, plan_tokens, channels), BF16),
            vmem((images, plan_tokens, channels), BF16),
            vmem((2 * tokens, channels), BF16),
            vmem((2, 2, 2 * tokens, channels), BF16),
            vmem((images, 2 * band_rows, columns, channels), BF16),
            vmem((2 * tokens, 128), BF16),
            vmem((4 * big, channels), F32),
            vmem((4 * big, channels), BF16),
            vmem((3, big, channels), BF16),
            vmem((big, channels), F32),
            vmem((3, small, channels), F32),
            vmem((small, channels), F32),
            vmem((zh, 8, channels), F32),
            vmem((max(nz, BANDS), 8, channels), F32),
            vmem((8, channels), F32),
            vmem((CORE, 8, channels), F32),
            dma, dma((rounds,)), dma((6,)), dma, dma, dma, dma, dma,
            dma((rounds,)), dma((rounds,)), dma((rounds,)), dma((rounds,)), dma((rounds,)),
            dma((7,)), dma((8,)),
            dma((8,)), dma((2,)), dma((2,)), dma((2,)), dma((2,)), dma((2,)), dma((2,)),
            dma((2,)), dma((2,)), pltpu.SemaphoreType.REGULAR((2,)),
        ],
        compiler_params=pltpu.CompilerParams(
            collective_id=0, has_side_effects=True, vmem_limit_bytes=VMEM_LIMIT
        ),
        name="block",
    )(latents, plan, conv_weight, attn_weights, gn_gain, cotangent))


def solution(mesh):
    return jax.shard_map(
        body,
        mesh=mesh,
        in_specs=(
            P("dp", "spatial", None, None),
            P("dp", "spatial", None),
            P(None, "dp", None),
            P(),
            P(None, "dp", None),
            P("dp", "spatial", None, None),
        ),
        out_specs=(P("dp", "spatial", None, None), P("dp", None, None)),
        check_vma=False,
    )
```

```python
import functools
import math

import jax
import jax.numpy as jnp
from jax import lax
from jax.experimental import pallas as pl
from jax.experimental.pallas import tpu as pltpu
from jax.sharding import PartitionSpec as P

GROUPS = 32
HEAD = 64
NX = 4
NY = 4
BANDS = 16
CORE = 2 * NY
SHARD = 20
UNIT = 4 * SHARD
MESH = pl.DeviceIdType.MESH
VMEM_LIMIT = 62 * 1024 * 1024
SPANS = ((0, 2), (2, 4), (4, 5))
GRAD_SPANS = ((0, 3), (3, 5))
ORDER = (
    ("a", 0), ("a", 1), ("b", 0), ("plan", 2), ("norm", 0), ("c", 0), ("b", 1), ("d", 0), ("a", 2),
    ("c", 1), ("a", 3), ("plan", 3), ("e", 0), ("b", 2), ("d", 1), ("b", 3), ("c", 2), ("e", 1),
    ("left", 0), ("plan", 4), ("c", 3), ("d", 2), ("ext", 0), ("left", 1), ("d", 3), ("e", 2), ("plan", 5), ("e", 3),
)
BF16 = jnp.bfloat16
F32 = jnp.float32
NT = (((1,), (1,)), ((), ()))

eps_norm = 1e-05


def wrap(value, n):
    return lax.rem(value + n, n)


class Spot:
    def __init__(self, nz):
        self.nz = nz
        self.dp = lax.axis_index("dp")
        self.s = lax.axis_index("spatial")
        self.xh = lax.div(self.dp, nz)
        self.z = lax.rem(self.dp, nz)
        self.xl = lax.div(self.s, CORE)
        self.y = lax.rem(lax.div(self.s, 2), NY)
        self.c = lax.rem(self.s, 2)
        self.x = 2 * self.xh + self.xl

    def at(self, x=None, y=None, z=None, c=None):
        x = self.x if x is None else wrap(x, NX)
        y = self.y if y is None else wrap(y, NY)
        z = self.z if z is None else wrap(z, self.nz)
        c = self.c if c is None else c
        return (lax.div(x, 2) * self.nz + z, (lax.rem(x, 2) * NY + y) * 2 + c)

    def place(self, x, y):
        at = lax.rem(wrap(x, NX), 2) * NY + wrap(y, NY)
        return at + jnp.where(at >= 6, 2 * self.c, 0)

    def sid(self, x, y):
        return self.c * CORE + lax.rem(wrap(x, NX), 2) * NY + wrap(y, NY)


def send(src, dst, send_sem, recv_sem, device):
    pltpu.make_async_remote_copy(
        src_ref=src,
        dst_ref=dst,
        send_sem=send_sem,
        recv_sem=recv_sem,
        device_id=device,
        device_id_type=MESH,
    ).start()


def await_bytes(ref, sem):
    pltpu.make_async_copy(ref, ref, sem).wait()


def reach(nz):
    steps = [0]
    for k in range(1, nz // 2):
        steps += [k, -k]
    return steps + [nz // 2]


def ints(shape, axis):
    return lax.broadcasted_iota(jnp.int32, shape, axis)


def floor_of(values, width):
    return jnp.floor((values + 0.5) * (1.0 / width))


def one_hot(names, rows):
    at = ints((rows, names.shape[1]), 0).astype(F32)
    return jnp.where(at == names, 1.0, 0.0).astype(BF16)


def arrival_order(me, channels):
    nz = me.nz
    bits = nz.bit_length() - 1
    place = ints((1, channels), 1)
    head = 2 * nz * 16
    late = place - head
    main = place < head
    slot = jnp.where(main, place >> 4, late >> 2)
    row = jnp.where(main, place & 15, 16 + (late & 3))
    half, slot = slot >> bits, slot & (nz - 1)
    step = jnp.where((slot & 1) == 1, (slot + 1) >> 1, -(slot >> 1))
    names = (half * nz + ((me.z + step + nz) & (nz - 1))) * SHARD + row
    return one_hot(names.astype(F32), channels)


def scatter_order(me, channels):
    zh = me.nz // 2
    small = 5 * zh
    place = ints((1, channels), 1).astype(F32)
    outer = floor_of(place, 4 * small)
    place = place - outer * (4 * small)
    inner = floor_of(place, small)
    place = place - inner * small
    zi = floor_of(place, 5)
    i = place - 5 * zi
    first = me.c == 0
    xx = jnp.where(first, inner, outer)
    yy = jnp.where(first, outer, inner)
    half = floor_of(xx, 2)
    names = (half * me.nz + 2 * zi + xx - 2 * half) * SHARD + yy * 5 + i
    return one_hot(names, channels)


def group_table(channels):
    rows = ints((channels, 128), 0).astype(F32)
    lanes = ints((channels, 128), 1).astype(F32)
    return jnp.where(floor_of(rows, channels // GROUPS) == lanes, 1.0, 0.0)


def own_slice(me, conv, attn, wide, wslice, extra, spare):
    taps, _, channels = conv.shape
    rows = attn[...].astype(F32)
    for m in range(attn.shape[1]):
        wide[m] = rows[:, m, :]
    first = 4 * (me.xl * NY + me.y)
    for j in range(4):
        block = first + j
        shared = block - 24 + 8 * me.c
        alone = block < 24
        matrix = jnp.where(alone, lax.div(block, 2), jnp.minimum(shared, 12))
        at = jnp.where(shared < 12, 2, shared - 12)
        at = jnp.where(alone, lax.rem(block, 2) + 3 * me.c, at)
        lanes = pl.ds(pl.multiple_of(at * 128, 128), 128)
        one = conv[jnp.minimum(matrix, taps - 1), :, lanes].astype(F32)
        two = wide[jnp.maximum(matrix - taps, 0), :, lanes]
        rows = jnp.where(matrix < taps, one, two)
        wslice[16 * j:16 * j + 16, :] = rows[0:16].astype(BF16)
        spare[4 * j:4 * j + 4, :] = rows[16:20]
    wslice[64:80, :] = spare[...].astype(BF16)
    extra[0:20, :] = wide[attn.shape[1] - 1, :, channels - 128:channels].astype(BF16)
    extra[20:32, :] = jnp.zeros((12, 128), BF16)


def band_sums(lat, table, sums):
    images, band_rows, columns, channels = lat.shape
    rows = []
    for power in (1, 2):
        for i in range(images):
            cells = lat[i].reshape(band_rows * columns, channels).astype(F32)
            rows.append(jnp.sum(cells * cells if power == 2 else cells, axis=0, keepdims=True))
    rows.append(jnp.zeros((8 - 2 * images, channels), F32))
    sums[...] = jnp.dot(
        jnp.concatenate(rows, axis=0), table,
        preferred_element_type=F32, precision=lax.Precision.HIGHEST,
    )


def norm_taps(me, band_rows, latu, gain, halo, sbuf, order, taps):
    images, rows, columns, channels = latu.shape
    tot = sbuf[0]
    for i in range(1, BANDS):
        tot = tot + sbuf[i]
    grouped = lax.dot_general(
        tot, group_table(channels), NT, preferred_element_type=F32, precision=lax.Precision.HIGHEST
    )
    counted = float(band_rows * BANDS * columns * (channels // GROUPS))
    row_at = ints((columns, channels), 0)
    for i in range(images):
        mean = grouped[i:i + 1] / counted
        variance = grouped[images + i:images + i + 1] / counted - mean * mean
        inverse = lax.rsqrt(variance + eps_norm)
        for r in range(rows + 2):
            if r == 0:
                cells = halo[0, i]
            elif r == rows + 1:
                cells = halo[1, i]
            else:
                cells = latu[i, r - 1]
            normed = (cells.astype(F32) - mean) * inverse * gain[...]
            hidden = (normed / (1.0 + jnp.exp(-normed))).astype(BF16)
            hidden = jnp.dot(hidden, order[...], preferred_element_type=F32)
            if r == 0:
                hidden = jnp.where(me.s < 2, 0.0, hidden)
            if r == rows + 1:
                hidden = jnp.where(me.s >= BANDS - 2, 0.0, hidden)
            before = jnp.where(row_at == 0, 0.0, pltpu.roll(hidden, 1, 0))
            after = jnp.where(row_at == columns - 1, 0.0, pltpu.roll(hidden, columns - 1, 0))
            taps[0, i, r] = before.astype(BF16)
            taps[1, i, r] = hidden.astype(BF16)
            taps[2, i, r] = after.astype(BF16)


class Weights:
    def __init__(self, wmain, wext, wleft):
        self.wmain, self.wext, self.wleft = wmain, wext, wleft

    def gather_left(self, r, first, last):
        wmain, wleft = self.wmain, self.wleft
        half = wleft.shape[1] // 2

        def step(sid, carry):
            tile = wmain[sid, :, r, :, :, 64:80, :].reshape(8, 16, 128).astype(F32)
            for part in range(2):
                for which, rows in enumerate(self.paired(tile[:, 8 * part:8 * part + 8])):
                    rows = rows.reshape(2, 16, 128)
                    wleft[4 * sid + 2 * part + which, 16 * r:16 * r + 16, :] = rows[0]
                    wleft[4 * sid + 2 * part + which, half + 16 * r:half + 16 * r + 16, :] = rows[1]
            return carry

        lax.fori_loop(first, last, step, 0)

    def gather_ext(self):
        wext = self.wext
        count = wext.shape[0] * wext.shape[1]
        tile = wext[:, :, 16:32, :].reshape(count, 16, 128).astype(F32)
        self.wleft[self.wleft.shape[0] - 1] = self.paired(tile[:, 0:8])[0]

    def paired(self, tile):
        count = tile.shape[0]
        low = ints((count // 2, 8, 128), 1) < 4
        tile = tile.reshape(count // 2, 2, 8, 128)
        even, odd = tile[:, 0], tile[:, 1]
        first = jnp.where(low, even, pltpu.roll(odd, 4, 1))
        second = jnp.where(low, pltpu.roll(even, 4, 1), odd)
        return [v.reshape(count * 4, 128).astype(BF16) for v in (first, second)]

    def block(self, index):
        wmain, wext = self.wmain, self.wext
        if index < 4 * wmain.shape[0]:
            j = index % 4
            head = wmain[index // 4, :, :, :, :, 16 * j:16 * j + 16, :]
        else:
            head = wext[:, :, 0:16, :]
        return jnp.concatenate([head.reshape(-1, 128), self.wleft[index]], axis=0)

    def alone(self, matrix):
        return jnp.concatenate([self.block(2 * matrix), self.block(2 * matrix + 1)], axis=1)

    def shared(self, start, stop):
        parts = [self.block(24 + n) for n in range(start, stop)]
        return parts[0] if len(parts) == 1 else jnp.concatenate(parts, axis=1)

    def out(self, start, stop):
        return self.shared(12 + start, 12 + stop)


def own_lanes(c):
    return pl.ds(pl.multiple_of(384 * c, 128), 256)


MIDDLE = slice(256, 384)


def order_plan(planb, order):
    images, bands, plan_rows, channels = planb.shape
    for i in range(images):
        rows = planb[i].reshape(bands * plan_rows, channels)
        rows = jnp.dot(rows, order[...], preferred_element_type=F32).astype(BF16)
        planb[i] = rows.reshape(bands, plan_rows, channels)


def plan_side(c, cot, planb, weights, order, keys, vals, gatt):
    images, bands, plan_rows, channels = planb.shape
    for target, matrix in ((keys, 10), (vals, 11)):
        weight = weights.alone(matrix)
        for i in range(images):
            rows = planb[i].reshape(bands * plan_rows, channels)
            part = jnp.dot(rows, weight, preferred_element_type=F32).astype(BF16)
            target[i, :, own_lanes(c)] = part
        rows = planb[c].reshape(bands * plan_rows, channels)
        part = jnp.dot(rows, weights.shared(matrix, matrix + 1), preferred_element_type=F32)
        target[c, :, MIDDLE] = part.astype(BF16)
    total = None
    flat = cot[...]
    for start, stop in SPANS:
        part = lax.dot_general(
            flat[:, 128 * start:128 * stop], weights.out(start, stop), NT,
            preferred_element_type=F32,
        )
        total = part if total is None else total + part
    total = total.astype(BF16)
    for lanes, rows in ((own_lanes(c), own_lanes(c)), (MIDDLE, MIDDLE)):
        part = lax.dot_general(total, order[rows, :], NT, preferred_element_type=F32)
        gatt[:, lanes] = part.astype(BF16)


def convolve_alone(c, latu, weights, taps, mixed):
    images, rows, columns, channels = latu.shape
    tokens = images * rows * columns
    total = None
    for t in range(9):
        window = taps[t % 3, :, t // 3:t // 3 + rows].reshape(tokens, channels)
        part = jnp.dot(window, weights.alone(t), preferred_element_type=F32)
        total = part if total is None else total + part
    flat = latu[:, :, :, own_lanes(c)].reshape(tokens, 256)
    mixed[:, own_lanes(c)] = (flat.astype(F32) + total).astype(BF16)


def convolve_shared(c, band_rows, latu, weights, taps, mixed):
    images, _, columns, channels = latu.shape
    total = None
    first = band_rows * c
    for t in range(9):
        window = taps[t % 3, :, pl.ds(t // 3 + first, band_rows)]
        window = window.reshape(images * band_rows * columns, channels)
        part = jnp.dot(window, weights.shared(t, t + 1), preferred_element_type=F32)
        total = part if total is None else total + part
    flat = latu[:, pl.ds(first, band_rows), :, MIDDLE].reshape(-1, 128)
    middle = (flat.astype(F32) + total).astype(BF16)
    cells = band_rows * columns
    for i in range(images):
        mixed[own_cells(c, i, cells), MIDDLE] = middle[cells * i:cells * i + cells]


def own_cells(c, i, cells):
    return pl.ds(pl.multiple_of(2 * cells * i + cells * c, 16), cells)


def attend(c, mixed, weights, order, keys, vals, gatt, middle, attended, dquery):
    images = keys.shape[0]
    scale = 1.0 / math.sqrt(HEAD)
    cells = mixed.shape[0] // images
    left = ints((cells, 128), 1) < HEAD
    zero = jnp.zeros((cells, 128), BF16)

    def two_heads(value):
        return jnp.concatenate([jnp.where(left, value, zero), jnp.where(left, zero, value)], 0)

    def one_row(value):
        return jnp.where(left, value[:cells], value[cells:]).astype(BF16)

    def heads(query, i, rows, lanes):
        key, val = keys[i, :, lanes], vals[i, :, lanes]
        query, grad = two_heads(query), two_heads(gatt[rows, lanes])
        scores = lax.dot_general(query, key, NT, preferred_element_type=F32) * scale
        expo = jnp.exp(scores - jnp.max(scores, axis=-1, keepdims=True))
        probs = expo / jnp.sum(expo, axis=-1, keepdims=True)
        dprob = lax.dot_general(grad, val, NT, preferred_element_type=F32)
        inner = jnp.sum(probs * dprob, axis=-1, keepdims=True)
        dscore = (probs * (dprob - inner) * scale).astype(BF16)
        attended[rows, lanes] = one_row(
            jnp.dot(probs.astype(BF16), val, preferred_element_type=F32)
        )
        dquery[rows, lanes] = one_row(jnp.dot(dscore, key, preferred_element_type=F32))

    ordered = jnp.dot(mixed[...], order[...], preferred_element_type=F32).astype(BF16)
    queries = jnp.dot(ordered, weights.alone(9), preferred_element_type=F32).astype(BF16)
    middle[...] = jnp.dot(
        ordered, weights.shared(9, 10), preferred_element_type=F32
    ).astype(BF16)
    for n in range(2):
        lanes = pl.ds(pl.multiple_of(384 * c + 128 * n, 128), 128)
        for i in range(images):
            rows = slice(cells * i, cells * i + cells)
            heads(queries[rows, 128 * n:128 * n + 128], i, rows, lanes)
    rows = pl.ds(pl.multiple_of(cells * c, 128), cells)
    heads(middle[rows, :], c, rows, MIDDLE)


def project(c, mixed, weights, order, attended, block_out):
    images, band_rows, columns, channels = block_out.shape
    cells = band_rows * columns
    own = [attended[own_cells(c, i, cells), :] for i in range(images)]
    flat = [mixed[own_cells(c, i, cells), :] for i in range(images)]
    own, flat = jnp.concatenate(own, axis=0), jnp.concatenate(flat, axis=0)
    own = jnp.dot(own, order[...], preferred_element_type=F32).astype(BF16)
    for start, stop in SPANS:
        lanes = slice(128 * start, 128 * stop)
        result = flat[:, lanes].astype(F32) + jnp.dot(
            own, weights.out(start, stop), preferred_element_type=F32
        )
        block_out[:, :, :, lanes] = result.astype(BF16).reshape(
            images, band_rows, columns, 128 * (stop - start)
        )


def reduce_gradient(
    me, factor, ops, perm, out, meanwhile,
    gf, gb, r1, h, r2, total, zs, zr, fin,
    s1_send, s1_recv, s2_send, s2_recv, z_send, z_recv, o_send, o_recv,
):
    nz, x, y, z, c = me.nz, me.x, me.y, me.z, me.c
    zh = nz // 2
    small = zh * 5
    big = 4 * small
    mates = [(me.dp, wrap(me.s + k, BANDS)) for k in range(1, BANDS)]
    spans = [pl.ds(128 * a, 128 * (b - a)) for a, b in GRAD_SPANS]
    lhs = jnp.dot(ops[c, 0], perm[...], preferred_element_type=F32).astype(BF16)
    first = c == 0
    a1 = jnp.where(first, y, x)
    a2 = jnp.where(first, x, y)
    active = lax.rem(z, 2) == me.xl
    for p, (start, stop) in enumerate(GRAD_SPANS):
        lanes = slice(128 * start, 128 * stop)
        rhs = ops[c, 1, :, lanes]
        grads = lax.dot_general(
            lhs, rhs, (((0,), (0,)), ((), ())), preferred_element_type=F32
        ) * factor
        gf[:, lanes] = grads
        gb[:, lanes] = grads.astype(BF16)
        for k in (2, 1, 3):
            to = wrap(a1 + k, 4)
            device = me.at(x=jnp.where(first, x, to), y=jnp.where(first, to, y))
            send(
                gb.at[pl.ds(pl.multiple_of(to * big, 32), big), spans[p]],
                r1.at[k - 1, :, spans[p]], s1_send.at[p], s1_recv.at[p], device,
            )

    def part_two(p):
        span = spans[p]
        await_bytes(r1.at[:, :, span], s1_recv.at[p])
        acc = gf[pl.ds(pl.multiple_of(a1 * big, 32), big), span]
        for k in range(3):
            acc = acc + r1[k, :, span].astype(F32)
        h[:, span] = acc
        for k in (2, 1, 3):
            to = wrap(a2 + k, 4)
            device = me.at(x=jnp.where(first, to, x), y=jnp.where(first, y, to))
            send(
                h.at[pl.ds(pl.multiple_of(to * small, 8), small), span],
                r2.at[k - 1, :, span], s2_send.at[p], s2_recv.at[p], device,
            )

    def part_three(p):
        span = spans[p]
        await_bytes(r2.at[:, :, span], s2_recv.at[p])
        acc = h[pl.ds(pl.multiple_of(a2 * small, 8), small), span]
        for k in range(3):
            acc = acc + r2[k, :, span]
        total[:, span] = acc
        for i in range(zh):
            zs[i, 0:5, span] = total[5 * i:5 * i + 5, span]
        for i in range(zh):
            to = 2 * i + me.xl

            @pl.when(to != z)
            def _():
                send(
                    zs.at[i, :, span], zr.at[z, :, span],
                    z_send.at[p], z_recv.at[p], me.at(z=to),
                )

    zs[...] = jnp.zeros_like(zs)
    meanwhile()
    part_two(0)
    part_two(1)
    part_three(0)
    part_three(1)

    @pl.when(active)
    def _():
        for p, span in enumerate(spans):
            zr[z, :, span] = zs[lax.div(z, 2), :, span]
            await_bytes(zr.at[pl.ds(0, nz - 1), :, span], z_recv.at[p])
            piece = zr[0, :, span]
            for i in range(1, nz):
                piece = piece + zr[i, :, span]
            fin[:, span] = piece
            for mate in mates:
                send(
                    fin.at[:, span], out.at[c * NY + y, :, span], o_send.at[p], o_recv.at[p], mate
                )
            out[c * NY + y, :, span] = piece
        for p, span in enumerate(spans):
            await_bytes(out.at[pl.ds(0, CORE - 1), :, span], o_recv.at[p])
            await_bytes(zr.at[pl.ds(0, BANDS - 1), :, span], o_send.at[p])
            await_bytes(zs.at[pl.ds(0, zh - 1), :, span], z_send.at[p])

    @pl.when(jnp.logical_not(active))
    def _():
        for p, span in enumerate(spans):
            await_bytes(out.at[:, :, span], o_recv.at[p])
            await_bytes(zs.at[:, :, span], z_send.at[p])

    for p, span in enumerate(spans):
        await_bytes(r1.at[:, :, span], s1_send.at[p])
        await_bytes(r2.at[:, :, span], s2_send.at[p])


def block_kernel(
    nz, factor,
    lat, plan, conv, attn, gain, cot,
    block_out, grad_out,
    wmain, wext, wleft, wide, wslice, extra, spare, sums, planb, halo, sbuf, order, perm,
    taps, keys, vals, gatt, ops, latu, middle,
    gf, gb, r1, h, r2, total, zs, zr, fin, pieces,
    z_send, z_recv, x_sems, a_send, b_send, c_send, d_send, f_send,
    a_recv, b_recv, c_recv, d_recv, f_recv, misc_send, misc_recv,
    op_sems, s1_send, s1_recv, s2_send, s2_recv, g_send, g_recv, o_send, o_recv, near,
):
    me = Spot(nz)
    x, y, z, c, s = me.x, me.y, me.z, me.c, me.s
    channels = lat.shape[-1]
    rounds = nz // 4
    twin = me.at(c=1 - c)
    north, south = me.at(y=y + 1), me.at(y=y - 1)
    east, west = me.at(x=x + 1), me.at(x=x - 1)
    side = jnp.where(me.xl == 0, -1, 1)
    other_x = me.at(x=x + side)
    mates = [(me.dp, wrap(s + k, BANDS)) for k in range(1, BANDS)]
    greeted = mates + [me.at(z=z + k) for k in (1, -1, 2, -2)] + [other_x, me.at(x=x + 2)]
    barrier = pltpu.get_barrier_semaphore()
    for device in greeted:
        pl.semaphore_signal(barrier, inc=1, device_id=device, device_id_type=MESH)
    my_sid, my_place = me.sid(x, y), me.place(x, y)
    images, band_rows, columns, _ = lat.shape
    cells = band_rows * columns
    own_slice(me, conv, attn, wide, wslice, extra, spare)
    for i in range(images):
        ops[1, 1, own_cells(c, i, cells), :] = cot[i].reshape(cells, channels)
    pl.semaphore_wait(barrier, len(greeted))

    steps = reach(nz)

    def spread(low, high):
        for slot, step in enumerate(steps):
            if low < abs(step) <= high:
                back = steps.index(-step) if -step in steps else slot
                send(
                    wslice, wmain.at[my_place, me.xh, back // 4, back % 4 // 2, back % 2],
                    z_send, z_recv.at[back // 4], me.at(z=z + step),
                )

    def widen(k):
        for step in (k, -k):
            pl.semaphore_signal(
                near.at[k // 4], inc=1, device_id=me.at(z=z + step), device_id_type=MESH
            )

    spread(0, 2)
    widen(2)
    chip = wrap(lax.div(s, 2) + 2 * c - 1, BANDS // 2)
    for core in range(2):
        send(
            lat.at[:, c], halo.at[1 - c], misc_send.at[1], misc_recv.at[2 - c],
            (me.dp, 2 * chip + core),
        )
    send(lat, latu.at[:, pl.ds(band_rows * c, band_rows)], misc_send.at[2], misc_recv.at[7], twin)
    for i in range(images):
        ref = ops.at[1, 1, own_cells(c, i, cells)]
        send(ref, ref, op_sems.at[6], op_sems.at[7], twin)
    pair = (me.dp, ((1 - me.xl) * NY + y) * 2 + c)
    send(plan, planb.at[:, my_sid], misc_send.at[3], misc_recv.at[3], pair)
    for k in (1, 3, 2):
        send(plan, planb.at[:, my_sid], misc_send.at[4], misc_recv.at[4], me.at(y=y + k))
    band_sums(lat, group_table(channels), sums)
    pl.semaphore_wait(near.at[0], 2)
    spread(2, 4)
    widen(4)
    for mate in mates:
        send(sums, sbuf.at[s], misc_send.at[0], misc_recv.at[0], mate)
    order[...] = arrival_order(me, channels)
    pl.semaphore_wait(near.at[1], 2)
    spread(4, nz)

    @pl.when(c == 0)
    def _():
        for slot, step in enumerate(steps):
            if slot:
                back = steps.index(-step) if -step in steps else slot
                send(extra, wext.at[me.xh, back], x_sems.at[0], x_sems.at[1], me.at(z=z + step))

    wmain[my_place, me.xh, 0, 0, 0] = wslice[...]
    latu[:, pl.ds(band_rows * c, band_rows)] = lat[...]
    wext[me.xh, 0] = extra[...]
    planb[:, my_sid] = plan[...]
    sbuf[s] = sums[...]
    every = slice(None)

    def block(r, xx, yy, colours, dirs):
        return wmain.at[me.place(xx, yy), lax.div(wrap(xx, NX), 2), r, colours, dirs]

    def move(r, xx, yy, colours, dirs, send_sem, recv_sem, device):
        ref = block(r, xx, yy, colours, dirs)
        send(ref, ref, send_sem, recv_sem, device)

    def units(n):
        return wmain.at[pl.ds(0, n), 0, 0]

    def part_a(r):
        await_bytes(zwait(r), z_recv.at[r])
        for device in (east, west, north, south):
            move(r, x, y, every, every, a_send, a_recv.at[r], device)

    def zwait(r):
        return wmain.at[pl.ds(0, 3), 0, 0, 0, 0] if r == 0 else wmain.at[pl.ds(0, 4), 0, 0, 0, 0]

    def part_b(r):
        await_bytes(units(4), a_recv.at[r])
        low, high = pl.ds(0, 1), pl.ds(1, 1)
        move(r, x - 1, y, every, low, b_send, b_recv.at[r], east)
        move(r, x + 1, y, every, high, b_send, b_recv.at[r], west)
        move(r, x, y - 1, every, low, b_send, b_recv.at[r], north)
        move(r, x, y + 1, every, high, b_send, b_recv.at[r], south)
        for k in (1, -1):
            for device in (north, south):
                move(r, x + k, y, low, every, c_send, c_recv.at[r], device)
            for device in (east, west):
                move(r, x, y + k, high, every, c_send, c_recv.at[r], device)

    def part_c(r):
        await_bytes(units(2), b_recv.at[r])
        low, high = pl.ds(0, 1), pl.ds(1, 1)
        for device in (north, south):
            move(r, x + 2, y, low, every, c_send, c_recv.at[r], device)
        for device in (east, west):
            move(r, x, y + 2, high, every, c_send, c_recv.at[r], device)

    def part_d(r):
        await_bytes(units(6), c_recv.at[r])
        low, high = pl.ds(0, 1), pl.ds(1, 1)
        for k in (1, -1, 2):
            move(r, x + k, y - 1, low, low, d_send, d_recv.at[r], north)
            move(r, x + k, y + 1, low, high, d_send, d_recv.at[r], south)
            move(r, x - 1, y + k, high, low, d_send, d_recv.at[r], east)
            move(r, x + 1, y + k, high, high, d_send, d_recv.at[r], west)

    def part_e(r):
        await_bytes(units(3), d_recv.at[r])
        both = wmain.at[pl.ds(6 + 2 * c, 2), :, r]
        send(both, both, f_send, f_recv.at[r], twin)

    def normalise():
        await_bytes(sbuf.at[pl.ds(0, BANDS - 1)], misc_recv.at[0])
        await_bytes(halo.at[0], misc_recv.at[1])
        await_bytes(halo.at[0], misc_recv.at[2])
        await_bytes(lat, misc_recv.at[7])
        norm_taps(me, band_rows, latu, gain, halo, sbuf, order, taps)

    def plan_two():
        await_bytes(planb.at[:, 0], misc_recv.at[3])
        theirs = planb.at[:, c * CORE + (1 - me.xl) * NY + y]
        for k in (1, 3, 2):
            send(theirs, theirs, misc_send.at[5], misc_recv.at[5], me.at(y=y + k))

    def plan_three():
        await_bytes(planb.at[:, pl.ds(0, 3)], misc_recv.at[4])
        await_bytes(planb.at[:, pl.ds(0, 3)], misc_recv.at[5])
        mine = planb.at[:, pl.ds(c * CORE, CORE)]
        send(mine, mine, misc_send.at[6], misc_recv.at[6], twin)

    def plan_four():
        await_bytes(planb.at[:, pl.ds(0, CORE)], misc_recv.at[6])
        await_bytes(planb.at[:, pl.ds(0, CORE)], misc_send.at[6])
        await_bytes(planb.at[:, 0], misc_send.at[3])
        await_bytes(planb.at[:, pl.ds(0, 3)], misc_send.at[4])
        await_bytes(planb.at[:, pl.ds(0, 3)], misc_send.at[5])
        order_plan(planb, order)
        perm[...] = scatter_order(me, channels)

    weights = Weights(wmain, wext, wleft)

    def left(r):
        await_bytes(wmain.at[pl.ds(0, 2), :, 0], f_recv.at[r])
        weights.gather_left(r, 0, 10)

    def ext(_):
        @pl.when(c == 0)
        def _():
            await_bytes(wext.at[0, pl.ds(0, nz - 1)], x_sems.at[1])
            half = wext.at[me.xh]
            send(half, half, x_sems.at[2], x_sems.at[3], other_x)

    def ext_two():
        @pl.when(c == 0)
        def _():
            await_bytes(wext.at[0], x_sems.at[3])
            send(wext, wext, x_sems.at[4], x_sems.at[5], twin)

    plans = {5: ext_two, 2: plan_two, 3: plan_three, 4: plan_four}
    acts = dict(
        a=part_a, b=part_b, c=part_c, d=part_d, e=part_e, left=left, ext=ext,
        plan=lambda k: plans[k](), norm=lambda _: normalise(),
    )
    for name, r in ORDER:
        acts[name](r)

    for r in (2, 3):
        weights.gather_left(r, 0, 6)
    mixed, attended, dquery = ops.at[0, 0], ops.at[1, 0], ops.at[0, 1]
    part = mixed.at[pl.ds(0, images * cells)]

    def swap_columns(ref, own_rows, sem):
        wide = ref.at[:, own_lanes(c)]
        send(wide, wide, op_sems.at[sem], op_sems.at[sem + 1], twin)
        for rows in own_rows:
            slim = ref.at[rows, MIDDLE]
            send(slim, slim, op_sems.at[sem], op_sems.at[sem + 1], twin)

    convolve_alone(c, latu, weights, taps, mixed)
    wide = mixed.at[:, own_lanes(c)]
    send(wide, wide, op_sems.at[0], op_sems.at[1], twin)
    for r in (2, 3):
        await_bytes(wmain.at[pl.ds(0, 2), :, 0], f_recv.at[r])
        weights.gather_left(r, 6, 10)
    convolve_shared(c, band_rows, latu, weights, taps, mixed)
    for i in range(images):
        slim = mixed.at[own_cells(c, i, cells), MIDDLE]
        send(slim, slim, op_sems.at[0], op_sems.at[1], twin)

    @pl.when(c == 0)
    def _():
        await_bytes(wext.at[0, pl.ds(0, nz - 1)], x_sems.at[0])
        await_bytes(wext.at[0], x_sems.at[2])
        await_bytes(wext, x_sems.at[4])

    @pl.when(c != 0)
    def _():
        await_bytes(wext, x_sems.at[5])

    weights.gather_ext()
    await_bytes(part, op_sems.at[7])
    plan_side(c, ops.at[1, 1], planb, weights, order, keys, vals, gatt)
    await_bytes(part, op_sems.at[1])
    attend(c, mixed, weights, order, keys, vals, gatt, middle, attended, dquery)
    image = [pl.ds(pl.multiple_of(2 * cells * c, 128), 2 * cells)]
    swap_columns(attended, image, 2)
    swap_columns(dquery, image, 4)
    await_bytes(part, op_sems.at[3])
    await_bytes(part, op_sems.at[5])
    reduce_gradient(
        me, factor, ops, perm, pieces,
        lambda: project(c, mixed, weights, order, attended, block_out),
        gf, gb, r1, h, r2, total, zs, zr, fin,
        s1_send, s1_recv, s2_send, s2_recv, g_send, g_recv, o_send, o_recv,
    )
    for sem in (0, 2, 4, 6):
        await_bytes(part, op_sems.at[sem])

    for g in range(2):
        for k in range(NY):
            grad_out[5 * k:5 * k + 5, g, :] = pieces[g * NY + k, 0:5, :]

    await_bytes(sbuf.at[pl.ds(0, BANDS - 1)], misc_send.at[0])
    await_bytes(halo, misc_send.at[1])
    await_bytes(lat, misc_send.at[2])
    await_bytes(wmain.at[pl.ds(0, 5), 0, pl.ds(0, 3), 0, 0], z_send)
    await_bytes(wmain.at[pl.ds(0, 4), 0], a_send)
    await_bytes(wmain.at[pl.ds(0, 2), 0], b_send)
    await_bytes(wmain.at[pl.ds(0, 6), 0], c_send)
    await_bytes(wmain.at[pl.ds(0, 3), 0], d_send)
    await_bytes(wmain.at[pl.ds(0, 2)], f_send)


def body(latents, plan, conv_weight, gn_gain, attn_weights, cotangent):
    images, band_rows, columns, channels = latents.shape
    nz = lax.axis_size("dp") // 2
    tokens = images * band_rows * columns
    plan_tokens = BANDS * plan.shape[1]
    factor = 1.0 / math.sqrt(tokens * 2 * nz * BANDS)
    zh = nz // 2
    small, big = 5 * zh, 20 * zh
    rounds = nz // 4
    dma = pltpu.SemaphoreType.DMA
    vmem = pltpu.VMEM
    return tuple(pl.pallas_call(
        functools.partial(block_kernel, nz, factor),
        out_shape=[
            jax.ShapeDtypeStruct(latents.shape, BF16),
            jax.ShapeDtypeStruct((SHARD, 2, channels), F32),
        ],
        in_specs=[pl.BlockSpec(memory_space=vmem)] * 6,
        out_specs=[pl.BlockSpec(memory_space=vmem)] * 2,
        scratch_shapes=[
            vmem((10, 2, rounds, 2, 2, UNIT, 128), BF16),
            vmem((2, nz, 32, 128), BF16),
            vmem((41, 2 * nz * 4, 128), BF16),
            vmem((4, SHARD, channels), F32),
            vmem((UNIT, 128), BF16),
            vmem((32, 128), BF16),
            vmem((16, 128), F32),
            vmem((8, 128), F32),
            vmem((images, BANDS) + plan.shape[1:], BF16),
            vmem((2, images, columns, channels), BF16),
            vmem((BANDS, 8, 128), F32),
            vmem((channels, channels), BF16),
            vmem((channels, channels), BF16),
            vmem((3, images, 2 * band_rows + 2, columns, channels), BF16),
            vmem((images, plan_tokens, channels), BF16),
            vmem((images, plan_tokens, channels), BF16),
            vmem((2 * tokens, channels), BF16),
            vmem((2, 2, 2 * tokens, channels), BF16),
            vmem((images, 2 * band_rows, columns, channels), BF16),
            vmem((2 * tokens, 128), BF16),
            vmem((4 * big, channels), F32),
            vmem((4 * big, channels), BF16),
            vmem((3, big, channels), BF16),
            vmem((big, channels), F32),
            vmem((3, small, channels), F32),
            vmem((small, channels), F32),
            vmem((zh, 8, channels), F32),
            vmem((max(nz, BANDS), 8, channels), F32),
            vmem((8, channels), F32),
            vmem((CORE, 8, channels), F32),
            dma, dma((rounds,)), dma((6,)), dma, dma, dma, dma, dma,
            dma((rounds,)), dma((rounds,)), dma((rounds,)), dma((rounds,)), dma((rounds,)),
            dma((7,)), dma((8,)),
            dma((8,)), dma((2,)), dma((2,)), dma((2,)), dma((2,)), dma((2,)), dma((2,)),
            dma((2,)), dma((2,)), pltpu.SemaphoreType.REGULAR((2,)),
        ],
        compiler_params=pltpu.CompilerParams(
            collective_id=0, has_side_effects=True, vmem_limit_bytes=VMEM_LIMIT
        ),
        name="block",
    )(latents, plan, conv_weight, attn_weights.transpose(1, 0, 2), gn_gain, cotangent))


def solution(mesh):
    return jax.shard_map(
        body,
        mesh=mesh,
        in_specs=(
            P("dp", "spatial", None, None),
            P("dp", "spatial", None),
            P(None, "dp", None),
            P(),
            P(None, "dp", None),
            P("dp", "spatial", None, None),
        ),
        out_specs=(P("dp", "spatial", None, None), P("dp", None, None)),
        check_vma=False,
    )
```

```python
import functools
import math

import jax
import jax.numpy as jnp
from jax import lax
from jax.experimental import pallas as pl
from jax.experimental.pallas import tpu as pltpu
from jax.sharding import PartitionSpec as P

GROUPS = 32
HEAD = 64
NX = 4
NY = 4
BANDS = 16
CORE = 2 * NY
SHARD = 20
UNIT = 4 * SHARD
MESH = pl.DeviceIdType.MESH
VMEM_LIMIT = 62 * 1024 * 1024
SPANS = ((0, 2), (2, 4), (4, 5))
GRAD_SPANS = ((0, 3), (3, 5))
ORDER = (
    ("a", 0), ("a", 1), ("b", 0), ("plan", 2), ("norm", 0), ("c", 0), ("b", 1), ("d", 0), ("a", 2),
    ("c", 1), ("a", 3), ("plan", 3), ("e", 0), ("b", 2), ("d", 1), ("b", 3), ("c", 2), ("e", 1),
    ("left", 0), ("plan", 4), ("c", 3), ("d", 2), ("ext", 0), ("left", 1), ("d", 3), ("e", 2), ("plan", 5), ("e", 3),
)
BF16 = jnp.bfloat16
F32 = jnp.float32
NT = (((1,), (1,)), ((), ()))

eps_norm = 1e-05


def wrap(value, n):
    return lax.rem(value + n, n)


class Spot:
    def __init__(self, nz):
        self.nz = nz
        self.dp = lax.axis_index("dp")
        self.s = lax.axis_index("spatial")
        self.xh = lax.div(self.dp, nz)
        self.z = lax.rem(self.dp, nz)
        self.xl = lax.div(self.s, CORE)
        self.y = lax.rem(lax.div(self.s, 2), NY)
        self.c = lax.rem(self.s, 2)
        self.x = 2 * self.xh + self.xl

    def at(self, x=None, y=None, z=None, c=None):
        x = self.x if x is None else wrap(x, NX)
        y = self.y if y is None else wrap(y, NY)
        z = self.z if z is None else wrap(z, self.nz)
        c = self.c if c is None else c
        return (lax.div(x, 2) * self.nz + z, (lax.rem(x, 2) * NY + y) * 2 + c)

    def place(self, x, y):
        at = lax.rem(wrap(x, NX), 2) * NY + wrap(y, NY)
        return at + jnp.where(at >= 6, 2 * self.c, 0)

    def sid(self, x, y):
        return self.c * CORE + lax.rem(wrap(x, NX), 2) * NY + wrap(y, NY)


def send(src, dst, send_sem, recv_sem, device):
    pltpu.make_async_remote_copy(
        src_ref=src,
        dst_ref=dst,
        send_sem=send_sem,
        recv_sem=recv_sem,
        device_id=device,
        device_id_type=MESH,
    ).start()


def await_bytes(ref, sem):
    pltpu.make_async_copy(ref, ref, sem).wait()


def reach(nz):
    steps = [0]
    for k in range(1, nz // 2):
        steps += [k, -k]
    return steps + [nz // 2]


def ints(shape, axis):
    return lax.broadcasted_iota(jnp.int32, shape, axis)


def floor_of(values, width):
    return jnp.floor((values + 0.5) * (1.0 / width))


def one_hot(names, rows):
    at = ints((rows, names.shape[1]), 0).astype(F32)
    return jnp.where(at == names, 1.0, 0.0).astype(BF16)


def arrival_order(me, channels):
    nz = me.nz
    bits = nz.bit_length() - 1
    place = ints((1, channels), 1)
    head = 2 * nz * 16
    late = place - head
    main = place < head
    slot = jnp.where(main, place >> 4, late >> 2)
    row = jnp.where(main, place & 15, 16 + (late & 3))
    half, slot = slot >> bits, slot & (nz - 1)
    step = jnp.where((slot & 1) == 1, (slot + 1) >> 1, -(slot >> 1))
    names = (half * nz + ((me.z + step + nz) & (nz - 1))) * SHARD + row
    return one_hot(names.astype(F32), channels)


def scatter_order(me, channels):
    zh = me.nz // 2
    small = 5 * zh
    place = ints((1, channels), 1).astype(F32)
    outer = floor_of(place, 4 * small)
    place = place - outer * (4 * small)
    inner = floor_of(place, small)
    place = place - inner * small
    zi = floor_of(place, 5)
    i = place - 5 * zi
    first = me.c == 0
    xx = jnp.where(first, inner, outer)
    yy = jnp.where(first, outer, inner)
    half = floor_of(xx, 2)
    names = (half * me.nz + 2 * zi + xx - 2 * half) * SHARD + yy * 5 + i
    return one_hot(names, channels)


def group_table(channels):
    rows = ints((channels, 128), 0).astype(F32)
    lanes = ints((channels, 128), 1).astype(F32)
    return jnp.where(floor_of(rows, channels // GROUPS) == lanes, 1.0, 0.0)


def own_slice(me, conv, attn, wide, wslice, extra, spare):
    taps, _, channels = conv.shape
    rows = attn[...].astype(F32)
    for m in range(attn.shape[1]):
        wide[m] = rows[:, m, :]
    first = 4 * (me.xl * NY + me.y)
    for j in range(4):
        block = first + j
        shared = block - 24 + 8 * me.c
        alone = block < 24
        matrix = jnp.where(alone, lax.div(block, 2), jnp.minimum(shared, 12))
        at = jnp.where(shared < 12, 2, shared - 12)
        at = jnp.where(alone, lax.rem(block, 2) + 3 * me.c, at)
        lanes = pl.ds(pl.multiple_of(at * 128, 128), 128)
        one = conv[jnp.minimum(matrix, taps - 1), :, lanes].astype(F32)
        two = wide[jnp.maximum(matrix - taps, 0), :, lanes]
        rows = jnp.where(matrix < taps, one, two)
        wslice[16 * j:16 * j + 16, :] = rows[0:16].astype(BF16)
        spare[4 * j:4 * j + 4, :] = rows[16:20]
    wslice[64:80, :] = spare[...].astype(BF16)
    extra[0:20, :] = wide[attn.shape[1] - 1, :, channels - 128:channels].astype(BF16)
    extra[20:32, :] = jnp.zeros((12, 128), BF16)


def band_sums(lat, table, sums):
    images, band_rows, columns, channels = lat.shape
    rows = []
    for power in (1, 2):
        for i in range(images):
            cells = lat[i].reshape(band_rows * columns, channels).astype(F32)
            rows.append(jnp.sum(cells * cells if power == 2 else cells, axis=0, keepdims=True))
    rows.append(jnp.zeros((8 - 2 * images, channels), F32))
    sums[...] = jnp.dot(
        jnp.concatenate(rows, axis=0), table,
        preferred_element_type=F32, precision=lax.Precision.HIGHEST,
    )


def norm_taps(me, band_rows, latu, gain, halo, sbuf, order, taps):
    images, rows, columns, channels = latu.shape
    tot = sbuf[0]
    for i in range(1, BANDS):
        tot = tot + sbuf[i]
    grouped = lax.dot_general(
        tot, group_table(channels), NT, preferred_element_type=F32, precision=lax.Precision.HIGHEST
    )
    counted = float(band_rows * BANDS * columns * (channels // GROUPS))
    row_at = ints((columns, channels), 0)
    for i in range(images):
        mean = grouped[i:i + 1] / counted
        variance = grouped[images + i:images + i + 1] / counted - mean * mean
        inverse = lax.rsqrt(variance + eps_norm)
        for r in range(rows + 2):
            if r == 0:
                cells = halo[0, i]
            elif r == rows + 1:
                cells = halo[1, i]
            else:
                cells = latu[i, r - 1]
            normed = (cells.astype(F32) - mean) * inverse * gain[...]
            hidden = (normed / (1.0 + jnp.exp(-normed))).astype(BF16)
            hidden = jnp.dot(hidden, order[...], preferred_element_type=F32)
            if r == 0:
                hidden = jnp.where(me.s < 2, 0.0, hidden)
            if r == rows + 1:
                hidden = jnp.where(me.s >= BANDS - 2, 0.0, hidden)
            before = jnp.where(row_at == 0, 0.0, pltpu.roll(hidden, 1, 0))
            after = jnp.where(row_at == columns - 1, 0.0, pltpu.roll(hidden, columns - 1, 0))
            taps[0, i, r] = before.astype(BF16)
            taps[1, i, r] = hidden.astype(BF16)
            taps[2, i, r] = after.astype(BF16)


class Weights:
    def __init__(self, wmain, wext, wleft):
        self.wmain, self.wext, self.wleft = wmain, wext, wleft

    def gather_left(self, r, first, last):
        wmain, wleft = self.wmain, self.wleft
        half = wleft.shape[1] // 2

        def step(sid, carry):
            tile = wmain[sid, :, r, :, :, 64:80, :].reshape(8, 16, 128).astype(F32)
            for part in range(2):
                for which, rows in enumerate(self.paired(tile[:, 8 * part:8 * part + 8])):
                    rows = rows.reshape(2, 16, 128)
                    wleft[4 * sid + 2 * part + which, 16 * r:16 * r + 16, :] = rows[0]
                    wleft[4 * sid + 2 * part + which, half + 16 * r:half + 16 * r + 16, :] = rows[1]
            return carry

        lax.fori_loop(first, last, step, 0)

    def gather_ext(self):
        wext = self.wext
        count = wext.shape[0] * wext.shape[1]
        tile = wext[:, :, 16:32, :].reshape(count, 16, 128).astype(F32)
        self.wleft[self.wleft.shape[0] - 1] = self.paired(tile[:, 0:8])[0]

    def paired(self, tile):
        count = tile.shape[0]
        low = ints((count // 2, 8, 128), 1) < 4
        tile = tile.reshape(count // 2, 2, 8, 128)
        even, odd = tile[:, 0], tile[:, 1]
        first = jnp.where(low, even, pltpu.roll(odd, 4, 1))
        second = jnp.where(low, pltpu.roll(even, 4, 1), odd)
        return [v.reshape(count * 4, 128).astype(BF16) for v in (first, second)]

    def block(self, index):
        wmain, wext = self.wmain, self.wext
        if index < 4 * wmain.shape[0]:
            j = index % 4
            head = wmain[index // 4, :, :, :, :, 16 * j:16 * j + 16, :]
        else:
            head = wext[:, :, 0:16, :]
        return jnp.concatenate([head.reshape(-1, 128), self.wleft[index]], axis=0)

    def alone(self, matrix):
        return jnp.concatenate([self.block(2 * matrix), self.block(2 * matrix + 1)], axis=1)

    def shared(self, start, stop):
        parts = [self.block(24 + n) for n in range(start, stop)]
        return parts[0] if len(parts) == 1 else jnp.concatenate(parts, axis=1)

    def out(self, start, stop):
        return self.shared(12 + start, 12 + stop)


def own_lanes(c):
    return pl.ds(pl.multiple_of(384 * c, 128), 256)


MIDDLE = slice(256, 384)


def order_plan(planb, order):
    images, bands, plan_rows, channels = planb.shape
    for i in range(images):
        rows = planb[i].reshape(bands * plan_rows, channels)
        rows = jnp.dot(rows, order[...], preferred_element_type=F32).astype(BF16)
        planb[i] = rows.reshape(bands, plan_rows, channels)


def plan_side(c, cot, planb, weights, order, keys, vals, gatt):
    images, bands, plan_rows, channels = planb.shape
    for target, matrix in ((keys, 10), (vals, 11)):
        weight = weights.alone(matrix)
        for i in range(images):
            rows = planb[i].reshape(bands * plan_rows, channels)
            part = jnp.dot(rows, weight, preferred_element_type=F32).astype(BF16)
            target[i, :, own_lanes(c)] = part
        rows = planb[c].reshape(bands * plan_rows, channels)
        part = jnp.dot(rows, weights.shared(matrix, matrix + 1), preferred_element_type=F32)
        target[c, :, MIDDLE] = part.astype(BF16)
    total = None
    flat = cot[...]
    for start, stop in SPANS:
        part = lax.dot_general(
            flat[:, 128 * start:128 * stop], weights.out(start, stop), NT,
            preferred_element_type=F32,
        )
        total = part if total is None else total + part
    total = total.astype(BF16)
    for lanes, rows in ((own_lanes(c), own_lanes(c)), (MIDDLE, MIDDLE)):
        part = lax.dot_general(total, order[rows, :], NT, preferred_element_type=F32)
        gatt[:, lanes] = part.astype(BF16)


def convolve_alone(c, latu, weights, taps, mixed):
    images, rows, columns, channels = latu.shape
    tokens = images * rows * columns
    total = None
    for t in range(9):
        window = taps[t % 3, :, t // 3:t // 3 + rows].reshape(tokens, channels)
        part = jnp.dot(window, weights.alone(t), preferred_element_type=F32)
        total = part if total is None else total + part
    flat = latu[:, :, :, own_lanes(c)].reshape(tokens, 256)
    mixed[:, own_lanes(c)] = (flat.astype(F32) + total).astype(BF16)


def convolve_shared(c, band_rows, latu, weights, taps, mixed):
    images, _, columns, channels = latu.shape
    total = None
    first = band_rows * c
    for t in range(9):
        window = taps[t % 3, :, pl.ds(t // 3 + first, band_rows)]
        window = window.reshape(images * band_rows * columns, channels)
        part = jnp.dot(window, weights.shared(t, t + 1), preferred_element_type=F32)
        total = part if total is None else total + part
    flat = latu[:, pl.ds(first, band_rows), :, MIDDLE].reshape(-1, 128)
    middle = (flat.astype(F32) + total).astype(BF16)
    cells = band_rows * columns
    for i in range(images):
        mixed[own_cells(c, i, cells), MIDDLE] = middle[cells * i:cells * i + cells]


def own_cells(c, i, cells):
    return pl.ds(pl.multiple_of(2 * cells * i + cells * c, 16), cells)


def attend(c, mixed, weights, order, keys, vals, gatt, middle, attended, dquery):
    images = keys.shape[0]
    scale = 1.0 / math.sqrt(HEAD)
    cells = mixed.shape[0] // images
    left = ints((cells, 128), 1) < HEAD
    zero = jnp.zeros((cells, 128), BF16)

    def two_heads(value):
        return jnp.concatenate([jnp.where(left, value, zero), jnp.where(left, zero, value)], 0)

    def one_row(value):
        return jnp.where(left, value[:cells], value[cells:]).astype(BF16)

    def heads(query, i, rows, lanes):
        key, val = keys[i, :, lanes], vals[i, :, lanes]
        query, grad = two_heads(query), two_heads(gatt[rows, lanes])
        scores = lax.dot_general(query, key, NT, preferred_element_type=F32) * scale
        expo = jnp.exp(scores - jnp.max(scores, axis=-1, keepdims=True))
        probs = expo / jnp.sum(expo, axis=-1, keepdims=True)
        dprob = lax.dot_general(grad, val, NT, preferred_element_type=F32)
        inner = jnp.sum(probs * dprob, axis=-1, keepdims=True)
        dscore = (probs * (dprob - inner) * scale).astype(BF16)
        attended[rows, lanes] = one_row(
            jnp.dot(probs.astype(BF16), val, preferred_element_type=F32)
        )
        dquery[rows, lanes] = one_row(jnp.dot(dscore, key, preferred_element_type=F32))

    ordered = jnp.dot(mixed[...], order[...], preferred_element_type=F32).astype(BF16)
    queries = jnp.dot(ordered, weights.alone(9), preferred_element_type=F32).astype(BF16)
    middle[...] = jnp.dot(
        ordered, weights.shared(9, 10), preferred_element_type=F32
    ).astype(BF16)
    for n in range(2):
        lanes = pl.ds(pl.multiple_of(384 * c + 128 * n, 128), 128)
        for i in range(images):
            rows = slice(cells * i, cells * i + cells)
            heads(queries[rows, 128 * n:128 * n + 128], i, rows, lanes)
    rows = pl.ds(pl.multiple_of(cells * c, 128), cells)
    heads(middle[rows, :], c, rows, MIDDLE)


def project(c, mixed, weights, order, attended, block_out):
    images, band_rows, columns, channels = block_out.shape
    cells = band_rows * columns
    own = [attended[own_cells(c, i, cells), :] for i in range(images)]
    flat = [mixed[own_cells(c, i, cells), :] for i in range(images)]
    own, flat = jnp.concatenate(own, axis=0), jnp.concatenate(flat, axis=0)
    own = jnp.dot(own, order[...], preferred_element_type=F32).astype(BF16)
    for start, stop in SPANS:
        lanes = slice(128 * start, 128 * stop)
        result = flat[:, lanes].astype(F32) + jnp.dot(
            own, weights.out(start, stop), preferred_element_type=F32
        )
        block_out[:, :, :, lanes] = result.astype(BF16).reshape(
            images, band_rows, columns, 128 * (stop - start)
        )


def reduce_gradient(
    me, factor, ops, perm, out, meanwhile,
    gf, gb, r1, h, r2, total, zs, zr, fin,
    s1_send, s1_recv, s2_send, s2_recv, z_send, z_recv, o_send, o_recv,
):
    nz, x, y, z, c = me.nz, me.x, me.y, me.z, me.c
    zh = nz // 2
    small = zh * 5
    big = 4 * small
    mates = [(me.dp, wrap(me.s + k, BANDS)) for k in range(1, BANDS)]
    spans = [pl.ds(128 * a, 128 * (b - a)) for a, b in GRAD_SPANS]
    lhs = jnp.dot(ops[c, 0], perm[...], preferred_element_type=F32).astype(BF16)
    first = c == 0
    a1 = jnp.where(first, y, x)
    a2 = jnp.where(first, x, y)
    active = lax.rem(z, 2) == me.xl
    for p, (start, stop) in enumerate(GRAD_SPANS):
        lanes = slice(128 * start, 128 * stop)
        rhs = ops[c, 1, :, lanes]
        grads = lax.dot_general(
            lhs, rhs, (((0,), (0,)), ((), ())), preferred_element_type=F32
        ) * factor
        gf[:, lanes] = grads
        gb[:, lanes] = grads.astype(BF16)
        for k in (2, 1, 3):
            to = wrap(a1 + k, 4)
            device = me.at(x=jnp.where(first, x, to), y=jnp.where(first, to, y))
            send(
                gb.at[pl.ds(pl.multiple_of(to * big, 32), big), spans[p]],
                r1.at[k - 1, :, spans[p]], s1_send.at[p], s1_recv.at[p], device,
            )

    def part_two(p):
        span = spans[p]
        await_bytes(r1.at[:, :, span], s1_recv.at[p])
        acc = gf[pl.ds(pl.multiple_of(a1 * big, 32), big), span]
        for k in range(3):
            acc = acc + r1[k, :, span].astype(F32)
        h[:, span] = acc
        for k in (2, 1, 3):
            to = wrap(a2 + k, 4)
            device = me.at(x=jnp.where(first, to, x), y=jnp.where(first, y, to))
            send(
                h.at[pl.ds(pl.multiple_of(to * small, 8), small), span],
                r2.at[k - 1, :, span], s2_send.at[p], s2_recv.at[p], device,
            )

    def part_three(p):
        span = spans[p]
        await_bytes(r2.at[:, :, span], s2_recv.at[p])
        acc = h[pl.ds(pl.multiple_of(a2 * small, 8), small), span]
        for k in range(3):
            acc = acc + r2[k, :, span]
        total[:, span] = acc
        for i in range(zh):
            zs[i, 0:5, span] = total[5 * i:5 * i + 5, span]
        for i in range(zh):
            to = 2 * i + me.xl

            @pl.when(to != z)
            def _():
                send(
                    zs.at[i, :, span], zr.at[z, :, span],
                    z_send.at[p], z_recv.at[p], me.at(z=to),
                )

    zs[...] = jnp.zeros_like(zs)
    meanwhile()
    part_two(0)
    part_two(1)
    part_three(0)
    part_three(1)

    @pl.when(active)
    def _():
        for p, span in enumerate(spans):
            zr[z, :, span] = zs[lax.div(z, 2), :, span]
            await_bytes(zr.at[pl.ds(0, nz - 1), :, span], z_recv.at[p])
            piece = zr[0, :, span]
            for i in range(1, nz):
                piece = piece + zr[i, :, span]
            fin[:, span] = piece
            for mate in mates:
                send(
                    fin.at[:, span], out.at[c * NY + y, :, span], o_send.at[p], o_recv.at[p], mate
                )
            out[c * NY + y, :, span] = piece
        for p, span in enumerate(spans):
            await_bytes(out.at[pl.ds(0, CORE - 1), :, span], o_recv.at[p])
            await_bytes(zr.at[pl.ds(0, BANDS - 1), :, span], o_send.at[p])
            await_bytes(zs.at[pl.ds(0, zh - 1), :, span], z_send.at[p])

    @pl.when(jnp.logical_not(active))
    def _():
        for p, span in enumerate(spans):
            await_bytes(out.at[:, :, span], o_recv.at[p])
            await_bytes(zs.at[:, :, span], z_send.at[p])

    for p, span in enumerate(spans):
        await_bytes(r1.at[:, :, span], s1_send.at[p])
        await_bytes(r2.at[:, :, span], s2_send.at[p])


def block_kernel(
    nz, factor,
    lat, plan, conv, attn, gain, cot,
    block_out, grad_out,
    wmain, wext, wleft, wide, wslice, extra, spare, sums, planb, halo, sbuf, order, perm,
    taps, keys, vals, gatt, ops, latu, middle,
    gf, gb, r1, h, r2, total, zs, zr, fin, pieces,
    z_send, z_recv, x_sems, a_send, b_send, c_send, d_send, f_send,
    a_recv, b_recv, c_recv, d_recv, f_recv, misc_send, misc_recv,
    op_sems, s1_send, s1_recv, s2_send, s2_recv, g_send, g_recv, o_send, o_recv, near,
):
    me = Spot(nz)
    x, y, z, c, s = me.x, me.y, me.z, me.c, me.s
    channels = lat.shape[-1]
    rounds = nz // 4
    twin = me.at(c=1 - c)
    north, south = me.at(y=y + 1), me.at(y=y - 1)
    east, west = me.at(x=x + 1), me.at(x=x - 1)
    side = jnp.where(me.xl == 0, -1, 1)
    other_x = me.at(x=x + side)
    mates = [(me.dp, wrap(s + k, BANDS)) for k in range(1, BANDS)]
    greeted = mates + [me.at(z=z + k) for k in (1, -1, 2, -2)] + [other_x, me.at(x=x + 2)]
    barrier = pltpu.get_barrier_semaphore()
    for device in greeted:
        pl.semaphore_signal(barrier, inc=1, device_id=device, device_id_type=MESH)
    my_sid, my_place = me.sid(x, y), me.place(x, y)
    images, band_rows, columns, _ = lat.shape
    cells = band_rows * columns
    own_slice(me, conv, attn, wide, wslice, extra, spare)
    for i in range(images):
        ops[1, 1, own_cells(c, i, cells), :] = cot[i].reshape(cells, channels)
    pl.semaphore_wait(barrier, len(greeted))

    steps = reach(nz)

    def spread(low, high):
        for slot, step in enumerate(steps):
            if low < abs(step) <= high:
                back = steps.index(-step) if -step in steps else slot
                send(
                    wslice, wmain.at[my_place, me.xh, back // 4, back % 4 // 2, back % 2],
                    z_send, z_recv.at[back // 4], me.at(z=z + step),
                )

    def widen(k):
        for step in (k, -k):
            pl.semaphore_signal(
                near.at[k // 4], inc=1, device_id=me.at(z=z + step), device_id_type=MESH
            )

    spread(0, 2)
    widen(2)
    for device in (east, west, north, south):
        send(wslice, wmain.at[my_place, me.xh, 0, 0, 0], a_send, a_recv.at[0], device)
    chip = wrap(lax.div(s, 2) + 2 * c - 1, BANDS // 2)
    for core in range(2):
        send(
            lat.at[:, c], halo.at[1 - c], misc_send.at[1], misc_recv.at[2 - c],
            (me.dp, 2 * chip + core),
        )
    send(lat, latu.at[:, pl.ds(band_rows * c, band_rows)], misc_send.at[2], misc_recv.at[7], twin)
    for i in range(images):
        ref = ops.at[1, 1, own_cells(c, i, cells)]
        send(ref, ref, op_sems.at[6], op_sems.at[7], twin)
    pair = (me.dp, ((1 - me.xl) * NY + y) * 2 + c)
    send(plan, planb.at[:, my_sid], misc_send.at[3], misc_recv.at[3], pair)
    for k in (1, 3, 2):
        send(plan, planb.at[:, my_sid], misc_send.at[4], misc_recv.at[4], me.at(y=y + k))
    band_sums(lat, group_table(channels), sums)
    pl.semaphore_wait(near.at[0], 2)
    spread(2, 4)
    widen(4)
    for mate in mates:
        send(sums, sbuf.at[s], misc_send.at[0], misc_recv.at[0], mate)
    order[...] = arrival_order(me, channels)
    pl.semaphore_wait(near.at[1], 2)
    spread(4, nz)

    @pl.when(c == 0)
    def _():
        for slot, step in enumerate(steps):
            if slot:
                back = steps.index(-step) if -step in steps else slot
                send(extra, wext.at[me.xh, back], x_sems.at[0], x_sems.at[1], me.at(z=z + step))

    wmain[my_place, me.xh, 0, 0, 0] = wslice[...]
    latu[:, pl.ds(band_rows * c, band_rows)] = lat[...]
    wext[me.xh, 0] = extra[...]
    planb[:, my_sid] = plan[...]
    sbuf[s] = sums[...]
    every = slice(None)

    def block(r, xx, yy, colours, dirs):
        return wmain.at[me.place(xx, yy), lax.div(wrap(xx, NX), 2), r, colours, dirs]

    def move(r, xx, yy, colours, dirs, send_sem, recv_sem, device):
        ref = block(r, xx, yy, colours, dirs)
        send(ref, ref, send_sem, recv_sem, device)

    def units(n):
        return wmain.at[pl.ds(0, n), 0, 0]

    def part_a(r):
        await_bytes(zwait(r), z_recv.at[r])
        for device in (east, west, north, south):
            if r:
                move(r, x, y, every, every, a_send, a_recv.at[r], device)
            else:
                move(r, x, y, pl.ds(0, 1), pl.ds(1, 1), a_send, a_recv.at[r], device)
                move(r, x, y, pl.ds(1, 1), every, a_send, a_recv.at[r], device)

    def zwait(r):
        return wmain.at[pl.ds(0, 3), 0, 0, 0, 0] if r == 0 else wmain.at[pl.ds(0, 4), 0, 0, 0, 0]

    def part_b(r):
        await_bytes(units(4), a_recv.at[r])
        low, high = pl.ds(0, 1), pl.ds(1, 1)
        move(r, x - 1, y, every, low, b_send, b_recv.at[r], east)
        move(r, x + 1, y, every, high, b_send, b_recv.at[r], west)
        move(r, x, y - 1, every, low, b_send, b_recv.at[r], north)
        move(r, x, y + 1, every, high, b_send, b_recv.at[r], south)
        for k in (1, -1):
            for device in (north, south):
                move(r, x + k, y, low, every, c_send, c_recv.at[r], device)
            for device in (east, west):
                move(r, x, y + k, high, every, c_send, c_recv.at[r], device)

    def part_c(r):
        await_bytes(units(2), b_recv.at[r])
        low, high = pl.ds(0, 1), pl.ds(1, 1)
        for device in (north, south):
            move(r, x + 2, y, low, every, c_send, c_recv.at[r], device)
        for device in (east, west):
            move(r, x, y + 2, high, every, c_send, c_recv.at[r], device)

    def part_d(r):
        await_bytes(units(6), c_recv.at[r])
        low, high = pl.ds(0, 1), pl.ds(1, 1)
        for k in (1, -1, 2):
            move(r, x + k, y - 1, low, low, d_send, d_recv.at[r], north)
            move(r, x + k, y + 1, low, high, d_send, d_recv.at[r], south)
            move(r, x - 1, y + k, high, low, d_send, d_recv.at[r], east)
            move(r, x + 1, y + k, high, high, d_send, d_recv.at[r], west)

    def part_e(r):
        await_bytes(units(3), d_recv.at[r])
        both = wmain.at[pl.ds(6 + 2 * c, 2), :, r]
        send(both, both, f_send, f_recv.at[r], twin)

    def normalise():
        await_bytes(sbuf.at[pl.ds(0, BANDS - 1)], misc_recv.at[0])
        await_bytes(halo.at[0], misc_recv.at[1])
        await_bytes(halo.at[0], misc_recv.at[2])
        await_bytes(lat, misc_recv.at[7])
        norm_taps(me, band_rows, latu, gain, halo, sbuf, order, taps)

    def plan_two():
        await_bytes(planb.at[:, 0], misc_recv.at[3])
        theirs = planb.at[:, c * CORE + (1 - me.xl) * NY + y]
        for k in (1, 3, 2):
            send(theirs, theirs, misc_send.at[5], misc_recv.at[5], me.at(y=y + k))

    def plan_three():
        await_bytes(planb.at[:, pl.ds(0, 3)], misc_recv.at[4])
        await_bytes(planb.at[:, pl.ds(0, 3)], misc_recv.at[5])
        mine = planb.at[:, pl.ds(c * CORE, CORE)]
        send(mine, mine, misc_send.at[6], misc_recv.at[6], twin)

    def plan_four():
        await_bytes(planb.at[:, pl.ds(0, CORE)], misc_recv.at[6])
        await_bytes(planb.at[:, pl.ds(0, CORE)], misc_send.at[6])
        await_bytes(planb.at[:, 0], misc_send.at[3])
        await_bytes(planb.at[:, pl.ds(0, 3)], misc_send.at[4])
        await_bytes(planb.at[:, pl.ds(0, 3)], misc_send.at[5])
        order_plan(planb, order)
        perm[...] = scatter_order(me, channels)

    weights = Weights(wmain, wext, wleft)

    def left(r):
        await_bytes(wmain.at[pl.ds(0, 2), :, 0], f_recv.at[r])
        weights.gather_left(r, 0, 10)

    def ext(_):
        @pl.when(c == 0)
        def _():
            await_bytes(wext.at[0, pl.ds(0, nz - 1)], x_sems.at[1])
            half = wext.at[me.xh]
            send(half, half, x_sems.at[2], x_sems.at[3], other_x)

    def ext_two():
        @pl.when(c == 0)
        def _():
            await_bytes(wext.at[0], x_sems.at[3])
            send(wext, wext, x_sems.at[4], x_sems.at[5], twin)

    plans = {5: ext_two, 2: plan_two, 3: plan_three, 4: plan_four}
    acts = dict(
        a=part_a, b=part_b, c=part_c, d=part_d, e=part_e, left=left, ext=ext,
        plan=lambda k: plans[k](), norm=lambda _: normalise(),
    )
    for name, r in ORDER:
        acts[name](r)

    for r in (2, 3):
        weights.gather_left(r, 0, 6)
    mixed, attended, dquery = ops.at[0, 0], ops.at[1, 0], ops.at[0, 1]
    part = mixed.at[pl.ds(0, images * cells)]

    def swap_columns(ref, own_rows, sem):
        wide = ref.at[:, own_lanes(c)]
        send(wide, wide, op_sems.at[sem], op_sems.at[sem + 1], twin)
        for rows in own_rows:
            slim = ref.at[rows, MIDDLE]
            send(slim, slim, op_sems.at[sem], op_sems.at[sem + 1], twin)

    convolve_alone(c, latu, weights, taps, mixed)
    wide = mixed.at[:, own_lanes(c)]
    send(wide, wide, op_sems.at[0], op_sems.at[1], twin)
    for r in (2, 3):
        await_bytes(wmain.at[pl.ds(0, 2), :, 0], f_recv.at[r])
        weights.gather_left(r, 6, 10)
    convolve_shared(c, band_rows, latu, weights, taps, mixed)
    for i in range(images):
        slim = mixed.at[own_cells(c, i, cells), MIDDLE]
        send(slim, slim, op_sems.at[0], op_sems.at[1], twin)

    @pl.when(c == 0)
    def _():
        await_bytes(wext.at[0, pl.ds(0, nz - 1)], x_sems.at[0])
        await_bytes(wext.at[0], x_sems.at[2])
        await_bytes(wext, x_sems.at[4])

    @pl.when(c != 0)
    def _():
        await_bytes(wext, x_sems.at[5])

    weights.gather_ext()
    await_bytes(part, op_sems.at[7])
    plan_side(c, ops.at[1, 1], planb, weights, order, keys, vals, gatt)
    await_bytes(part, op_sems.at[1])
    attend(c, mixed, weights, order, keys, vals, gatt, middle, attended, dquery)
    image = [pl.ds(pl.multiple_of(2 * cells * c, 128), 2 * cells)]
    swap_columns(attended, image, 2)
    swap_columns(dquery, image, 4)
    await_bytes(part, op_sems.at[3])
    await_bytes(part, op_sems.at[5])
    reduce_gradient(
        me, factor, ops, perm, pieces,
        lambda: project(c, mixed, weights, order, attended, block_out),
        gf, gb, r1, h, r2, total, zs, zr, fin,
        s1_send, s1_recv, s2_send, s2_recv, g_send, g_recv, o_send, o_recv,
    )
    for sem in (0, 2, 4, 6):
        await_bytes(part, op_sems.at[sem])

    for g in range(2):
        for k in range(NY):
            grad_out[5 * k:5 * k + 5, g, :] = pieces[g * NY + k, 0:5, :]

    await_bytes(sbuf.at[pl.ds(0, BANDS - 1)], misc_send.at[0])
    await_bytes(halo, misc_send.at[1])
    await_bytes(lat, misc_send.at[2])
    await_bytes(wmain.at[pl.ds(0, 5), 0, pl.ds(0, 3), 0, 0], z_send)
    await_bytes(wmain.at[pl.ds(0, 4), 0], a_send)
    await_bytes(wmain.at[pl.ds(0, 2), 0], b_send)
    await_bytes(wmain.at[pl.ds(0, 6), 0], c_send)
    await_bytes(wmain.at[pl.ds(0, 3), 0], d_send)
    await_bytes(wmain.at[pl.ds(0, 2)], f_send)


def body(latents, plan, conv_weight, gn_gain, attn_weights, cotangent):
    images, band_rows, columns, channels = latents.shape
    nz = lax.axis_size("dp") // 2
    tokens = images * band_rows * columns
    plan_tokens = BANDS * plan.shape[1]
    factor = 1.0 / math.sqrt(tokens * 2 * nz * BANDS)
    zh = nz // 2
    small, big = 5 * zh, 20 * zh
    rounds = nz // 4
    dma = pltpu.SemaphoreType.DMA
    vmem = pltpu.VMEM
    return tuple(pl.pallas_call(
        functools.partial(block_kernel, nz, factor),
        out_shape=[
            jax.ShapeDtypeStruct(latents.shape, BF16),
            jax.ShapeDtypeStruct((SHARD, 2, channels), F32),
        ],
        in_specs=[pl.BlockSpec(memory_space=vmem)] * 6,
        out_specs=[pl.BlockSpec(memory_space=vmem)] * 2,
        scratch_shapes=[
            vmem((10, 2, rounds, 2, 2, UNIT, 128), BF16),
            vmem((2, nz, 32, 128), BF16),
            vmem((41, 2 * nz * 4, 128), BF16),
            vmem((4, SHARD, channels), F32),
            vmem((UNIT, 128), BF16),
            vmem((32, 128), BF16),
            vmem((16, 128), F32),
            vmem((8, 128), F32),
            vmem((images, BANDS) + plan.shape[1:], BF16),
            vmem((2, images, columns, channels), BF16),
            vmem((BANDS, 8, 128), F32),
            vmem((channels, channels), BF16),
            vmem((channels, channels), BF16),
            vmem((3, images, 2 * band_rows + 2, columns, channels), BF16),
            vmem((images, plan_tokens, channels), BF16),
            vmem((images, plan_tokens, channels), BF16),
            vmem((2 * tokens, channels), BF16),
            vmem((2, 2, 2 * tokens, channels), BF16),
            vmem((images, 2 * band_rows, columns, channels), BF16),
            vmem((2 * tokens, 128), BF16),
            vmem((4 * big, channels), F32),
            vmem((4 * big, channels), BF16),
            vmem((3, big, channels), BF16),
            vmem((big, channels), F32),
            vmem((3, small, channels), F32),
            vmem((small, channels), F32),
            vmem((zh, 8, channels), F32),
            vmem((max(nz, BANDS), 8, channels), F32),
            vmem((8, channels), F32),
            vmem((CORE, 8, channels), F32),
            dma, dma((rounds,)), dma((6,)), dma, dma, dma, dma, dma,
            dma((rounds,)), dma((rounds,)), dma((rounds,)), dma((rounds,)), dma((rounds,)),
            dma((7,)), dma((8,)),
            dma((8,)), dma((2,)), dma((2,)), dma((2,)), dma((2,)), dma((2,)), dma((2,)),
            dma((2,)), dma((2,)), pltpu.SemaphoreType.REGULAR((2,)),
        ],
        compiler_params=pltpu.CompilerParams(
            collective_id=0, has_side_effects=True, vmem_limit_bytes=VMEM_LIMIT
        ),
        name="block",
    )(latents, plan, conv_weight, attn_weights.transpose(1, 0, 2), gn_gain, cotangent))


def solution(mesh):
    return jax.shard_map(
        body,
        mesh=mesh,
        in_specs=(
            P("dp", "spatial", None, None),
            P("dp", "spatial", None),
            P(None, "dp", None),
            P(),
            P(None, "dp", None),
            P("dp", "spatial", None, None),
        ),
        out_specs=(P("dp", "spatial", None, None), P("dp", None, None)),
        check_vma=False,
    )
```
